256 devices in a mesh: head: 8 (over z), page: 32 (over y, x, core).
Axes of the slice: x: 4, y: 4, z: 8, core: 2. Of those that a mesh axis runs over, the one named last changes fastest.
Arguments:
- doc_states: bfloat16 [2048, 2048], P('page'), may hold values from -6 to 6
- gain_attn: float32 [2048], replicated, may hold values from 0.1 to 1.9
- query_weight: bfloat16 [2048, 2048], P(None, 'head'), may hold values from -0.125 to 0.125
- cache_keys: bfloat16 [64, 128, 2048], P('page', None, 'head'), may hold values from -144 to 144
- cache_values: bfloat16 [64, 128, 2048], P('page', None, 'head'), may hold values from -6 to 6
- rel_bucket: int32 [64, 128], P('page'), may hold values from 0 to 31
- bias_table: float32 [32, 32], P(None, 'head'), may hold values from -4 to 4
- out_weight: bfloat16 [2048, 2048], P('head'), may hold values from -0.125 to 0.125
- gain_ffn: float32 [2048], replicated, may hold values from 0.1 to 1.9
- wi_gate: bfloat16 [2048, 5120], P(None, 'head'), may hold values from -0.125 to 0.125
- wi_up: bfloat16 [2048, 5120], P(None, 'head'), may hold values from -0.125 to 0.125
- wo_ffn: bfloat16 [5120, 2048], P('head'), may hold values from -0.078125 to 0.078125
- score_vector: float32 [2048], replicated, may hold values from -0.125 to 0.125
- query_lengths: int32 [8], replicated, may hold values from 1 to 1024
- doc_query: int32 [256], replicated, may hold values from 0 to 7
- doc_of_token: int32 [2048], replicated, may hold values from 0 to 255, as said below
- page_table: int32 [64], replicated, may hold values from 0 to 63, each once
Outputs:
- doc_scores: float32 [256], P('page')
The draws below stay inside these ranges and needn't reach their ends.
Inputs may be any that keep to these rules, and one draw needn't show every extreme that they name: page_table lists every physical page once. `doc_of_token`: the tokens of each document form one contiguous run of 1 to 256 tokens; every document has one run, and some document has exactly 256 tokens.
All inputs are finite; a program needn't handle non-finite values.
Results may differ from the reference program's by a relative error of at most 0.03.
Values may be sent and summed in bfloat16 or wider, within the bound.
No kernel may reach another device: no remote copies, remote signals or barrier semaphores. Data moves between devices by JAX's collectives and lax.ppermute only.
A program may use at most 320 MiB of HBM per device.

```python
import jax
import jax.numpy as jnp
from jax import lax

D = 2048
H = 32
DH = 64
FF = 5120
NB = 32
PAGE_LEN = 128
NQ = 8
TOK_DEV = 64
TOKENS = 2048
PAGES = 64
MAXP = 8
NDOC = 256
MOST_DOC = 256


def draw_cache_keys(key, part):
    order = jax.random.permutation(jax.random.fold_in(key, 11), H)
    factor = jnp.where(order == 0, 80.0, jnp.where(order == 1, 40.0, jnp.where(order == 2, 16.0, 1.0)))
    column = jnp.repeat(factor, DH)
    entries = jax.random.fold_in(key, 12)
    shape = (PAGES, PAGE_LEN, H * DH)
    base = jnp.clip(jax.random.normal(entries, shape, jnp.float32), -6.0, 6.0)
    return (0.3 * base * column[None, None, :]).astype(jnp.bfloat16)


def draw_doc_of_token(key, part):
    middle = NDOC - 2
    remain = TOKENS - TOK_DEV - MOST_DOC
    stride = remain // middle
    index = jnp.arange(middle + 1, dtype=jnp.int32)
    jitter = jax.random.randint(jax.random.fold_in(key, 21), (middle + 1,), 0, stride, dtype=jnp.int32)
    jitter = jnp.where((index == 0) | (index == middle), 0, jitter)
    cuts = index * remain // middle + jitter
    starts = jnp.concatenate([jnp.array([0, TOK_DEV], jnp.int32), (TOK_DEV + MOST_DOC + cuts[:-1]).astype(jnp.int32)])
    positions = jnp.arange(TOKENS, dtype=jnp.int32)
    segment = jnp.sum((positions[:, None] >= starts[None, 1:]).astype(jnp.int32), axis=1).astype(jnp.int32)
    order = jax.random.permutation(jax.random.fold_in(key, 22), NDOC).astype(jnp.int32)
    pinned = NDOC // 2
    order = jnp.where(order == pinned, order[0], order)
    order = order.at[0].set(pinned)
    return order[segment].astype(jnp.int32)


def plant(values, rng, least, high):
    longest = values.shape.index(max(values.shape))
    spots = []
    for shift in (0, 1):
        where = [jax.random.randint(jax.random.fold_in(rng, axis), (), 0, length) for axis, length in enumerate(values.shape)]
        where[longest] = (where[longest] + shift) % values.shape[longest]
        spots.append(tuple(where))
    return values.at[spots[0]].set(least).at[spots[1]].set(high)


def block_scale(rng, dims, split, smallest, largest):
    level = 1.0
    for dim, parts in split:
        heights = jax.random.uniform(jax.random.fold_in(jax.random.fold_in(rng, 6), dim), (parts,), jnp.float32, smallest / len(split), largest / len(split))
        level = level * jnp.repeat(jnp.exp(heights), dims[dim] // parts).reshape((-1,) + (1,) * (len(dims) - 1 - dim))
    return level


def noise(own_key, extent, spread, bound, split=(), kind=jnp.bfloat16):
    values = jax.random.normal(own_key, extent, jnp.float32) * spread
    if len(split) > 0:
        values = block_scale(own_key, extent, split, -0.22, 0.18) * values
    return jnp.clip(values, min=-bound, max=bound).astype(kind)


def setup_inputs(seed: int = 0) -> dict:
    key_list = jax.random.split(jax.random.key(seed), 18)
    return {
        "doc_states": noise(key_list[0], (TOKENS, D), 1.0, 6.0, ((0, 32),)),
        "gain_attn": jnp.clip(1.0 + 0.18 * jax.random.normal(key_list[1], (D,), jnp.float32), 0.1, 1.9),
        "query_weight": noise(key_list[2], (D, H * DH), D ** -0.5, 0.125, ((1, 8),)),
        "cache_keys": draw_cache_keys(jax.random.fold_in(key_list[17], 71), 0),
        "cache_values": noise(key_list[4], (PAGES, PAGE_LEN, H * DH), 1.0, 6.0, ((0, 32), (2, 8))),
        "rel_bucket": plant(jax.random.randint(key_list[5], (PAGES, PAGE_LEN), 0, NB), jax.random.fold_in(key_list[5], 1), 0, NB - 1).astype(jnp.int32),
        "bias_table": noise(key_list[6], (NB, H), 1.0, 4.0, ((1, 8),), jnp.float32),
        "out_weight": noise(key_list[7], (H * DH, D), (H * DH) ** -0.5, 0.125, ((0, 8),)),
        "gain_ffn": jnp.clip(1.0 + 0.18 * jax.random.normal(key_list[8], (D,), jnp.float32), 0.1, 1.9),
        "wi_gate": noise(key_list[9], (D, FF), D ** -0.5, 0.125, ((1, 8),)),
        "wi_up": noise(key_list[10], (D, FF), D ** -0.5, 0.125, ((1, 8),)),
        "wo_ffn": noise(key_list[11], (FF, D), FF ** -0.5, 0.078125, ((0, 8),)),
        "score_vector": noise(key_list[12], (D,), D ** -0.5, 0.125, (), jnp.float32),
        "query_lengths": plant(jax.random.randint(key_list[13], (NQ,), 1, MAXP * PAGE_LEN + 1), jax.random.fold_in(key_list[13], 1), 1, MAXP * PAGE_LEN).astype(jnp.int32),
        "doc_query": plant(jax.random.randint(key_list[14], (NDOC,), 0, NQ), jax.random.fold_in(key_list[14], 1), 0, NQ - 1).astype(jnp.int32),
        "doc_of_token": draw_doc_of_token(jax.random.fold_in(key_list[17], 71), 0),
        "page_table": jax.random.permutation(key_list[16], PAGES).astype(jnp.int32),
    }


def rms_scale(values, gain):
    values = values.astype(jnp.float32)
    return values * lax.rsqrt(lax.optimization_barrier(jnp.mean(values * values, axis=-1, keepdims=True)) + 1e-06) * gain

def reference(doc_states, gain_attn, query_weight, cache_keys, cache_values, rel_bucket, bias_table, out_weight, gain_ffn, wi_gate, wi_up, wo_ffn, score_vector, query_lengths, doc_query, doc_of_token, page_table):
    width = H * DH
    span = MAXP * PAGE_LEN
    normed = rms_scale(doc_states, gain_attn).astype(jnp.bfloat16)
    queries = jnp.dot(normed, query_weight, preferred_element_type=jnp.float32).astype(jnp.bfloat16)
    tok_query = doc_query[doc_of_token].astype(jnp.int32)
    table = page_table.reshape(NQ, MAXP)
    keys_all = cache_keys[table].reshape(NQ, span, H, DH).astype(jnp.float32)
    values_all = cache_values[table].reshape(NQ, span, H, DH).astype(jnp.float32)
    bias_all = jnp.transpose(bias_table[rel_bucket[table].reshape(NQ, span)], (0, 2, 1))
    valid_all = jnp.arange(span)[None, :] < query_lengths[:, None]
    block = min(512, TOKENS)
    count = TOKENS // block

    def one_block(pair):
        rows, owners = pair
        heads = rows.reshape(block, H, DH).astype(jnp.float32)

        def per_query(carry, index):
            scores = jnp.einsum('rhd,khd->rhk', heads, keys_all[index], precision=lax.Precision.HIGHEST) + bias_all[index][None]
            mask = valid_all[index][None, None, :]
            top = lax.optimization_barrier(jnp.max(jnp.where(mask, scores, -1e+30), axis=-1))
            weights = jnp.where(mask, jnp.exp(scores - top[..., None]), 0.0)
            total = lax.optimization_barrier(jnp.sum(weights, axis=-1))
            rounded = weights.astype(jnp.bfloat16).astype(jnp.float32)
            summed = jnp.einsum('rhk,khd->rhd', rounded, values_all[index], precision=lax.Precision.HIGHEST)
            chosen = (owners == index)[:, None, None]
            context = jnp.where(chosen, summed / jnp.where(chosen[:, :, 0], total, 1.0)[..., None], carry)
            return (context, None)
        start = jnp.zeros((block, H, DH), jnp.float32)
        result, unused = lax.scan(per_query, start, jnp.arange(NQ, dtype=jnp.int32))
        return result.reshape(block, width).astype(jnp.bfloat16)
    context = lax.map(one_block, (queries.reshape(count, block, width), tok_query.reshape(count, block))).reshape(TOKENS, width)
    hidden = doc_states.astype(jnp.float32) + jnp.dot(context, out_weight, preferred_element_type=jnp.float32)
    normed_two = rms_scale(hidden, gain_ffn).astype(jnp.bfloat16)
    gate = jnp.dot(normed_two, wi_gate, preferred_element_type=jnp.float32)
    upper = jnp.dot(normed_two, wi_up, preferred_element_type=jnp.float32)
    middle = (jax.nn.gelu(gate, approximate=True) * upper).astype(jnp.bfloat16)
    final = hidden + jnp.dot(middle, wo_ffn, preferred_element_type=jnp.float32)
    tok_score = jnp.dot(final, score_vector, precision=lax.Precision.HIGHEST)
    sums = jax.ops.segment_sum(tok_score, doc_of_token, num_segments=NDOC)
    counts = jax.ops.segment_sum(jnp.ones((TOKENS,), jnp.float32), doc_of_token, num_segments=NDOC)
    return sums / counts
```

```python
import jax
import jax.numpy as jnp
from jax import lax
from jax.experimental import pallas as pl
from jax.experimental.pallas import tpu as pltpu
from jax.sharding import PartitionSpec as P

NQ = 8
MASKED = -1e30
BF = jnp.bfloat16
F32 = jnp.float32


def rms_scale(values, gain):
    values = values.astype(F32)
    return values * lax.rsqrt(jnp.mean(values * values, axis=-1, keepdims=True) + 1e-06) * gain


def split_three(value):
    first = value.astype(BF)
    rest = value - first.astype(F32)
    second = rest.astype(BF)
    third = (rest - second.astype(F32)).astype(BF)
    return first, second, third


def attention_kernel(page_info, queries, keys_a, keys_b, values_a, values_b, buckets_a, buckets_b,
                     bias_table, tok_query, out, bias_wide, key_query, values_t):
    chips, tok_dev, width = queries.shape
    pages, page_len, _ = keys_a.shape
    heads = bias_table.shape[1]
    depth = width // heads
    keys_all = 2 * pages * page_len
    bucket_count = bias_table.shape[0]
    pieces = split_three(bias_table[...])
    stacked = jnp.concatenate([piece.astype(F32) for piece in pieces], axis=0)
    spread = jnp.concatenate(
        [jnp.broadcast_to(stacked[:, h : h + 1], (3 * bucket_count, 128)) for h in range(heads)], axis=1
    ).astype(BF)
    row = lax.broadcasted_iota(jnp.int32, (3 * bucket_count, page_len), 0) % bucket_count
    slot = lax.broadcasted_iota(jnp.int32, (page_len, 128), 0)
    for part, (buckets, values) in enumerate(((buckets_a, values_a), (buckets_b, values_b))):
        for page in range(pages):
            local = part * pages + page
            span = pl.ds(local * page_len, page_len)
            onehot = (jnp.broadcast_to(buckets[page : page + 1, :], row.shape) == row).astype(F32).astype(BF)
            bias_wide[span, :] = lax.dot_general(
                onehot, spread, (((0,), (0,)), ((), ())), preferred_element_type=F32
            )
            key_query[span, :] = jnp.where(slot < page_info[1, local], page_info[0, local], -1)
            values_t[:, span] = values[page].astype(F32).T.astype(BF)
    tile_chips = 4
    tile = tile_chips * tok_dev
    lane = lax.broadcasted_iota(jnp.int32, (1, 128), 1)
    left = lane < tok_dev

    def one_tile(step, carry):
        rows = queries[pl.ds(step * tile_chips, tile_chips)].reshape(tile, width)
        owner = tok_query[pl.ds(step, 1), :]
        sums = []
        logs = []
        for h in range(heads):
            cols = slice(h * depth, (h + 1) * depth)
            rows_h = rows[:, cols]
            scores = jnp.concatenate(
                [
                    lax.dot_general(
                        keys[...].reshape(pages * page_len, width)[:, cols],
                        rows_h,
                        (((1,), (1,)), ((), ())),
                        preferred_element_type=F32,
                    )
                    for keys in (keys_a, keys_b)
                ],
                axis=0,
            )
            bias = jnp.concatenate([bias_wide[:, h * 128 : (h + 1) * 128]] * (tile // 128), axis=1)
            holder = jnp.concatenate([key_query[...]] * (tile // 128), axis=1)
            scores = jnp.where(holder == owner, scores + bias, MASKED)
            top = jnp.max(scores, axis=0, keepdims=True)
            weights = jnp.exp(scores - top)
            total = jnp.sum(weights, axis=0, keepdims=True)
            summed = jnp.dot(values_t[cols, :], weights.astype(BF), preferred_element_type=F32)
            sums.append(summed / total)
            logs.append(top + jnp.log(total))
        for half in range(tile // 128):
            lanes = slice(half * 128, (half + 1) * 128)
            upper = jnp.concatenate([sums[0][:, lanes], sums[1][:, lanes]], axis=0)
            lower = jnp.concatenate([sums[2][:, lanes], sums[3][:, lanes]], axis=0)
            first = jnp.where(left, upper, pltpu.roll(lower, tok_dev, 1))
            second = jnp.where(left, pltpu.roll(upper, tok_dev, 1), lower)
            stat_u = jnp.concatenate([logs[0][:, lanes], logs[1][:, lanes]] + [jnp.zeros((6, 128), F32)], axis=0)
            stat_l = jnp.concatenate([logs[2][:, lanes], logs[3][:, lanes]] + [jnp.zeros((6, 128), F32)], axis=0)
            stat_1 = jnp.where(left, stat_u, pltpu.roll(stat_l, tok_dev, 1))
            stat_2 = jnp.where(left, pltpu.roll(stat_u, tok_dev, 1), stat_l)
            for which, (block, stat) in enumerate(((first, stat_1), (second, stat_2))):
                chip = step * tile_chips + half * 2 + which
                out[chip, 0:128, :] = block.astype(BF)
                a, b, c = split_three(stat)
                packed = jnp.concatenate(
                    [a[0:2].astype(F32), b[0:2].astype(F32), c[0:2].astype(F32), jnp.zeros((10, 128), F32)], axis=0
                )
                out[chip, 128:144, :] = packed.astype(BF)
        return carry

    lax.fori_loop(0, chips // tile_chips, one_tile, 0)


def combine_kernel(parts, out_weight, out):
    chips = parts.shape[0]
    logs = []
    for chip in range(chips):
        stat = parts[chip, 128:144, :].astype(F32)
        logs.append(stat[0:2] + stat[2:4] + stat[4:6])
    top = logs[0]
    for chip in range(1, chips):
        top = jnp.maximum(top, logs[chip])
    scales = [jnp.exp(log - top) for log in logs]
    whole = scales[0]
    for chip in range(1, chips):
        whole = whole + scales[chip]
    sums = [jnp.zeros((64, 128), F32), jnp.zeros((64, 128), F32)]
    for chip in range(chips):
        share = scales[chip] / whole
        for r in range(2):
            sums[r] = sums[r] + share[r : r + 1] * parts[chip, r * 64 : (r + 1) * 64, :].astype(F32)
    joined = jnp.concatenate(sums, axis=0).T
    context = jnp.concatenate([joined[0:64], joined[64:128]], axis=1).astype(BF)
    out[...] = jnp.dot(context, out_weight[...], preferred_element_type=F32).astype(BF)


def vmem():
    return pl.BlockSpec(memory_space=pltpu.VMEM)


def per_device(
    doc_states,
    gain_attn,
    query_weight,
    cache_keys,
    cache_values,
    rel_bucket,
    bias_table,
    out_weight,
    gain_ffn,
    wi_gate,
    wi_up,
    wo_ffn,
    score_vector,
    query_lengths,
    doc_query,
    doc_of_token,
    page_table,
):
    tok_dev, model = doc_states.shape
    local_pages, page_len, local_width = cache_keys.shape
    page_size = lax.axis_size("page")
    head_size = lax.axis_size("head")
    chips = page_size // 2
    all_pages = page_table.shape[0]
    max_pages = all_pages // NQ
    page_rank = lax.axis_index("page")
    head_rank = lax.axis_index("head")
    core = page_rank % 2
    swap = [(i, i ^ 1) for i in range(page_size)]
    chip_groups = [[2 * i + c for i in range(chips)] for c in range(2)]

    other_keys = lax.ppermute(cache_keys, "page", swap)
    other_values = lax.ppermute(cache_values, "page", swap)
    other_bucket = lax.ppermute(rel_bucket, "page", swap)

    normed = rms_scale(doc_states, gain_attn).astype(BF)
    queries = jnp.dot(normed, query_weight, preferred_element_type=F32).astype(BF)
    copies = jnp.broadcast_to(queries[None], (chips, tok_dev, local_width))
    gathered = lax.all_to_all(copies, "page", 0, 0, axis_index_groups=chip_groups, tiled=True)

    doc_ids = jnp.arange(doc_query.shape[0], dtype=jnp.int32)
    served = lax.dynamic_slice_in_dim(doc_of_token.reshape(chips, 2, tok_dev), core, 1, 1).reshape(chips // 4, 4 * tok_dev)
    tok_query = jnp.sum(
        jnp.where(served[None] == doc_ids[:, None, None], doc_query[:, None, None], 0), axis=0
    )
    ours = page_rank * local_pages + jnp.arange(local_pages, dtype=jnp.int32)
    theirs = (page_rank ^ 1) * local_pages + jnp.arange(local_pages, dtype=jnp.int32)
    page_ids = jnp.concatenate([ours, theirs])
    slots = jnp.arange(all_pages, dtype=jnp.int32)
    located = jnp.sum(jnp.where(page_table[None, :] == page_ids[:, None], slots[None, :], 0), axis=1)
    owner = located // max_pages
    query_ids = jnp.arange(NQ, dtype=jnp.int32)
    owner_len = jnp.sum(jnp.where(owner[:, None] == query_ids[None, :], query_lengths[None, :], 0), axis=1)
    page_info = jnp.stack([owner, owner_len - (located % max_pages) * page_len])

    key_count = 2 * local_pages * page_len
    local_heads = bias_table.shape[1]
    partials = pl.pallas_call(
        attention_kernel,
        out_shape=jax.ShapeDtypeStruct((chips, 144, 128), BF),
        in_specs=[pl.BlockSpec(memory_space=pltpu.SMEM)] + [vmem()] * 9,
        out_specs=vmem(),
        scratch_shapes=[
            pltpu.VMEM((key_count, local_heads * 128), F32),
            pltpu.VMEM((key_count, 128), jnp.int32),
            pltpu.VMEM((local_width, key_count), BF),
        ],
        compiler_params=pltpu.CompilerParams(vmem_limit_bytes=32 << 20),
        name="attention",
    )(page_info, gathered, cache_keys, other_keys, cache_values, other_values, rel_bucket, other_bucket,
      bias_table, tok_query)
    returned = lax.all_to_all(partials, "page", 0, 0, axis_index_groups=chip_groups, tiled=True)
    projected = pl.pallas_call(
        combine_kernel,
        out_shape=jax.ShapeDtypeStruct((tok_dev, model), BF),
        in_specs=[vmem(), vmem()],
        out_specs=vmem(),
        compiler_params=pltpu.CompilerParams(vmem_limit_bytes=32 << 20),
        name="combine",
    )(returned, out_weight)

    own = tok_dev // head_size
    terms = lax.all_to_all(projected.reshape(head_size, own, model), "head", 0, 0, tiled=True)
    own_states = lax.dynamic_slice_in_dim(doc_states, head_rank * own, own, 0)
    hidden = own_states.astype(F32) + jnp.sum(terms.astype(F32), axis=0)
    normed_two = rms_scale(hidden, gain_ffn).astype(BF)
    hidden_score = jnp.sum(hidden * score_vector, axis=-1)
    spread = jnp.broadcast_to(normed_two[None], (head_size, own, model))
    rows = lax.all_to_all(spread, "head", 0, 0, tiled=True).reshape(tok_dev, model)
    gate = jnp.dot(rows, wi_gate, preferred_element_type=F32)
    upper = jnp.dot(rows, wi_up, preferred_element_type=F32)
    middle = (jax.nn.gelu(gate, approximate=True) * upper).astype(BF)
    down_score = jnp.sum(wo_ffn.astype(F32) * score_vector, axis=-1)
    tok_part = jnp.sum(middle.astype(F32) * down_score, axis=-1)
    tok_ids = jnp.arange(tok_dev, dtype=jnp.int32)
    mine = tok_ids[:, None] == head_rank * own + jnp.arange(own, dtype=jnp.int32)[None, :]
    tok_part = tok_part + jnp.sum(jnp.where(mine, hidden_score[None, :], 0.0), axis=1)

    doc_dev = doc_query.shape[0] // page_size
    own_docs = lax.dynamic_slice_in_dim(doc_of_token, page_rank * tok_dev, tok_dev, 0)
    doc_lanes = jnp.arange(page_size * 128, dtype=jnp.int32).reshape(page_size, 128)
    doc_at = jnp.where(doc_lanes % 128 < doc_dev, (doc_lanes // 128) * doc_dev + doc_lanes % 128, -1)
    doc_sums = jnp.sum(
        jnp.where(own_docs[:, None, None] == doc_at[None], tok_part[:, None, None], 0.0), axis=0
    )
    arrived = lax.all_to_all(doc_sums, "page", 0, 0, tiled=True)
    pooled = lax.psum(jnp.sum(arrived, axis=0), "head")[:doc_dev]
    mine_docs = page_rank * doc_dev + jnp.arange(doc_dev, dtype=jnp.int32)
    counts = jnp.sum((doc_of_token[:, None] == mine_docs[None, :]).astype(F32), axis=0)
    return pooled / counts


def solution(mesh):
    return jax.shard_map(
        per_device,
        mesh=mesh,
        in_specs=(
            P("page", None),
            P(),
            P(None, "head"),
            P("page", None, "head"),
            P("page", None, "head"),
            P("page", None),
            P(None, "head"),
            P("head", None),
            P(),
            P(None, "head"),
            P(None, "head"),
            P("head", None),
            P(),
            P(),
            P(),
            P(),
            P(),
        ),
        out_specs=P("page"),
        check_vma=False,
    )
```

```python
import jax
import jax.numpy as jnp
from jax import lax
from jax.experimental import pallas as pl
from jax.experimental.pallas import tpu as pltpu
from jax.sharding import PartitionSpec as P

NQ = 8
MASKED = -1e30
BF = jnp.bfloat16
F32 = jnp.float32


def rms_scale(values, gain):
    values = values.astype(F32)
    return values * lax.rsqrt(jnp.mean(values * values, axis=-1, keepdims=True) + 1e-06) * gain


def split_three(value):
    first = value.astype(BF)
    rest = value - first.astype(F32)
    second = rest.astype(BF)
    third = (rest - second.astype(F32)).astype(BF)
    return first, second, third


def project_kernel(states, gain, weight, out, states_here, gain_here, weight_here, arrivals):
    pairs = ((states, states_here), (gain, gain_here), (weight, weight_here))
    copies = [pltpu.make_async_copy(there, here, arrivals.at[i]) for i, (there, here) in enumerate(pairs)]
    for copy in copies:
        copy.start()
    copies[0].wait()
    copies[1].wait()
    normed = rms_scale(states_here[...], gain_here[...]).astype(BF)
    copies[2].wait()
    queries = jnp.dot(normed, weight_here[...], preferred_element_type=F32).astype(BF)
    for chip in range(out.shape[0]):
        out[chip] = queries


def prepare_kernel(rank, page_table, query_lengths, k0, k1, k2, k3, v0, v1, v2, v3, b01, b23, bias_table, doc_query,
                   doc_rows, keys_aug, values_t, extra, info, held_caches, arrivals):
    pages, page_len, width = k0.shape
    heads = bias_table.shape[0]
    depth = width // heads
    bucket_count = bias_table.shape[1]
    slot_count = page_table.shape[0]
    max_pages = slot_count // NQ
    tokens = extra.shape[0]
    tok_dev = doc_rows.shape[1] // 2
    row_chips = 4
    copies = [
        pltpu.make_async_copy(cache, held_caches.at[i], arrivals.at[i])
        for i, cache in enumerate((k0, k1, k2, k3, v0, v1, v2, v3))
    ]
    for copy in copies:
        copy.start()
    core = rank[0] % 2
    chip = rank[0] // 2
    pair = chip - chip % 2
    base = (chip // row_chips * row_chips + chip % 2) * 2 * pages
    held = 4 * pages
    for s in range(slot_count):
        place = page_table[s] - base
        near = (place >= 0) & (place < 2 * pages)
        far = (place >= 4 * pages) & (place < 6 * pages)
        place = jnp.where(near, place, jnp.where(far, place - 2 * pages, held))
        info[0, place] = s // max_pages
        info[1, place] = query_lengths[s // max_pages] - (s % max_pages) * page_len
    doc_count = doc_query.shape[1]
    left = lax.broadcasted_iota(jnp.int32, (1, 128), 1) < tok_dev
    doc_id = lax.broadcasted_iota(jnp.int32, (doc_count, 128), 0)
    blocks = []
    for y in range(tokens // (2 * tok_dev)):
        two = doc_rows[pl.ds(y * row_chips + pair % row_chips, 2), :]
        turned = pltpu.roll(two, tok_dev, 1)
        row = jnp.where(
            left,
            jnp.where(core == 0, two[0:1], turned[0:1]),
            jnp.where(core == 0, turned[1:2], two[1:2]),
        )
        blocks.append((doc_id == row).astype(F32).astype(BF))
    member = jnp.concatenate(blocks, axis=1)
    asked = jnp.broadcast_to(doc_query[...].astype(F32), (128, doc_count)).astype(BF)
    tok_query = jnp.dot(asked, member, preferred_element_type=F32)
    mark = lax.broadcasted_iota(jnp.int32, (128, tokens), 0) % 64
    columns = jnp.where(
        mark < NQ,
        jnp.where(tok_query == mark.astype(F32), 0.0, MASKED),
        jnp.where(mark == NQ, MASKED, jnp.where(mark < NQ + 4, 1.0, 0.0)),
    )
    extra[...] = columns.T.astype(BF)
    low = lax.broadcasted_iota(jnp.int32, (1, 128), 1) < depth
    table = jnp.concatenate([bias_table[...], jnp.zeros((8 - heads, bucket_count), F32)], axis=0).T
    col = lax.broadcasted_iota(jnp.int32, (bucket_count, 128), 1) % 64
    spreads = []
    for h in range(heads):
        a, b, c = split_three(jnp.broadcast_to(table[:, h : h + 1], (bucket_count, 128)))
        third = jnp.where(col == NQ + 3, c.astype(F32), 0.0)
        spreads.append(
            jnp.where(col == NQ + 1, a.astype(F32), jnp.where(col == NQ + 2, b.astype(F32), third)).astype(BF)
        )
    spread = jnp.concatenate(spreads, axis=1)
    bucket_row = lax.broadcasted_iota(jnp.int32, (bucket_count, page_len), 0)
    slot = lax.broadcasted_iota(jnp.int32, (page_len, 128), 0)
    key_col = lax.broadcasted_iota(jnp.int32, (page_len, 128), 1) % 64
    mine = ((chip % row_chips // 2) * 2 + core) * pages
    for copy in copies:
        copy.wait()
    for part, (buckets, first) in enumerate(((b01, 0), (b01, pages), (b23, 0), (b23, pages))):
        for page in range(pages):
            place = (mine ^ (part * pages)) + page
            span = pl.ds((part * pages + page) * page_len, page_len)
            bucket = buckets[first + page : first + page + 1, :]
            onehot = (jnp.broadcast_to(bucket, bucket_row.shape) == bucket_row).astype(F32).astype(BF)
            bias = lax.dot_general(onehot, spread, (((0,), (0,)), ((), ())), preferred_element_type=F32)
            holder = jnp.where(slot < info[1, place], info[0, place], NQ)
            marks = (key_col == holder).astype(F32)
            key = held_caches[part, page].astype(F32)
            for h in range(heads):
                keep = low if h % 2 == 0 else jnp.logical_not(low)
                half = key[:, (h // 2) * 128 : (h // 2 + 1) * 128]
                keys_aug[h, span, :] = jnp.where(keep, half, bias[:, h * 128 : (h + 1) * 128] + marks).astype(BF)
            values_t[:, span] = held_caches[4 + part, page].astype(F32).T.astype(BF)


def attention_kernel(queries, keys_aug, values_t, extra, out, rows_aug):
    chips, tok_dev, width = queries.shape
    heads = keys_aug.shape[0]
    depth = width // heads
    low = lax.broadcasted_iota(jnp.int32, (1, 128), 1) < depth
    left = lax.broadcasted_iota(jnp.int32, (1, 128), 1) < tok_dev
    rows = queries[...].reshape(chips * tok_dev, width)
    for h in range(heads):
        half = rows[:, (h // 2) * 128 : (h // 2 + 1) * 128].astype(F32)
        keep = low if h % 2 == 0 else jnp.logical_not(low)
        rows_aug[h] = jnp.where(keep, half, extra[...].astype(F32)).astype(BF)
    sums = []
    logs = []
    for h in range(heads):
        scores = lax.dot_general(
            keys_aug[h], rows_aug[h], (((1,), (1,)), ((), ())), preferred_element_type=F32
        )
        top = jnp.max(scores, axis=0, keepdims=True)
        weights = jnp.exp(scores - top)
        total = jnp.sum(weights, axis=0, keepdims=True)
        summed = jnp.dot(
            values_t[h * depth : (h + 1) * depth, :], weights.astype(BF), preferred_element_type=F32
        )
        sums.append(summed / total)
        logs.append(top + jnp.log(total))
    for duo in range(chips // 2):
        lanes = slice(duo * 128, (duo + 1) * 128)
        pad = [jnp.zeros((6, 128), F32)]
        upper = jnp.concatenate([sums[0][:, lanes], sums[1][:, lanes]], axis=0)
        lower = jnp.concatenate([sums[2][:, lanes], sums[3][:, lanes]], axis=0)
        stat_upper = jnp.concatenate([logs[0][:, lanes], logs[1][:, lanes]] + pad, axis=0)
        stat_lower = jnp.concatenate([logs[2][:, lanes], logs[3][:, lanes]] + pad, axis=0)
        block = (
            jnp.where(left, upper, pltpu.roll(lower, tok_dev, 1)),
            jnp.where(left, pltpu.roll(upper, tok_dev, 1), lower),
        )
        stat = (
            jnp.where(left, stat_upper, pltpu.roll(stat_lower, tok_dev, 1)),
            jnp.where(left, pltpu.roll(stat_upper, tok_dev, 1), stat_lower),
        )
        for which in range(2):
            a, b, c = split_three(stat[which])
            packed = [a[0:2].astype(F32), b[0:2].astype(F32), c[0:2].astype(F32), jnp.zeros((2, 128), F32)]
            out[duo * 2 + which, 0:128, :] = block[which].astype(BF)
            out[duo * 2 + which, 128:136, :] = jnp.concatenate(packed, axis=0).astype(BF)


def combine_kernel(parts, out_weight, out):
    chips = parts.shape[0]
    logs = []
    for chip in range(chips):
        stat = parts[chip, 128:136, :].astype(F32)
        logs.append(stat[0:2] + stat[2:4] + stat[4:6])
    top = logs[0]
    for chip in range(1, chips):
        top = jnp.maximum(top, logs[chip])
    scales = [jnp.exp(log - top) for log in logs]
    whole = scales[0]
    for chip in range(1, chips):
        whole = whole + scales[chip]
    sums = [jnp.zeros((64, 128), F32), jnp.zeros((64, 128), F32)]
    for chip in range(chips):
        share = scales[chip] / whole
        for r in range(2):
            sums[r] = sums[r] + share[r : r + 1] * parts[chip, r * 64 : (r + 1) * 64, :].astype(F32)
    joined = jnp.concatenate(sums, axis=0).T
    context = jnp.concatenate([joined[0:64], joined[64:128]], axis=1).astype(BF)
    out[...] = jnp.dot(context, out_weight[...], preferred_element_type=F32).astype(BF)


def norm_kernel(terms, states, gain, score_vector, out, score):
    hidden = states[...].astype(F32)
    for source in range(terms.shape[0]):
        hidden = hidden + terms[source].astype(F32)
    normed = rms_scale(hidden, gain[...]).astype(BF)
    for target in range(out.shape[0]):
        out[target] = normed
    score[...] = jnp.broadcast_to(jnp.sum(hidden * score_vector[...], axis=-1, keepdims=True), score.shape)


def feed_kernel(rows, gate_weight, up_weight, down_score, own_score, own_docs, out, gate, upper):
    step = pl.program_id(0)

    @pl.when(step == 0)
    def _():
        gate[...] = jnp.zeros_like(gate)
        upper[...] = jnp.zeros_like(upper)

    part = rows[...]
    gate[...] += jnp.dot(part, gate_weight[...], preferred_element_type=F32)
    upper[...] += jnp.dot(part, up_weight[...], preferred_element_type=F32)

    @pl.when(step == pl.num_programs(0) - 1)
    def _():
        middle = (jax.nn.gelu(gate[...], approximate=True) * upper[...]).astype(BF).astype(F32)
        tok_score = jnp.sum(middle * down_score[...], axis=-1, keepdims=True) + own_score[...]
        docs = own_docs[...]
        doc_dev = 256 // out.shape[0]
        lane = lax.broadcasted_iota(jnp.int32, (docs.shape[0], 128), 1)
        holder = (docs // doc_dev == lane).astype(F32).astype(BF)
        placed = jnp.where(docs % doc_dev == lane, tok_score, 0.0)
        sums = jnp.zeros((128, 128), F32)
        for piece in split_three(placed):
            sums += lax.dot_general(holder, piece, (((0,), (0,)), ((), ())), preferred_element_type=F32)
        out[...] = sums[0 : out.shape[0]]


def vmem():
    return pl.BlockSpec(memory_space=pltpu.VMEM)


def smem():
    return pl.BlockSpec(memory_space=pltpu.SMEM)


def hbm():
    return pl.BlockSpec(memory_space=pltpu.HBM)


def anywhere():
    return pl.BlockSpec(memory_space=pl.ANY)


def call(kernel, name, shapes, specs, scratch=()):
    single = not isinstance(shapes, (list, tuple))
    return pl.pallas_call(
        kernel,
        out_shape=shapes,
        in_specs=specs,
        out_specs=vmem() if single else [vmem()] * len(shapes),
        scratch_shapes=list(scratch),
        compiler_params=pltpu.CompilerParams(vmem_limit_bytes=40 << 20),
        name=name,
    )


def per_device(
    doc_states,
    gain_attn,
    query_weight,
    cache_keys,
    cache_values,
    rel_bucket,
    bias_table,
    out_weight,
    gain_ffn,
    wi_gate,
    wi_up,
    wo_ffn,
    score_vector,
    query_lengths,
    doc_query,
    doc_of_token,
    page_table,
):
    shape = jax.ShapeDtypeStruct
    tok_dev, model = doc_states.shape
    local_pages, page_len, local_width = cache_keys.shape
    local_heads = bias_table.shape[1]
    page_size = lax.axis_size("page")
    head_size = lax.axis_size("head")
    page_rank = lax.axis_index("page")
    head_rank = lax.axis_index("head")
    group = page_size // 4
    groups = [
        [y * 8 + (x + side) * 2 + core for y in range(4) for side in range(2)] for x in (0, 2) for core in range(2)
    ]
    core_swap = [(i, i ^ 1) for i in range(page_size)]
    side_swap = [(i, i ^ 4) for i in range(page_size)]

    def swap(value, pairs):
        return lax.ppermute(value, "page", pairs)

    keys_side = swap(cache_keys, side_swap)
    values_side = swap(cache_values, side_swap)
    keys_core = swap(cache_keys, core_swap)
    values_core = swap(cache_values, core_swap)
    bucket_pair = jnp.concatenate([rel_bucket, swap(rel_bucket, core_swap)])
    bucket_side = swap(bucket_pair, side_swap)
    keys_far = swap(keys_side, core_swap)
    values_far = swap(values_side, core_swap)

    copies = call(
        project_kernel, "project", shape((group, tok_dev, local_width), BF), [hbm()] * 3,
        [
            pltpu.VMEM((tok_dev, model), BF),
            pltpu.VMEM((1, model), F32),
            pltpu.VMEM((model, local_width), BF),
            pltpu.SemaphoreType.DMA((3,)),
        ],
    )(doc_states, gain_attn.reshape(1, model), query_weight)
    gathered = lax.all_to_all(copies, "page", 0, 0, axis_index_groups=groups, tiled=True)

    key_count = 4 * local_pages * page_len
    keys_aug, values_t, extra = call(
        prepare_kernel,
        "prepare",
        [
            shape((local_heads, key_count, 128), BF),
            shape((local_width, key_count), BF),
            shape((group * tok_dev, 128), BF),
        ],
        [smem()] * 3 + [hbm()] + [anywhere()] * 3 + [hbm()] + [anywhere()] * 3 + [vmem()] * 5,
        [
            pltpu.SMEM((2, 4 * local_pages + 1), jnp.int32),
            pltpu.VMEM((8, local_pages, page_len, local_width), BF),
            pltpu.SemaphoreType.DMA((8,)),
        ],
    )(
        page_rank.reshape(1),
        page_table,
        query_lengths,
        cache_keys,
        keys_core,
        keys_side,
        keys_far,
        cache_values,
        values_core,
        values_side,
        values_far,
        bucket_pair,
        bucket_side,
        bias_table.T,
        doc_query.reshape(1, -1),
        doc_of_token.reshape(-1, 2 * tok_dev),
    )
    partials = call(
        attention_kernel,
        "attention",
        shape((group, 136, 128), BF),
        [vmem()] * 4,
        [pltpu.VMEM((local_heads, group * tok_dev, 128), BF)],
    )(gathered, keys_aug, values_t, extra)
    returned = lax.all_to_all(partials, "page", 0, 0, axis_index_groups=groups, tiled=True)
    projected = call(combine_kernel, "combine", shape((tok_dev, model), BF), [vmem()] * 2)(returned, out_weight)

    own = tok_dev // head_size
    terms = lax.all_to_all(projected.reshape(head_size, own, model), "head", 0, 0, tiled=True)
    own_states = lax.dynamic_slice_in_dim(doc_states, head_rank * own, own, 0)
    spread, hidden_score = call(
        norm_kernel,
        "norm",
        [shape((head_size, own, model), BF), shape((own, 128), F32)],
        [vmem()] * 4,
    )(terms, own_states, gain_ffn.reshape(1, model), score_vector.reshape(1, model))
    rows = lax.all_to_all(spread, "head", 0, 0, tiled=True).reshape(tok_dev, model)
    down_score = jnp.sum(wo_ffn.astype(F32) * score_vector, axis=-1)
    token = jnp.arange(tok_dev, dtype=jnp.int32)[:, None]
    own_score = jnp.where(token // own == head_rank, jnp.tile(hidden_score[:, :1], (head_size, 1)), 0.0)
    own_docs = lax.dynamic_slice_in_dim(doc_of_token, page_rank * tok_dev, tok_dev, 0)[:, None]
    doc_dev = doc_query.shape[0] // page_size
    hidden_units = wi_gate.shape[1]
    steps = 4
    doc_sums = pl.pallas_call(
        feed_kernel,
        out_shape=shape((page_size, 128), F32),
        grid=(steps,),
        in_specs=[
            pl.BlockSpec((tok_dev, model // steps), lambda i: (0, i)),
            pl.BlockSpec((model // steps, hidden_units), lambda i: (i, 0)),
            pl.BlockSpec((model // steps, hidden_units), lambda i: (i, 0)),
            pl.BlockSpec((1, hidden_units), lambda i: (0, 0)),
            pl.BlockSpec((tok_dev, 1), lambda i: (0, 0)),
            pl.BlockSpec((tok_dev, 1), lambda i: (0, 0)),
        ],
        out_specs=pl.BlockSpec((page_size, 128), lambda i: (0, 0)),
        scratch_shapes=[pltpu.VMEM((tok_dev, hidden_units), F32)] * 2,
        compiler_params=pltpu.CompilerParams(vmem_limit_bytes=40 << 20),
        name="feed",
    )(rows, wi_gate, wi_up, down_score.reshape(1, -1), own_score, own_docs)
    doc_sums = doc_sums.reshape(page_size, 1, 128)
    arrived = lax.all_to_all(doc_sums, "page", 0, 0, tiled=True)
    pooled = jnp.broadcast_to(jnp.sum(arrived, axis=0), (head_size, 1, 128))
    pooled = jnp.sum(lax.all_to_all(pooled, "head", 0, 0, tiled=True), axis=(0, 1))[:doc_dev]
    mine_docs = page_rank * doc_dev + jnp.arange(doc_dev, dtype=jnp.int32)
    counts = jnp.sum((doc_of_token[:, None] == mine_docs[None, :]).astype(F32), axis=0)
    return pooled / counts


def solution(mesh):
    return jax.shard_map(
        per_device,
        mesh=mesh,
        in_specs=(
            P("page", None),
            P(),
            P(None, "head"),
            P("page", None, "head"),
            P("page", None, "head"),
            P("page", None),
            P(None, "head"),
            P("head", None),
            P(),
            P(None, "head"),
            P(None, "head"),
            P("head", None),
            P(),
            P(),
            P(),
            P(),
            P(),
        ),
        out_specs=P("page"),
        check_vma=False,
    )
```

```python
import functools

import jax
import jax.numpy as jnp
from jax import lax
from jax.experimental import pallas as pl
from jax.experimental.pallas import tpu as pltpu
from jax.sharding import PartitionSpec as P

NQ = 8
DOCS = 256
MASKED = -1e30
BF = jnp.bfloat16
F32 = jnp.float32


def rms_scale(values, gain):
    values = values.astype(F32)
    return values * lax.rsqrt(jnp.mean(values * values, axis=-1, keepdims=True) + 1e-06) * gain


def split_three(value):
    first = value.astype(BF)
    rest = value - first.astype(F32)
    second = rest.astype(BF)
    third = (rest - second.astype(F32)).astype(BF)
    return first, second, third


def project_kernel(states, gain, weight, out, states_here, gain_here, weight_here, arrivals):
    pairs = ((states, states_here), (gain, gain_here), (weight, weight_here))
    copies = [pltpu.make_async_copy(there, here, arrivals.at[i]) for i, (there, here) in enumerate(pairs)]
    for copy in copies:
        copy.start()
    copies[0].wait()
    copies[1].wait()
    normed = rms_scale(states_here[...], gain_here[...]).astype(BF)
    copies[2].wait()
    queries = jnp.dot(normed, weight_here[...], preferred_element_type=F32).astype(BF)
    for chip in range(out.shape[0]):
        out[chip] = queries


def columns_kernel(rank, doc_query, doc_rows, extra, query_here, rows_here, arrivals):
    copies = [
        pltpu.make_async_copy(doc_query, query_here, arrivals.at[0]),
        pltpu.make_async_copy(doc_rows, rows_here, arrivals.at[1]),
    ]
    for copy in copies:
        copy.start()
    tokens = extra.shape[0]
    tok_dev = doc_rows.shape[1] // 2
    row_chips = 4
    core = rank[0] % 2
    chip = rank[0] // 2
    pair = chip - chip % 2
    doc_count = doc_query.shape[1]
    left = lax.broadcasted_iota(jnp.int32, (1, 128), 1) < tok_dev
    doc_id = lax.broadcasted_iota(jnp.int32, (doc_count, 128), 0)
    for copy in copies:
        copy.wait()
    blocks = []
    for y in range(tokens // (2 * tok_dev)):
        two = rows_here[pl.ds(y * row_chips + pair % row_chips, 2), :]
        turned = pltpu.roll(two, tok_dev, 1)
        row = jnp.where(
            left,
            jnp.where(core == 0, two[0:1], turned[0:1]),
            jnp.where(core == 0, turned[1:2], two[1:2]),
        )
        blocks.append((doc_id == row).astype(F32).astype(BF))
    member = jnp.concatenate(blocks, axis=1)
    asked = jnp.broadcast_to(query_here[...].astype(F32), (128, doc_count)).astype(BF)
    tok_query = jnp.dot(asked, member, preferred_element_type=F32)
    mark = lax.broadcasted_iota(jnp.int32, (128, tokens), 0) % 64
    columns = jnp.where(
        mark < NQ,
        jnp.where(tok_query == mark.astype(F32), 0.0, MASKED),
        jnp.where(mark == NQ, MASKED, jnp.where(mark < NQ + 4, 1.0, 0.0)),
    )
    extra[...] = columns.T.astype(BF)


def prepare_kernel(rank, k0, k1, v0, v1, b0, b1, bias_table, page_table, query_lengths, keys_aug, values_t,
                   held, bucket_here, table_here, slots_here, lengths_here, info, arrivals, *, side):
    pages, page_len, width = k0.shape
    heads, bucket_count = bias_table.shape
    depth = width // heads
    slot_count = page_table.shape[0]
    max_pages = slot_count // NQ
    row_chips = 4
    pairs = [(page_table, slots_here), (query_lengths, lengths_here), (bias_table, table_here)]
    pairs += [(b0, bucket_here.at[0]), (b1, bucket_here.at[1])]
    pairs += [(cache, held.at[i]) for i, cache in enumerate((k0, k1, v0, v1))]
    copies = [pltpu.make_async_copy(there, here, arrivals.at[i]) for i, (there, here) in enumerate(pairs)]
    for copy in copies:
        copy.start()
    core = rank[0] % 2
    chip = rank[0] // 2
    base = (chip // row_chips * row_chips + chip % 2) * 2 * pages
    count = 4 * pages
    copies[0].wait()
    copies[1].wait()
    for s in range(slot_count):
        place = slots_here[s] - base
        near = (place >= 0) & (place < 2 * pages)
        far = (place >= 4 * pages) & (place < 6 * pages)
        place = jnp.where(near, place, jnp.where(far, place - 2 * pages, count))
        info[0, place] = s // max_pages
        info[1, place] = lengths_here[s // max_pages] - (s % max_pages) * page_len
    low = lax.broadcasted_iota(jnp.int32, (1, 128), 1) < depth
    col = lax.broadcasted_iota(jnp.int32, (bucket_count, 128), 1) % 64
    copies[2].wait()
    table = jnp.concatenate([table_here[...], jnp.zeros((8 - heads, bucket_count), F32)], axis=0).T
    spreads = []
    for h in range(heads):
        a, b, c = split_three(jnp.broadcast_to(table[:, h : h + 1], (bucket_count, 128)))
        third = jnp.where(col == NQ + 3, c.astype(F32), 0.0)
        spreads.append(
            jnp.where(col == NQ + 1, a.astype(F32), jnp.where(col == NQ + 2, b.astype(F32), third)).astype(BF)
        )
    spread = jnp.concatenate(spreads, axis=1)
    bucket_row = lax.broadcasted_iota(jnp.int32, (bucket_count, page_len), 0)
    slot = lax.broadcasted_iota(jnp.int32, (page_len, 128), 0)
    key_col = lax.broadcasted_iota(jnp.int32, (page_len, 128), 1) % 64
    mine = ((chip % row_chips // 2) * 2 + core) * pages
    for copy in copies[3:]:
        copy.wait()
    for part in range(2):
        for page in range(pages):
            place = (mine ^ ((2 * side + part) * pages)) + page
            span = pl.ds((part * pages + page) * page_len, page_len)
            bucket = bucket_here[part, page : page + 1, :]
            onehot = (jnp.broadcast_to(bucket, bucket_row.shape) == bucket_row).astype(F32).astype(BF)
            bias = lax.dot_general(onehot, spread, (((0,), (0,)), ((), ())), preferred_element_type=F32)
            holder = jnp.where(slot < info[1, place], info[0, place], NQ)
            marks = (key_col == holder).astype(F32)
            key = held[part, page].astype(F32)
            for h in range(heads):
                keep = low if h % 2 == 0 else jnp.logical_not(low)
                half = key[:, (h // 2) * 128 : (h // 2 + 1) * 128]
                keys_aug[h, span, :] = jnp.where(keep, half, bias[:, h * 128 : (h + 1) * 128] + marks).astype(BF)
            values_t[:, span] = held[2 + part, page].astype(F32).T.astype(BF)


def attention_kernel(queries, keys_near, keys_far, values_near, values_far, extra, out, rows_aug):
    chips, tok_dev, width = queries.shape
    heads = keys_near.shape[0]
    depth = width // heads
    low = lax.broadcasted_iota(jnp.int32, (1, 128), 1) < depth
    left = lax.broadcasted_iota(jnp.int32, (1, 128), 1) < tok_dev
    rows = queries[...].reshape(chips * tok_dev, width)
    for h in range(heads):
        half = rows[:, (h // 2) * 128 : (h // 2 + 1) * 128].astype(F32)
        keep = low if h % 2 == 0 else jnp.logical_not(low)
        rows_aug[h] = jnp.where(keep, half, extra[...].astype(F32)).astype(BF)
    sums = []
    logs = []
    for h in range(heads):
        span = slice(h * depth, (h + 1) * depth)
        scores = [
            lax.dot_general(keys[h], rows_aug[h], (((1,), (1,)), ((), ())), preferred_element_type=F32)
            for keys in (keys_near, keys_far)
        ]
        top = jnp.maximum(
            jnp.max(scores[0], axis=0, keepdims=True), jnp.max(scores[1], axis=0, keepdims=True)
        )
        total = jnp.zeros_like(top)
        summed = jnp.zeros((depth, chips * tok_dev), F32)
        for part, values in zip(scores, (values_near, values_far)):
            weights = jnp.exp(part - top)
            total += jnp.sum(weights, axis=0, keepdims=True)
            summed += jnp.dot(values[span, :], weights.astype(BF), preferred_element_type=F32)
        sums.append(summed / total)
        logs.append(top + jnp.log(total))
    for duo in range(chips // 2):
        lanes = slice(duo * 128, (duo + 1) * 128)
        pad = [jnp.zeros((6, 128), F32)]
        upper = jnp.concatenate([sums[0][:, lanes], sums[1][:, lanes]], axis=0)
        lower = jnp.concatenate([sums[2][:, lanes], sums[3][:, lanes]], axis=0)
        stat_upper = jnp.concatenate([logs[0][:, lanes], logs[1][:, lanes]] + pad, axis=0)
        stat_lower = jnp.concatenate([logs[2][:, lanes], logs[3][:, lanes]] + pad, axis=0)
        block = (
            jnp.where(left, upper, pltpu.roll(lower, tok_dev, 1)),
            jnp.where(left, pltpu.roll(upper, tok_dev, 1), lower),
        )
        stat = (
            jnp.where(left, stat_upper, pltpu.roll(stat_lower, tok_dev, 1)),
            jnp.where(left, pltpu.roll(stat_upper, tok_dev, 1), stat_lower),
        )
        for which in range(2):
            a, b, c = split_three(stat[which])
            packed = [a[0:2].astype(F32), b[0:2].astype(F32), c[0:2].astype(F32), jnp.zeros((2, 128), F32)]
            out[duo * 2 + which, 0:128, :] = block[which].astype(BF)
            out[duo * 2 + which, 128:136, :] = jnp.concatenate(packed, axis=0).astype(BF)


def combine_kernel(parts, out_weight, out, weight_here, arrival):
    copy = pltpu.make_async_copy(out_weight, weight_here, arrival)
    copy.start()
    chips = parts.shape[0]
    logs = []
    for chip in range(chips):
        stat = parts[chip, 128:136, :].astype(F32)
        logs.append(stat[0:2] + stat[2:4] + stat[4:6])
    top = logs[0]
    for chip in range(1, chips):
        top = jnp.maximum(top, logs[chip])
    scales = [jnp.exp(log - top) for log in logs]
    whole = scales[0]
    for chip in range(1, chips):
        whole = whole + scales[chip]
    sums = [jnp.zeros((64, 128), F32), jnp.zeros((64, 128), F32)]
    for chip in range(chips):
        share = scales[chip] / whole
        for r in range(2):
            sums[r] = sums[r] + share[r : r + 1] * parts[chip, r * 64 : (r + 1) * 64, :].astype(F32)
    joined = jnp.concatenate(sums, axis=0).T
    context = jnp.concatenate([joined[0:64], joined[64:128]], axis=1).astype(BF)
    copy.wait()
    out[...] = jnp.dot(context, weight_here[...], preferred_element_type=F32).astype(BF)


def norm_kernel(terms, states, gain, score_vector, out, score):
    hidden = states[...].astype(F32)
    for source in range(terms.shape[0]):
        hidden = hidden + terms[source].astype(F32)
    normed = rms_scale(hidden, gain[...]).astype(BF)
    for target in range(out.shape[0]):
        out[target] = normed
    score[...] = jnp.broadcast_to(jnp.sum(hidden * score_vector[...], axis=-1, keepdims=True), score.shape)


def feed_kernel(rows, gate_weight, up_weight, down_score, own_score, own_docs, out, gate_here, up_here, arrivals):
    steps = gate_here.shape[0]
    size = rows.shape[1] // steps
    copies = []
    for i in range(steps):
        for j, (there, here) in enumerate(((gate_weight, gate_here), (up_weight, up_here))):
            copies.append(
                pltpu.make_async_copy(there.at[pl.ds(i * size, size)], here.at[i], arrivals.at[2 * i + j])
            )
    for copy in copies:
        copy.start()
    gate = jnp.zeros((rows.shape[0], gate_weight.shape[1]), F32)
    upper = gate
    for i in range(steps):
        part = rows[:, i * size : (i + 1) * size]
        copies[2 * i].wait()
        gate += jnp.dot(part, gate_here[i], preferred_element_type=F32)
        copies[2 * i + 1].wait()
        upper += jnp.dot(part, up_here[i], preferred_element_type=F32)
    middle = (jax.nn.gelu(gate, approximate=True) * upper).astype(BF).astype(F32)
    tok_score = jnp.sum(middle * down_score[...], axis=-1, keepdims=True) + own_score[...]
    docs = own_docs[...]
    doc_dev = DOCS // out.shape[0]
    lane = lax.broadcasted_iota(jnp.int32, (docs.shape[0], 128), 1)
    holder = (docs // doc_dev == lane).astype(F32).astype(BF)
    placed = jnp.where(docs % doc_dev == lane, tok_score, 0.0)
    sums = jnp.zeros((128, 128), F32)
    for piece in split_three(placed):
        sums += lax.dot_general(holder, piece, (((0,), (0,)), ((), ())), preferred_element_type=F32)
    out[...] = sums[0 : out.shape[0]]


def fold_kernel(terms, out):
    out[...] = jnp.broadcast_to(jnp.sum(terms[...], axis=0, keepdims=True), out.shape)


def vmem():
    return pl.BlockSpec(memory_space=pltpu.VMEM)


def smem():
    return pl.BlockSpec(memory_space=pltpu.SMEM)


def in_hbm(value):
    return pltpu.with_memory_space_constraint(value, pltpu.HBM)


def hbm():
    return pl.BlockSpec(memory_space=pltpu.HBM)


def anywhere():
    return pl.BlockSpec(memory_space=pl.ANY)


def call(kernel, name, shapes, specs, scratch=()):
    single = not isinstance(shapes, (list, tuple))
    return pl.pallas_call(
        kernel,
        out_shape=shapes,
        in_specs=specs,
        out_specs=vmem() if single else [vmem()] * len(shapes),
        scratch_shapes=list(scratch),
        compiler_params=pltpu.CompilerParams(vmem_limit_bytes=40 << 20),
        name=name,
    )


def per_device(
    doc_states,
    gain_attn,
    query_weight,
    cache_keys,
    cache_values,
    rel_bucket,
    bias_table,
    out_weight,
    gain_ffn,
    wi_gate,
    wi_up,
    wo_ffn,
    score_vector,
    query_lengths,
    doc_query,
    doc_of_token,
    page_table,
):
    shape = jax.ShapeDtypeStruct
    tok_dev, model = doc_states.shape
    local_pages, page_len, local_width = cache_keys.shape
    local_heads = bias_table.shape[1]
    page_size = lax.axis_size("page")
    head_size = lax.axis_size("head")
    page_rank = lax.axis_index("page")
    head_rank = lax.axis_index("head")
    group = page_size // 4
    groups = [
        [y * 8 + (x + side) * 2 + core for y in range(4) for side in range(2)] for x in (0, 2) for core in range(2)
    ]
    core_swap = [(i, i ^ 1) for i in range(page_size)]
    side_swap = [(i, i ^ 4) for i in range(page_size)]

    def swap(value, pairs):
        return lax.ppermute(value, "page", pairs)

    far_swap = [(i, i ^ 5) for i in range(page_size)]
    copies = call(
        project_kernel, "project", shape((group, tok_dev, local_width), BF), [hbm()] * 3,
        [
            pltpu.VMEM((tok_dev, model), BF),
            pltpu.VMEM((1, model), F32),
            pltpu.VMEM((model, local_width), BF),
            pltpu.SemaphoreType.DMA((3,)),
        ],
    )(in_hbm(doc_states), in_hbm(gain_attn.reshape(1, model)), in_hbm(query_weight))
    sent_keys, sent_values, copies = lax.optimization_barrier((cache_keys, cache_values, copies))
    keys_side = swap(sent_keys, side_swap)
    values_side = swap(sent_values, side_swap)
    keys_core = swap(cache_keys, core_swap)
    values_core = swap(cache_values, core_swap)
    bucket_core = swap(rel_bucket, core_swap)
    bucket_side = swap(rel_bucket, side_swap)
    bucket_far = swap(rel_bucket, far_swap)
    keys_far = swap(keys_side, core_swap)
    values_far = swap(values_side, core_swap)
    gathered = lax.all_to_all(copies, "page", 0, 0, axis_index_groups=groups, tiled=True)

    rank = page_rank.reshape(1)
    doc_rows = doc_of_token.reshape(-1, 2 * tok_dev)
    extra = call(
        columns_kernel, "columns", shape((group * tok_dev, 128), BF), [smem()] + [hbm()] * 2,
        [
            pltpu.VMEM((1, doc_query.shape[0]), jnp.int32),
            pltpu.VMEM(doc_rows.shape, jnp.int32),
            pltpu.SemaphoreType.DMA((2,)),
        ],
    )(rank, in_hbm(doc_query.reshape(1, -1)), in_hbm(doc_rows))
    key_count = 2 * local_pages * page_len

    def prepared(side, caches, buckets):
        return call(
            functools.partial(prepare_kernel, side=side),
            "prepare",
            [shape((local_heads, key_count, 128), BF), shape((local_width, key_count), BF)],
            [smem()] + [anywhere()] * 6 + [hbm()] * 3,
            [
                pltpu.VMEM((4, local_pages, page_len, local_width), BF),
                pltpu.VMEM((2, local_pages, page_len), jnp.int32),
                pltpu.VMEM(bias_table.T.shape, F32),
                pltpu.SMEM(page_table.shape, jnp.int32),
                pltpu.SMEM(query_lengths.shape, jnp.int32),
                pltpu.SMEM((2, 4 * local_pages + 1), jnp.int32),
                pltpu.SemaphoreType.DMA((9,)),
            ],
        )(rank, *caches, *buckets, in_hbm(bias_table.T), in_hbm(page_table), in_hbm(query_lengths))

    near = (in_hbm(cache_keys), keys_core, in_hbm(cache_values), values_core)
    keys_near, values_near = prepared(0, near, (in_hbm(rel_bucket), bucket_core))
    keys_away, values_away = prepared(1, (keys_side, keys_far, values_side, values_far), (bucket_side, bucket_far))
    partials = call(
        attention_kernel,
        "attention",
        shape((group, 136, 128), BF),
        [vmem()] * 6,
        [pltpu.VMEM((local_heads, group * tok_dev, 128), BF)],
    )(gathered, keys_near, keys_away, values_near, values_away, extra)
    returned = lax.all_to_all(partials, "page", 0, 0, axis_index_groups=groups, tiled=True)
    projected = call(
        combine_kernel, "combine", shape((tok_dev, model), BF), [vmem(), hbm()],
        [pltpu.VMEM((local_width, model), BF), pltpu.SemaphoreType.DMA(())],
    )(returned, in_hbm(out_weight))

    own = tok_dev // head_size
    terms = lax.all_to_all(projected.reshape(head_size, own, model), "head", 0, 0, tiled=True)
    own_states = lax.dynamic_slice_in_dim(doc_states, head_rank * own, own, 0)
    spread, hidden_score = call(
        norm_kernel,
        "norm",
        [shape((head_size, own, model), BF), shape((own, 128), F32)],
        [vmem()] * 4,
    )(terms, own_states, gain_ffn.reshape(1, model), score_vector.reshape(1, model))
    rows = lax.all_to_all(spread, "head", 0, 0, tiled=True).reshape(tok_dev, model)
    down_score = jnp.sum(wo_ffn.astype(F32) * score_vector, axis=-1)
    token = jnp.arange(tok_dev, dtype=jnp.int32)[:, None]
    own_score = jnp.where(token // own == head_rank, jnp.tile(hidden_score[:, :1], (head_size, 1)), 0.0)
    own_docs = lax.dynamic_slice_in_dim(doc_of_token, page_rank * tok_dev, tok_dev, 0)[:, None]
    doc_dev = doc_query.shape[0] // page_size
    steps = 4
    weight_slices = pltpu.VMEM((steps, model // steps, wi_gate.shape[1]), BF)
    doc_sums = call(
        feed_kernel, "feed", shape((page_size, 128), F32), [vmem(), hbm(), hbm(), vmem(), vmem(), vmem()],
        [weight_slices, weight_slices, pltpu.SemaphoreType.DMA((2 * steps,))],
    )(rows, in_hbm(wi_gate), in_hbm(wi_up), down_score.reshape(1, -1), own_score, own_docs)
    doc_sums = doc_sums.reshape(page_size, 1, 128)
    arrived = lax.all_to_all(doc_sums, "page", 0, 0, tiled=True)
    pooled = call(fold_kernel, "fold", shape((head_size, 1, 128), F32), [vmem()])(arrived)
    pooled = jnp.sum(lax.all_to_all(pooled, "head", 0, 0, tiled=True), axis=(0, 1))[:doc_dev]
    mine_docs = page_rank * doc_dev + jnp.arange(doc_dev, dtype=jnp.int32)
    counts = jnp.sum((doc_of_token[:, None] == mine_docs[None, :]).astype(F32), axis=0)
    return pooled / counts


def solution(mesh):
    return jax.shard_map(
        per_device,
        mesh=mesh,
        in_specs=(
            P("page", None),
            P(),
            P(None, "head"),
            P("page", None, "head"),
            P("page", None, "head"),
            P("page", None),
            P(None, "head"),
            P("head", None),
            P(),
            P(None, "head"),
            P(None, "head"),
            P("head", None),
            P(),
            P(),
            P(),
            P(),
            P(),
        ),
        out_specs=P("page"),
        check_vma=False,
    )
```

```python
import functools

import jax
import jax.numpy as jnp
from jax import lax
from jax.experimental import pallas as pl
from jax.experimental.pallas import tpu as pltpu
from jax.sharding import PartitionSpec as P

NQ = 8
DOCS = 256
MASKED = -1e30
BF = jnp.bfloat16
F32 = jnp.float32


def rms_scale(values, gain):
    values = values.astype(F32)
    return values * lax.rsqrt(jnp.mean(values * values, axis=-1, keepdims=True) + 1e-06) * gain


def split_three(value):
    first = value.astype(BF)
    rest = value - first.astype(F32)
    second = rest.astype(BF)
    third = (rest - second.astype(F32)).astype(BF)
    return first, second, third


def project_kernel(states, gain, weight, keys, buckets, out, payload, states_here, gain_here, weight_here, buckets_here,
                   arrivals):
    count = keys.shape[0]
    pairs = (
        (states, states_here),
        (gain, gain_here),
        (weight, weight_here),
        (buckets, buckets_here),
        (keys, payload.at[pl.ds(0, count)]),
    )
    copies = [pltpu.make_async_copy(there, here, arrivals.at[i]) for i, (there, here) in enumerate(pairs)]
    for copy in copies:
        copy.start()
    copies[0].wait()
    copies[1].wait()
    normed = rms_scale(states_here[...], gain_here[...]).astype(BF)
    copies[3].wait()
    both = jnp.concatenate([buckets_here[0:1, :], buckets_here[1:2, :]], axis=1).astype(F32)
    payload[count : count + 8, :] = jnp.broadcast_to(both, (8, both.shape[1])).astype(BF)
    copies[2].wait()
    queries = jnp.dot(normed, weight_here[...], preferred_element_type=F32).astype(BF)
    for chip in range(out.shape[0]):
        out[chip] = queries
    copies[4].wait()


def columns_kernel(rank, doc_query, doc_rows, extra, query_here, rows_here, arrivals):
    copies = [
        pltpu.make_async_copy(doc_query, query_here, arrivals.at[0]),
        pltpu.make_async_copy(doc_rows, rows_here, arrivals.at[1]),
    ]
    for copy in copies:
        copy.start()
    tokens = extra.shape[0]
    tok_dev = doc_rows.shape[1] // 2
    row_chips = 4
    core = rank[0] % 2
    chip = rank[0] // 2
    pair = chip - chip % 2
    doc_count = doc_query.shape[1]
    left = lax.broadcasted_iota(jnp.int32, (1, 128), 1) < tok_dev
    doc_id = lax.broadcasted_iota(jnp.int32, (doc_count, 128), 0)
    for copy in copies:
        copy.wait()
    blocks = []
    for y in range(tokens // (2 * tok_dev)):
        two = rows_here[pl.ds(y * row_chips + pair % row_chips, 2), :]
        turned = pltpu.roll(two, tok_dev, 1)
        row = jnp.where(
            left,
            jnp.where(core == 0, two[0:1], turned[0:1]),
            jnp.where(core == 0, turned[1:2], two[1:2]),
        )
        blocks.append((doc_id == row).astype(F32).astype(BF))
    member = jnp.concatenate(blocks, axis=1)
    asked = jnp.broadcast_to(query_here[...].astype(F32), (128, doc_count)).astype(BF)
    tok_query = jnp.dot(asked, member, preferred_element_type=F32)
    mark = lax.broadcasted_iota(jnp.int32, (128, tokens), 0) % 64
    columns = jnp.where(
        mark < NQ,
        jnp.where(tok_query == mark.astype(F32), 0.0, MASKED),
        jnp.where(mark == NQ, MASKED, jnp.where(mark < NQ + 4, 1.0, 0.0)),
    )
    extra[...] = columns.T.astype(BF)


def prepare_kernel(rank, k0, k1, v0, v1, bias_table, page_table, query_lengths, keys_aug, values_t, held, held_values,
                   table_here, slots_here, lengths_here, info, arrivals, *, side, pages):
    width, total = values_t.shape
    page_len = total // (2 * pages)
    keys = pages * page_len
    heads, bucket_count = bias_table.shape
    depth = width // heads
    slot_count = page_table.shape[0]
    max_pages = slot_count // NQ
    row_chips = 4
    pairs = [(page_table, slots_here), (query_lengths, lengths_here), (bias_table, table_here)]
    pairs += [(k0, held.at[0]), (k1, held.at[1]), (v0, held_values.at[0]), (v1, held_values.at[1])]
    copies = [pltpu.make_async_copy(there, here, arrivals.at[i]) for i, (there, here) in enumerate(pairs)]
    for copy in copies:
        copy.start()
    core = rank[0] % 2
    chip = rank[0] // 2
    base = (chip // row_chips * row_chips + chip % 2) * 2 * pages
    count = 4 * pages
    copies[0].wait()
    copies[1].wait()
    for s in range(slot_count):
        place = slots_here[s] - base
        near = (place >= 0) & (place < 2 * pages)
        far = (place >= 4 * pages) & (place < 6 * pages)
        place = jnp.where(near, place, jnp.where(far, place - 2 * pages, count))
        info[0, place] = s // max_pages
        info[1, place] = lengths_here[s // max_pages] - (s % max_pages) * page_len
    low = lax.broadcasted_iota(jnp.int32, (1, 128), 1) < depth
    col = lax.broadcasted_iota(jnp.int32, (bucket_count, 128), 1) % 64
    copies[2].wait()
    table = jnp.concatenate([table_here[...], jnp.zeros((8 - heads, bucket_count), F32)], axis=0).T
    spreads = []
    for h in range(heads):
        a, b, c = split_three(jnp.broadcast_to(table[:, h : h + 1], (bucket_count, 128)))
        third = jnp.where(col == NQ + 3, c.astype(F32), 0.0)
        spreads.append(
            jnp.where(col == NQ + 1, a.astype(F32), jnp.where(col == NQ + 2, b.astype(F32), third)).astype(BF)
        )
    spread = jnp.concatenate(spreads, axis=1)
    bucket_row = lax.broadcasted_iota(jnp.int32, (bucket_count, page_len), 0).astype(F32)
    slot = lax.broadcasted_iota(jnp.int32, (page_len, 128), 0)
    key_col = lax.broadcasted_iota(jnp.int32, (page_len, 128), 1) % 64
    mine = ((chip % row_chips // 2) * 2 + core) * pages
    for copy in copies[3:]:
        copy.wait()
    for part in range(2):
        for page in range(pages):
            place = (mine ^ ((2 * side + part) * pages)) + page
            span = pl.ds((part * pages + page) * page_len, page_len)
            bucket = held[part, keys : keys + 8, page * page_len : (page + 1) * page_len].astype(F32)[0:1]
            onehot = (jnp.broadcast_to(bucket, bucket_row.shape) == bucket_row).astype(F32).astype(BF)
            bias = lax.dot_general(onehot, spread, (((0,), (0,)), ((), ())), preferred_element_type=F32)
            holder = jnp.where(slot < info[1, place], info[0, place], NQ)
            marks = (key_col == holder).astype(F32)
            key = held[part, page * page_len : (page + 1) * page_len, :].astype(F32)
            for h in range(heads):
                keep = low if h % 2 == 0 else jnp.logical_not(low)
                half = key[:, (h // 2) * 128 : (h // 2 + 1) * 128]
                keys_aug[h, span, :] = jnp.where(keep, half, bias[:, h * 128 : (h + 1) * 128] + marks).astype(BF)
            value = held_values[part, page * page_len : (page + 1) * page_len, :]
            values_t[:, span] = value.astype(F32).T.astype(BF)


def attention_kernel(queries, keys_near, keys_far, values_near, values_far, extra, out, rows_aug):
    chips, tok_dev, width = queries.shape
    heads = keys_near.shape[0]
    depth = width // heads
    low = lax.broadcasted_iota(jnp.int32, (1, 128), 1) < depth
    left = lax.broadcasted_iota(jnp.int32, (1, 128), 1) < tok_dev
    rows = queries[...].reshape(chips * tok_dev, width)
    for h in range(heads):
        half = rows[:, (h // 2) * 128 : (h // 2 + 1) * 128].astype(F32)
        keep = low if h % 2 == 0 else jnp.logical_not(low)
        rows_aug[h] = jnp.where(keep, half, extra[...].astype(F32)).astype(BF)
    sums = []
    logs = []
    for h in range(heads):
        span = slice(h * depth, (h + 1) * depth)
        scores = [
            lax.dot_general(keys[h], rows_aug[h], (((1,), (1,)), ((), ())), preferred_element_type=F32)
            for keys in (keys_near, keys_far)
        ]
        top = jnp.maximum(
            jnp.max(scores[0], axis=0, keepdims=True), jnp.max(scores[1], axis=0, keepdims=True)
        )
        total = jnp.zeros_like(top)
        summed = jnp.zeros((depth, chips * tok_dev), F32)
        for part, values in zip(scores, (values_near, values_far)):
            weights = jnp.exp(part - top)
            total += jnp.sum(weights, axis=0, keepdims=True)
            summed += jnp.dot(values[span, :], weights.astype(BF), preferred_element_type=F32)
        sums.append(summed / total)
        logs.append(top + jnp.log(total))
    for duo in range(chips // 2):
        lanes = slice(duo * 128, (duo + 1) * 128)
        pad = [jnp.zeros((6, 128), F32)]
        upper = jnp.concatenate([sums[0][:, lanes], sums[1][:, lanes]], axis=0)
        lower = jnp.concatenate([sums[2][:, lanes], sums[3][:, lanes]], axis=0)
        stat_upper = jnp.concatenate([logs[0][:, lanes], logs[1][:, lanes]] + pad, axis=0)
        stat_lower = jnp.concatenate([logs[2][:, lanes], logs[3][:, lanes]] + pad, axis=0)
        block = (
            jnp.where(left, upper, pltpu.roll(lower, tok_dev, 1)),
            jnp.where(left, pltpu.roll(upper, tok_dev, 1), lower),
        )
        stat = (
            jnp.where(left, stat_upper, pltpu.roll(stat_lower, tok_dev, 1)),
            jnp.where(left, pltpu.roll(stat_upper, tok_dev, 1), stat_lower),
        )
        for which in range(2):
            a, b, c = split_three(stat[which])
            packed = [a[0:2].astype(F32), b[0:2].astype(F32), c[0:2].astype(F32), jnp.zeros((2, 128), F32)]
            out[duo * 2 + which, 0:128, :] = block[which].astype(BF)
            out[duo * 2 + which, 128:136, :] = jnp.concatenate(packed, axis=0).astype(BF)


def combine_kernel(parts, out_weight, out):
    chips = parts.shape[0]
    logs = []
    for chip in range(chips):
        stat = parts[chip, 128:136, :].astype(F32)
        logs.append(stat[0:2] + stat[2:4] + stat[4:6])
    top = logs[0]
    for chip in range(1, chips):
        top = jnp.maximum(top, logs[chip])
    scales = [jnp.exp(log - top) for log in logs]
    whole = scales[0]
    for chip in range(1, chips):
        whole = whole + scales[chip]
    sums = [jnp.zeros((64, 128), F32), jnp.zeros((64, 128), F32)]
    for chip in range(chips):
        share = scales[chip] / whole
        for r in range(2):
            sums[r] = sums[r] + share[r : r + 1] * parts[chip, r * 64 : (r + 1) * 64, :].astype(F32)
    joined = jnp.concatenate(sums, axis=0).T
    context = jnp.concatenate([joined[0:64], joined[64:128]], axis=1).astype(BF)
    out[...] = jnp.dot(context, out_weight[...], preferred_element_type=F32).astype(BF)


def norm_kernel(terms, states, gain, score_vector, out, score):
    hidden = states[...].astype(F32)
    for source in range(terms.shape[0]):
        hidden = hidden + terms[source].astype(F32)
    normed = rms_scale(hidden, gain[...]).astype(BF)
    for target in range(out.shape[0]):
        out[target] = normed
    score[...] = jnp.broadcast_to(jnp.sum(hidden * score_vector[...], axis=-1, keepdims=True), score.shape)


def down_kernel(weight, score_vector, out_weight, out, fetched, weight_here, arrivals):
    copy = pltpu.make_async_copy(weight, weight_here, arrivals.at[0])
    fetch = pltpu.make_async_copy(out_weight, fetched, arrivals.at[1])
    fetch.start()
    copy.start()
    pieces = [piece.astype(F32) for piece in split_three(score_vector[...])]
    rows = jnp.concatenate(pieces + [jnp.zeros((5, score_vector.shape[1]), F32)], axis=0).astype(BF)
    copy.wait()
    terms = lax.dot_general(rows, weight_here[...], (((1,), (1,)), ((), ())), preferred_element_type=F32)
    out[...] = terms[0:1] + terms[1:2] + terms[2:3]
    fetch.wait()


def fetch_kernel(weight, out, arrival):
    copy = pltpu.make_async_copy(weight, out, arrival)
    copy.start()
    copy.wait()


def feed_kernel(rows, gate_weight, up_weight, down_score, own_score, own_docs, out, up_here, arrivals):
    steps = up_here.shape[0]
    size = rows.shape[1] // steps
    copies = [
        pltpu.make_async_copy(up_weight.at[pl.ds(i * size, size)], up_here.at[i], arrivals.at[i]) for i in range(steps)
    ]
    for copy in copies:
        copy.start()
    gate = jnp.dot(rows[...], gate_weight[...], preferred_element_type=F32)
    gate = jax.nn.gelu(gate, approximate=True)
    upper = jnp.zeros_like(gate)
    for i in range(steps):
        copies[i].wait()
        upper += jnp.dot(rows[:, i * size : (i + 1) * size], up_here[i], preferred_element_type=F32)
    middle = (gate * upper).astype(BF).astype(F32)
    tok_score = jnp.sum(middle * down_score[...], axis=-1, keepdims=True) + own_score[...]
    docs = own_docs[...]
    doc_dev = DOCS // out.shape[0]
    lane = lax.broadcasted_iota(jnp.int32, (docs.shape[0], 128), 1)
    holder = (docs // doc_dev == lane).astype(F32).astype(BF)
    placed = jnp.where(docs % doc_dev == lane, tok_score, 0.0)
    pieces = jnp.concatenate([piece.astype(F32) for piece in split_three(placed)], axis=1).astype(BF)
    sums = lax.dot_general(holder, pieces, (((0,), (0,)), ((), ())), preferred_element_type=F32)[0 : out.shape[0]]
    out[...] = sums[:, 0:128] + sums[:, 128:256] + sums[:, 256:384]


def fold_kernel(terms, out):
    out[...] = jnp.broadcast_to(jnp.sum(terms[...], axis=0, keepdims=True), out.shape)


def vmem():
    return pl.BlockSpec(memory_space=pltpu.VMEM)


def smem():
    return pl.BlockSpec(memory_space=pltpu.SMEM)


def in_hbm(value):
    return pltpu.with_memory_space_constraint(value, pltpu.HBM)


def hbm():
    return pl.BlockSpec(memory_space=pltpu.HBM)


def anywhere():
    return pl.BlockSpec(memory_space=pl.ANY)


def call(kernel, name, shapes, specs, scratch=()):
    single = not isinstance(shapes, (list, tuple))
    return pl.pallas_call(
        kernel,
        out_shape=shapes,
        in_specs=specs,
        out_specs=vmem() if single else [vmem()] * len(shapes),
        scratch_shapes=list(scratch),
        compiler_params=pltpu.CompilerParams(vmem_limit_bytes=40 << 20),
        name=name,
    )


def per_device(
    doc_states,
    gain_attn,
    query_weight,
    cache_keys,
    cache_values,
    rel_bucket,
    bias_table,
    out_weight,
    gain_ffn,
    wi_gate,
    wi_up,
    wo_ffn,
    score_vector,
    query_lengths,
    doc_query,
    doc_of_token,
    page_table,
):
    shape = jax.ShapeDtypeStruct
    tok_dev, model = doc_states.shape
    local_pages, page_len, local_width = cache_keys.shape
    local_heads = bias_table.shape[1]
    page_size = lax.axis_size("page")
    head_size = lax.axis_size("head")
    page_rank = lax.axis_index("page")
    head_rank = lax.axis_index("head")
    group = page_size // 4
    groups = [
        [y * 8 + (x + side) * 2 + core for y in range(4) for side in range(2)] for x in (0, 2) for core in range(2)
    ]
    core_swap = [(i, i ^ 1) for i in range(page_size)]
    side_swap = [(i, i ^ 4) for i in range(page_size)]

    def swap(value, pairs):
        return lax.ppermute(value, "page", pairs)

    keys_held = local_pages * page_len
    copies, payload = call(
        project_kernel,
        "project",
        [shape((group, tok_dev, local_width), BF), shape((keys_held + 8, local_width), BF)],
        [hbm()] * 5,
        [
            pltpu.VMEM((tok_dev, model), BF),
            pltpu.VMEM((1, model), F32),
            pltpu.VMEM((model, local_width), BF),
            pltpu.VMEM((local_pages, page_len), jnp.int32),
            pltpu.SemaphoreType.DMA((5,)),
        ],
    )(
        in_hbm(doc_states),
        in_hbm(gain_attn.reshape(1, model)),
        in_hbm(query_weight),
        in_hbm(cache_keys.reshape(keys_held, local_width)),
        in_hbm(rel_bucket),
    )
    values_own = cache_values.reshape(keys_held, local_width)
    values_sent, copies = lax.optimization_barrier((values_own, copies))
    payload_side = swap(payload, side_swap)
    values_side = swap(values_sent, side_swap)
    payload_core = swap(payload, core_swap)
    values_core = swap(values_own, core_swap)
    payload_far = swap(payload_side, core_swap)
    values_far = swap(values_side, core_swap)
    gathered = lax.all_to_all(copies, "page", 0, 0, axis_index_groups=groups, tiled=True)

    rank = page_rank.reshape(1)
    doc_rows = doc_of_token.reshape(-1, 2 * tok_dev)
    extra = call(
        columns_kernel, "columns", shape((group * tok_dev, 128), BF), [smem()] + [hbm()] * 2,
        [
            pltpu.VMEM((1, doc_query.shape[0]), jnp.int32),
            pltpu.VMEM(doc_rows.shape, jnp.int32),
            pltpu.SemaphoreType.DMA((2,)),
        ],
    )(rank, in_hbm(doc_query.reshape(1, -1)), in_hbm(doc_rows))
    key_count = 2 * local_pages * page_len

    def prepared(side, caches):
        return call(
            functools.partial(prepare_kernel, side=side, pages=local_pages),
            "prepare",
            [shape((local_heads, key_count, 128), BF), shape((local_width, key_count), BF)],
            [smem()] + [anywhere()] * 4 + [hbm()] * 3,
            [
                pltpu.VMEM((2,) + payload.shape, BF),
                pltpu.VMEM((2,) + values_own.shape, BF),
                pltpu.VMEM(bias_table.T.shape, F32),
                pltpu.SMEM(page_table.shape, jnp.int32),
                pltpu.SMEM(query_lengths.shape, jnp.int32),
                pltpu.SMEM((2, 4 * local_pages + 1), jnp.int32),
                pltpu.SemaphoreType.DMA((7,)),
            ],
        )(rank, *caches, in_hbm(bias_table.T), in_hbm(page_table), in_hbm(query_lengths))

    keys_near, values_near = prepared(0, (payload, payload_core, in_hbm(values_own), values_core))
    keys_away, values_away = prepared(1, (payload_side, payload_far, values_side, values_far))
    partials = call(
        attention_kernel,
        "attention",
        shape((group, 136, 128), BF),
        [vmem()] * 6,
        [pltpu.VMEM((local_heads, group * tok_dev, 128), BF)],
    )(gathered, keys_near, keys_away, values_near, values_away, extra)
    partials, down_weight, late_weight = lax.optimization_barrier((partials, wo_ffn, out_weight))
    hidden_units = wi_gate.shape[1]
    down_score, fetched = call(
        down_kernel,
        "down",
        [shape((1, hidden_units), F32), shape(out_weight.shape, BF)],
        [hbm(), vmem(), hbm()],
        [pltpu.VMEM(wo_ffn.shape, BF), pltpu.SemaphoreType.DMA((2,))],
    )(in_hbm(down_weight), score_vector.reshape(1, model), in_hbm(late_weight))
    returned = lax.all_to_all(partials, "page", 0, 0, axis_index_groups=groups, tiled=True)
    projected = call(combine_kernel, "combine", shape((tok_dev, model), BF), [vmem()] * 2)(returned, fetched)

    own = tok_dev // head_size
    terms = lax.all_to_all(projected.reshape(head_size, own, model), "head", 0, 0, tiled=True)
    own_states = lax.dynamic_slice_in_dim(doc_states, head_rank * own, own, 0)
    spread, hidden_score = call(
        norm_kernel,
        "norm",
        [shape((head_size, own, model), BF), shape((own, 128), F32)],
        [vmem()] * 4,
    )(terms, own_states, gain_ffn.reshape(1, model), score_vector.reshape(1, model))
    spread, late_gate = lax.optimization_barrier((spread, wi_gate))
    gate_here = call(
        fetch_kernel, "fetch", shape(wi_gate.shape, BF), [hbm()], [pltpu.SemaphoreType.DMA(())]
    )(in_hbm(late_gate))
    rows = lax.all_to_all(spread, "head", 0, 0, tiled=True).reshape(tok_dev, model)
    token = jnp.arange(tok_dev, dtype=jnp.int32)[:, None]
    own_score = jnp.where(token // own == head_rank, jnp.tile(hidden_score[:, :1], (head_size, 1)), 0.0)
    own_docs = lax.dynamic_slice_in_dim(doc_of_token, page_rank * tok_dev, tok_dev, 0)[:, None]
    doc_dev = doc_query.shape[0] // page_size
    steps = 4
    doc_sums = call(
        feed_kernel, "feed", shape((page_size, 128), F32), [vmem(), vmem(), hbm(), vmem(), vmem(), vmem()],
        [pltpu.VMEM((steps, model // steps, hidden_units), BF), pltpu.SemaphoreType.DMA((steps,))],
    )(rows, gate_here, in_hbm(wi_up), down_score, own_score, own_docs)
    doc_sums = doc_sums.reshape(page_size, 1, 128)
    arrived = lax.all_to_all(doc_sums, "page", 0, 0, tiled=True)
    pooled = call(fold_kernel, "fold", shape((head_size, 1, 128), F32), [vmem()])(arrived)
    pooled = jnp.sum(lax.all_to_all(pooled, "head", 0, 0, tiled=True), axis=(0, 1))[:doc_dev]
    mine_docs = page_rank * doc_dev + jnp.arange(doc_dev, dtype=jnp.int32)
    counts = jnp.sum((doc_of_token[:, None] == mine_docs[None, :]).astype(F32), axis=0)
    return pooled / counts


def solution(mesh):
    return jax.shard_map(
        per_device,
        mesh=mesh,
        in_specs=(
            P("page", None),
            P(),
            P(None, "head"),
            P("page", None, "head"),
            P("page", None, "head"),
            P("page", None),
            P(None, "head"),
            P("head", None),
            P(),
            P(None, "head"),
            P(None, "head"),
            P("head", None),
            P(),
            P(),
            P(),
            P(),
            P(),
        ),
        out_specs=P("page"),
        check_vma=False,
    )
```

```python
import functools

import jax
import jax.numpy as jnp
from jax import lax
from jax.experimental import pallas as pl
from jax.experimental.pallas import tpu as pltpu
from jax.sharding import PartitionSpec as P

NQ = 8
DOCS = 256
MASKED = -1e30
BF = jnp.bfloat16
F32 = jnp.float32


def rms_scale(values, gain):
    values = values.astype(F32)
    return values * lax.rsqrt(jnp.mean(values * values, axis=-1, keepdims=True) + 1e-06) * gain


def split_three(value):
    first = value.astype(BF)
    rest = value - first.astype(F32)
    second = rest.astype(BF)
    third = (rest - second.astype(F32)).astype(BF)
    return first, second, third


def project_kernel(states, gain, weight, keys, values, buckets, out, payload, states_here, gain_here, weight_here,
                   buckets_here, arrivals):
    count = keys.shape[0]
    pairs = (
        (states, states_here),
        (gain, gain_here),
        (weight, weight_here),
        (buckets, buckets_here),
        (keys, payload.at[pl.ds(0, count)]),
        (values, payload.at[pl.ds(count + 8, count)]),
    )
    copies = [pltpu.make_async_copy(there, here, arrivals.at[i]) for i, (there, here) in enumerate(pairs)]
    for copy in copies:
        copy.start()
    copies[0].wait()
    copies[1].wait()
    normed = rms_scale(states_here[...], gain_here[...]).astype(BF)
    copies[3].wait()
    both = jnp.concatenate([buckets_here[0:1, :], buckets_here[1:2, :]], axis=1).astype(F32)
    payload[count : count + 8, :] = jnp.broadcast_to(both, (8, both.shape[1])).astype(BF)
    copies[2].wait()
    queries = jnp.dot(normed, weight_here[...], preferred_element_type=F32).astype(BF)
    for chip in range(out.shape[0]):
        out[chip] = queries
    copies[4].wait()
    copies[5].wait()


def near_kernel(rank, first, second, third, bias_table, page_table, query_lengths, doc_query, doc_rows, keys_aug, values_t,
                extra, table_here, slots_here, lengths_here, info, arrivals, query_here, rows_here, doc_arrivals, *, pages):
    copies = [
        pltpu.make_async_copy(doc_query, query_here, doc_arrivals.at[0]),
        pltpu.make_async_copy(doc_rows, rows_here, doc_arrivals.at[1]),
    ]
    for copy in copies:
        copy.start()

    def columns():
        for copy in copies:
            copy.wait()
        query_columns(rank, query_here, rows_here, extra)

    prepare_kernel(
        rank, first, second, third, bias_table, page_table, query_lengths, keys_aug, values_t, table_here, slots_here,
        lengths_here, info, arrivals, side=0, pages=pages, meanwhile=columns,
    )


def query_columns(rank, doc_query, doc_rows, extra):
    tokens = extra.shape[0]
    tok_dev = doc_rows.shape[1] // 2
    row_chips = 4
    core = rank[0] % 2
    chip = rank[0] // 2
    pair = chip - chip % 2
    doc_count = doc_query.shape[1]
    left = lax.broadcasted_iota(jnp.int32, (1, 128), 1) < tok_dev
    doc_id = lax.broadcasted_iota(jnp.int32, (doc_count, 128), 0)
    blocks = []
    for y in range(tokens // (2 * tok_dev)):
        two = doc_rows[pl.ds(y * row_chips + pair % row_chips, 2), :]
        turned = pltpu.roll(two, tok_dev, 1)
        row = jnp.where(
            left,
            jnp.where(core == 0, two[0:1], turned[0:1]),
            jnp.where(core == 0, turned[1:2], two[1:2]),
        )
        blocks.append((doc_id == row).astype(F32).astype(BF))
    member = jnp.concatenate(blocks, axis=1)
    asked = jnp.broadcast_to(doc_query[...].astype(F32), (128, doc_count)).astype(BF)
    tok_query = jnp.dot(asked, member, preferred_element_type=F32)
    mark = lax.broadcasted_iota(jnp.int32, (128, tokens), 0) % 64
    columns = jnp.where(
        mark < NQ,
        jnp.where(tok_query == mark.astype(F32), 0.0, MASKED),
        jnp.where(mark == NQ, MASKED, jnp.where(mark < NQ + 4, 1.0, 0.0)),
    )
    extra[...] = columns.T.astype(BF)


def prepare_kernel(rank, first, second, third, bias_table, page_table, query_lengths, keys_aug, values_t, table_here,
                   slots_here, lengths_here, info, arrivals, *, side, pages, meanwhile=None):
    width, total = values_t.shape
    page_len = total // (2 * pages)
    keys = pages * page_len
    heads, bucket_count = bias_table.shape
    depth = width // heads
    slot_count = page_table.shape[0]
    max_pages = slot_count // NQ
    row_chips = 4
    pairs = [(page_table, slots_here), (query_lengths, lengths_here), (bias_table, table_here)]
    copies = [pltpu.make_async_copy(there, here, arrivals.at[i]) for i, (there, here) in enumerate(pairs)]
    for copy in copies:
        copy.start()
    if meanwhile is not None:
        meanwhile()
    core = rank[0] % 2
    chip = rank[0] // 2
    base = (chip // row_chips * row_chips + chip % 2) * 2 * pages
    count = 4 * pages
    copies[0].wait()
    copies[1].wait()
    for s in range(slot_count):
        place = slots_here[s] - base
        near = (place >= 0) & (place < 2 * pages)
        far = (place >= 4 * pages) & (place < 6 * pages)
        place = jnp.where(near, place, jnp.where(far, place - 2 * pages, count))
        info[0, place] = s // max_pages
        info[1, place] = lengths_here[s // max_pages] - (s % max_pages) * page_len
    low = lax.broadcasted_iota(jnp.int32, (1, 128), 1) < depth
    col = lax.broadcasted_iota(jnp.int32, (bucket_count, 128), 1) % 64
    copies[2].wait()
    table = jnp.concatenate([table_here[...], jnp.zeros((8 - heads, bucket_count), F32)], axis=0).T
    spreads = []
    for h in range(heads):
        a, b, c = split_three(jnp.broadcast_to(table[:, h : h + 1], (bucket_count, 128)))
        last = jnp.where(col == NQ + 3, c.astype(F32), 0.0)
        spreads.append(
            jnp.where(col == NQ + 1, a.astype(F32), jnp.where(col == NQ + 2, b.astype(F32), last)).astype(BF)
        )
    spread = jnp.concatenate(spreads, axis=1)
    bucket_row = lax.broadcasted_iota(jnp.int32, (bucket_count, page_len), 0).astype(F32)
    slot = lax.broadcasted_iota(jnp.int32, (page_len, 128), 0)
    key_col = lax.broadcasted_iota(jnp.int32, (page_len, 128), 1) % 64
    mine = ((chip % row_chips // 2) * 2 + core) * pages
    sources = ((first, first, keys + 8), (second, third, 0))
    for part, (key_rows, value_rows, offset) in enumerate(sources):
        for page in range(pages):
            place = (mine ^ ((2 * side + part) * pages)) + page
            span = pl.ds((part * pages + page) * page_len, page_len)
            bucket = key_rows[keys : keys + 8, page * page_len : (page + 1) * page_len].astype(F32)[0:1]
            onehot = (jnp.broadcast_to(bucket, bucket_row.shape) == bucket_row).astype(F32).astype(BF)
            bias = lax.dot_general(onehot, spread, (((0,), (0,)), ((), ())), preferred_element_type=F32)
            holder = jnp.where(slot < info[1, place], info[0, place], NQ)
            marks = (key_col == holder).astype(F32)
            key = key_rows[page * page_len : (page + 1) * page_len, :].astype(F32)
            for h in range(heads):
                keep = low if h % 2 == 0 else jnp.logical_not(low)
                half = key[:, (h // 2) * 128 : (h // 2 + 1) * 128]
                keys_aug[h, span, :] = jnp.where(keep, half, bias[:, h * 128 : (h + 1) * 128] + marks).astype(BF)
            value = value_rows[offset + page * page_len : offset + (page + 1) * page_len, :]
            values_t[:, span] = value.astype(F32).T.astype(BF)


def attention_kernel(queries, keys_near, keys_far, values_near, values_far, extra, out, rows_aug):
    chips, tok_dev, width = queries.shape
    heads = keys_near.shape[0]
    depth = width // heads
    low = lax.broadcasted_iota(jnp.int32, (1, 128), 1) < depth
    left = lax.broadcasted_iota(jnp.int32, (1, 128), 1) < tok_dev
    rows = queries[...].reshape(chips * tok_dev, width)
    for h in range(heads):
        half = rows[:, (h // 2) * 128 : (h // 2 + 1) * 128].astype(F32)
        keep = low if h % 2 == 0 else jnp.logical_not(low)
        rows_aug[h] = jnp.where(keep, half, extra[...].astype(F32)).astype(BF)
    sums = []
    logs = []

    def score(h):
        return [
            lax.dot_general(keys[h], rows_aug[h], (((1,), (1,)), ((), ())), preferred_element_type=F32)
            for keys in (keys_near, keys_far)
        ]

    ready = score(0)
    for h in range(heads):
        span = slice(h * depth, (h + 1) * depth)
        scores = ready
        if h + 1 < heads:
            ready = score(h + 1)
        top = jnp.maximum(
            jnp.max(scores[0], axis=0, keepdims=True), jnp.max(scores[1], axis=0, keepdims=True)
        )
        total = jnp.zeros_like(top)
        summed = jnp.zeros((depth, chips * tok_dev), F32)
        for part, values in zip(scores, (values_near, values_far)):
            weights = jnp.exp(part - top)
            total += jnp.sum(weights, axis=0, keepdims=True)
            summed += jnp.dot(values[span, :], weights.astype(BF), preferred_element_type=F32)
        sums.append(summed / total)
        logs.append(top + jnp.log(total))
    for duo in range(chips // 2):
        lanes = slice(duo * 128, (duo + 1) * 128)
        pad = [jnp.zeros((6, 128), F32)]
        upper = jnp.concatenate([sums[0][:, lanes], sums[1][:, lanes]], axis=0)
        lower = jnp.concatenate([sums[2][:, lanes], sums[3][:, lanes]], axis=0)
        stat_upper = jnp.concatenate([logs[0][:, lanes], logs[1][:, lanes]] + pad, axis=0)
        stat_lower = jnp.concatenate([logs[2][:, lanes], logs[3][:, lanes]] + pad, axis=0)
        block = (
            jnp.where(left, upper, pltpu.roll(lower, tok_dev, 1)),
            jnp.where(left, pltpu.roll(upper, tok_dev, 1), lower),
        )
        stat = (
            jnp.where(left, stat_upper, pltpu.roll(stat_lower, tok_dev, 1)),
            jnp.where(left, pltpu.roll(stat_upper, tok_dev, 1), stat_lower),
        )
        for which in range(2):
            a, b, c = split_three(stat[which])
            packed = [a[0:2].astype(F32), b[0:2].astype(F32), c[0:2].astype(F32), jnp.zeros((2, 128), F32)]
            out[duo * 2 + which, 0:128, :] = block[which].astype(BF)
            out[duo * 2 + which, 128:136, :] = jnp.concatenate(packed, axis=0).astype(BF)


def combine_kernel(parts, out_weight, out):
    chips = parts.shape[0]
    logs = []
    for chip in range(chips):
        stat = parts[chip, 128:136, :].astype(F32)
        logs.append(stat[0:2] + stat[2:4] + stat[4:6])
    top = logs[0]
    for chip in range(1, chips):
        top = jnp.maximum(top, logs[chip])
    scales = [jnp.exp(log - top) for log in logs]
    whole = scales[0]
    for chip in range(1, chips):
        whole = whole + scales[chip]
    sums = [jnp.zeros((64, 128), F32), jnp.zeros((64, 128), F32)]
    for chip in range(chips):
        share = scales[chip] / whole
        for r in range(2):
            sums[r] = sums[r] + share[r : r + 1] * parts[chip, r * 64 : (r + 1) * 64, :].astype(F32)
    joined = jnp.concatenate(sums, axis=0).T
    context = jnp.concatenate([joined[0:64], joined[64:128]], axis=1).astype(BF)
    out[...] = jnp.dot(context, out_weight[...], preferred_element_type=F32).astype(BF)


def norm_kernel(terms, states, gain, score_vector, out, score):
    hidden = states[...].astype(F32)
    for source in range(terms.shape[0]):
        hidden = hidden + terms[source].astype(F32)
    normed = rms_scale(hidden, gain[...]).astype(BF)
    for target in range(out.shape[0]):
        out[target] = normed
    score[...] = jnp.broadcast_to(jnp.sum(hidden * score_vector[...], axis=-1, keepdims=True), score.shape)


def down_kernel(weight, score_vector, out_weight, out, fetched, weight_here, arrivals):
    copy = pltpu.make_async_copy(weight, weight_here, arrivals.at[0])
    fetch = pltpu.make_async_copy(out_weight, fetched, arrivals.at[1])
    fetch.start()
    copy.start()
    pieces = [piece.astype(F32) for piece in split_three(score_vector[...])]
    rows = jnp.concatenate(pieces + [jnp.zeros((5, score_vector.shape[1]), F32)], axis=0).astype(BF)
    copy.wait()
    terms = lax.dot_general(rows, weight_here[...], (((1,), (1,)), ((), ())), preferred_element_type=F32)
    out[...] = terms[0:1] + terms[1:2] + terms[2:3]
    fetch.wait()


def fetch_kernel(weight, out, arrival):
    copy = pltpu.make_async_copy(weight, out, arrival)
    copy.start()
    copy.wait()


def feed_kernel(rows, gate_weight, up_weight, down_score, own_score, own_docs, out, up_here, arrivals):
    steps = up_here.shape[0]
    size = rows.shape[1] // steps
    copies = [
        pltpu.make_async_copy(up_weight.at[pl.ds(i * size, size)], up_here.at[i], arrivals.at[i]) for i in range(steps)
    ]
    for copy in copies:
        copy.start()
    docs = own_docs[...]
    doc_dev = DOCS // out.shape[0]
    lane = lax.broadcasted_iota(jnp.int32, (docs.shape[0], 128), 1)
    holder = (docs // doc_dev == lane).astype(F32).astype(BF)
    gate = jnp.dot(rows[...], gate_weight[...], preferred_element_type=F32)
    gate = jax.nn.gelu(gate, approximate=True)
    upper = jnp.zeros_like(gate)
    for i in range(steps):
        copies[i].wait()
        upper += jnp.dot(rows[:, i * size : (i + 1) * size], up_here[i], preferred_element_type=F32)
    middle = (gate * upper).astype(BF).astype(F32)
    tok_score = jnp.sum(middle * down_score[...], axis=-1, keepdims=True) + own_score[...]
    placed = jnp.where(docs % doc_dev == lane, tok_score, 0.0)
    pieces = jnp.concatenate([piece.astype(F32) for piece in split_three(placed)], axis=1).astype(BF)
    sums = lax.dot_general(holder, pieces, (((0,), (0,)), ((), ())), preferred_element_type=F32)[0 : out.shape[0]]
    out[...] = sums[:, 0:128] + sums[:, 128:256] + sums[:, 256:384]


def fold_kernel(terms, out):
    out[...] = jnp.broadcast_to(jnp.sum(terms[...], axis=0, keepdims=True), out.shape)


def vmem():
    return pl.BlockSpec(memory_space=pltpu.VMEM)


def smem():
    return pl.BlockSpec(memory_space=pltpu.SMEM)


def in_hbm(value):
    return pltpu.with_memory_space_constraint(value, pltpu.HBM)


def hbm():
    return pl.BlockSpec(memory_space=pltpu.HBM)


def anywhere():
    return pl.BlockSpec(memory_space=pl.ANY)


def call(kernel, name, shapes, specs, scratch=()):
    single = not isinstance(shapes, (list, tuple))
    return pl.pallas_call(
        kernel,
        out_shape=shapes,
        in_specs=specs,
        out_specs=vmem() if single else [vmem()] * len(shapes),
        scratch_shapes=list(scratch),
        compiler_params=pltpu.CompilerParams(vmem_limit_bytes=40 << 20),
        name=name,
    )


def per_device(
    doc_states,
    gain_attn,
    query_weight,
    cache_keys,
    cache_values,
    rel_bucket,
    bias_table,
    out_weight,
    gain_ffn,
    wi_gate,
    wi_up,
    wo_ffn,
    score_vector,
    query_lengths,
    doc_query,
    doc_of_token,
    page_table,
):
    shape = jax.ShapeDtypeStruct
    tok_dev, model = doc_states.shape
    local_pages, page_len, local_width = cache_keys.shape
    local_heads = bias_table.shape[1]
    page_size = lax.axis_size("page")
    head_size = lax.axis_size("head")
    page_rank = lax.axis_index("page")
    head_rank = lax.axis_index("head")
    group = page_size // 4
    groups = [
        [y * 8 + (x + side) * 2 + core for y in range(4) for side in range(2)] for x in (0, 2) for core in range(2)
    ]
    core_swap = [(i, i ^ 1) for i in range(page_size)]
    side_swap = [(i, i ^ 4) for i in range(page_size)]

    def swap(value, pairs):
        return lax.ppermute(value, "page", pairs)

    keys_held = local_pages * page_len
    copies, payload = call(
        project_kernel,
        "project",
        [shape((group, tok_dev, local_width), BF), shape((2 * keys_held + 8, local_width), BF)],
        [hbm()] * 6,
        [
            pltpu.VMEM((tok_dev, model), BF),
            pltpu.VMEM((1, model), F32),
            pltpu.VMEM((model, local_width), BF),
            pltpu.VMEM((local_pages, page_len), jnp.int32),
            pltpu.SemaphoreType.DMA((6,)),
        ],
    )(
        in_hbm(doc_states),
        in_hbm(gain_attn.reshape(1, model)),
        in_hbm(query_weight),
        in_hbm(cache_keys.reshape(keys_held, local_width)),
        in_hbm(cache_values.reshape(keys_held, local_width)),
        in_hbm(rel_bucket),
    )
    values_own = cache_values.reshape(keys_held, local_width)
    payload_side = swap(payload, side_swap)
    keys_core = swap(payload[0 : keys_held + 8], core_swap)
    values_core = swap(values_own, core_swap)
    keys_far = swap(payload_side[0 : keys_held + 8], core_swap)
    values_far = swap(payload_side[keys_held + 8 :], core_swap)
    gathered = lax.all_to_all(copies, "page", 0, 0, axis_index_groups=groups, tiled=True)

    rank = page_rank.reshape(1)
    doc_rows = doc_of_token.reshape(-1, 2 * tok_dev)
    key_count = 2 * local_pages * page_len

    shapes = [shape((local_heads, key_count, 128), BF), shape((local_width, key_count), BF)]
    scratch = [
        pltpu.VMEM(bias_table.T.shape, F32),
        pltpu.SMEM(page_table.shape, jnp.int32),
        pltpu.SMEM(query_lengths.shape, jnp.int32),
        pltpu.SMEM((2, 4 * local_pages + 1), jnp.int32),
        pltpu.SemaphoreType.DMA((3,)),
    ]
    tables = (in_hbm(bias_table.T), in_hbm(page_table), in_hbm(query_lengths))
    keys_near, values_near, extra = call(
        functools.partial(near_kernel, pages=local_pages),
        "near",
        shapes + [shape((group * tok_dev, 128), BF)],
        [smem()] + [vmem()] * 3 + [hbm()] * 5,
        scratch
        + [
            pltpu.VMEM((1, doc_query.shape[0]), jnp.int32),
            pltpu.VMEM(doc_rows.shape, jnp.int32),
            pltpu.SemaphoreType.DMA((2,)),
        ],
    )(rank, payload, keys_core, values_core, *tables, in_hbm(doc_query.reshape(1, -1)), in_hbm(doc_rows))
    keys_away, values_away = call(
        functools.partial(prepare_kernel, side=1, pages=local_pages),
        "away",
        shapes,
        [smem()] + [vmem()] * 3 + [hbm()] * 3,
        scratch,
    )(rank, payload_side, keys_far, values_far, *tables)
    partials = call(
        attention_kernel,
        "attention",
        shape((group, 136, 128), BF),
        [vmem()] * 6,
        [pltpu.VMEM((local_heads, group * tok_dev, 128), BF)],
    )(gathered, keys_near, keys_away, values_near, values_away, extra)
    partials, down_weight, late_weight = lax.optimization_barrier((partials, wo_ffn, out_weight))
    hidden_units = wi_gate.shape[1]
    down_score, fetched = call(
        down_kernel,
        "down",
        [shape((1, hidden_units), F32), shape(out_weight.shape, BF)],
        [hbm(), vmem(), hbm()],
        [pltpu.VMEM(wo_ffn.shape, BF), pltpu.SemaphoreType.DMA((2,))],
    )(in_hbm(down_weight), score_vector.reshape(1, model), in_hbm(late_weight))
    returned = lax.all_to_all(partials, "page", 0, 0, axis_index_groups=groups, tiled=True)
    projected = call(combine_kernel, "combine", shape((tok_dev, model), BF), [vmem()] * 2)(returned, fetched)

    own = tok_dev // head_size
    terms = lax.all_to_all(projected.reshape(head_size, own, model), "head", 0, 0, tiled=True)
    own_states = lax.dynamic_slice_in_dim(doc_states, head_rank * own, own, 0)
    spread, hidden_score = call(
        norm_kernel,
        "norm",
        [shape((head_size, own, model), BF), shape((own, 128), F32)],
        [vmem()] * 4,
    )(terms, own_states, gain_ffn.reshape(1, model), score_vector.reshape(1, model))
    spread, late_gate = lax.optimization_barrier((spread, wi_gate))
    gate_here = call(
        fetch_kernel, "fetch", shape(wi_gate.shape, BF), [hbm()], [pltpu.SemaphoreType.DMA(())]
    )(in_hbm(late_gate))
    rows = lax.all_to_all(spread, "head", 0, 0, tiled=True).reshape(tok_dev, model)
    token = jnp.arange(tok_dev, dtype=jnp.int32)[:, None]
    own_score = jnp.where(token // own == head_rank, jnp.tile(hidden_score[:, :1], (head_size, 1)), 0.0)
    own_docs = lax.dynamic_slice_in_dim(doc_of_token, page_rank * tok_dev, tok_dev, 0)[:, None]
    doc_dev = doc_query.shape[0] // page_size
    steps = 4
    doc_sums = call(
        feed_kernel, "feed", shape((page_size, 128), F32), [vmem(), vmem(), hbm(), vmem(), vmem(), vmem()],
        [pltpu.VMEM((steps, model // steps, hidden_units), BF), pltpu.SemaphoreType.DMA((steps,))],
    )(rows, gate_here, in_hbm(wi_up), down_score, own_score, own_docs)
    doc_sums = doc_sums.reshape(page_size, 1, 128)
    arrived = lax.all_to_all(doc_sums, "page", 0, 0, tiled=True)
    pooled = call(fold_kernel, "fold", shape((head_size, 1, 128), F32), [vmem()])(arrived)
    pooled = jnp.sum(lax.all_to_all(pooled, "head", 0, 0, tiled=True), axis=(0, 1))[:doc_dev]
    mine_docs = page_rank * doc_dev + jnp.arange(doc_dev, dtype=jnp.int32)
    counts = jnp.sum((doc_of_token[:, None] == mine_docs[None, :]).astype(F32), axis=0)
    return pooled / counts


def solution(mesh):
    return jax.shard_map(
        per_device,
        mesh=mesh,
        in_specs=(
            P("page", None),
            P(),
            P(None, "head"),
            P("page", None, "head"),
            P("page", None, "head"),
            P("page", None),
            P(None, "head"),
            P("head", None),
            P(),
            P(None, "head"),
            P(None, "head"),
            P("head", None),
            P(),
            P(),
            P(),
            P(),
            P(),
        ),
        out_specs=P("page"),
        check_vma=False,
    )
```

```python
import functools

import jax
import jax.numpy as jnp
from jax import lax
from jax.experimental import pallas as pl
from jax.experimental.pallas import tpu as pltpu
from jax.sharding import PartitionSpec as P

NQ = 8
DOCS = 256
MASKED = -1e30
BF = jnp.bfloat16
F32 = jnp.float32


def rms_scale(values, gain):
    values = values.astype(F32)
    return values * lax.rsqrt(jnp.mean(values * values, axis=-1, keepdims=True) + 1e-06) * gain


def split_three(value):
    first = value.astype(BF)
    rest = value - first.astype(F32)
    second = rest.astype(BF)
    third = (rest - second.astype(F32)).astype(BF)
    return first, second, third


def project_kernel(states, gain, weight, keys, buckets, out, payload, states_here, gain_here, weight_here, buckets_here,
                   arrivals):
    count = keys.shape[0]
    steps = weight_here.shape[0]
    size = weight.shape[0] // steps
    pairs = [(states, states_here), (gain, gain_here)]
    pairs += [(weight.at[pl.ds(i * size, size)], weight_here.at[i]) for i in range(steps)]
    pairs += [(buckets, buckets_here), (keys, payload.at[pl.ds(0, count)])]
    copies = [pltpu.make_async_copy(there, here, arrivals.at[i]) for i, (there, here) in enumerate(pairs)]
    for copy in copies:
        copy.start()
    copies[0].wait()
    copies[1].wait()
    normed = rms_scale(states_here[...], gain_here[...]).astype(BF)
    queries = jnp.zeros((normed.shape[0], weight.shape[1]), F32)
    for i in range(steps):
        copies[2 + i].wait()
        queries += jnp.dot(normed[:, i * size : (i + 1) * size], weight_here[i], preferred_element_type=F32)
    queries = queries.astype(BF)
    for chip in range(out.shape[0]):
        out[chip] = queries
    copies[2 + steps].wait()
    both = jnp.concatenate([buckets_here[0:1, :], buckets_here[1:2, :]], axis=1).astype(F32)
    payload[count : count + 8, :] = jnp.broadcast_to(both, (8, both.shape[1])).astype(BF)
    copies[3 + steps].wait()


def near_kernel(rank, k0, k1, v0, v1, bias_table, page_table, query_lengths, doc_query, doc_rows, keys_aug, values_t,
                extra, table_here, slots_here, lengths_here, info, arrivals, query_here, rows_here, values_here,
                doc_arrivals, *, pages):
    copies = [
        pltpu.make_async_copy(doc_query, query_here, doc_arrivals.at[0]),
        pltpu.make_async_copy(doc_rows, rows_here, doc_arrivals.at[1]),
        pltpu.make_async_copy(v0, values_here, doc_arrivals.at[2]),
    ]
    for copy in copies:
        copy.start()

    def columns():
        copies[0].wait()
        copies[1].wait()
        query_columns(rank, query_here, rows_here, extra)
        copies[2].wait()

    prepare_kernel(
        rank, k0, k1, values_here, v1, bias_table, page_table, query_lengths, keys_aug, values_t, table_here, slots_here,
        lengths_here, info, arrivals, side=0, pages=pages, meanwhile=columns,
    )


def query_columns(rank, doc_query, doc_rows, extra):
    tokens = extra.shape[0]
    tok_dev = doc_rows.shape[1] // 2
    row_chips = 4
    core = rank[0] % 2
    chip = rank[0] // 2
    pair = chip - chip % 2
    doc_count = doc_query.shape[1]
    left = lax.broadcasted_iota(jnp.int32, (1, 128), 1) < tok_dev
    doc_id = lax.broadcasted_iota(jnp.int32, (doc_count, 128), 0)
    blocks = []
    for y in range(tokens // (2 * tok_dev)):
        two = doc_rows[pl.ds(y * row_chips + pair % row_chips, 2), :]
        turned = pltpu.roll(two, tok_dev, 1)
        row = jnp.where(
            left,
            jnp.where(core == 0, two[0:1], turned[0:1]),
            jnp.where(core == 0, turned[1:2], two[1:2]),
        )
        blocks.append((doc_id == row).astype(F32).astype(BF))
    member = jnp.concatenate(blocks, axis=1)
    asked = jnp.broadcast_to(doc_query[...].astype(F32), (128, doc_count)).astype(BF)
    tok_query = jnp.dot(asked, member, preferred_element_type=F32)
    mark = lax.broadcasted_iota(jnp.int32, (128, tokens), 0) % 64
    columns = jnp.where(
        mark < NQ,
        jnp.where(tok_query == mark.astype(F32), 0.0, MASKED),
        jnp.where(mark == NQ, MASKED, jnp.where(mark < NQ + 4, 1.0, 0.0)),
    )
    extra[...] = columns.T.astype(BF)


def prepare_kernel(rank, k0, k1, v0, v1, bias_table, page_table, query_lengths, keys_aug, values_t, table_here,
                   slots_here, lengths_here, info, arrivals, *, side, pages, meanwhile=None):
    width, total = values_t.shape
    page_len = total // (2 * pages)
    keys = pages * page_len
    heads, bucket_count = bias_table.shape
    depth = width // heads
    slot_count = page_table.shape[0]
    max_pages = slot_count // NQ
    row_chips = 4
    pairs = [(page_table, slots_here), (query_lengths, lengths_here), (bias_table, table_here)]
    copies = [pltpu.make_async_copy(there, here, arrivals.at[i]) for i, (there, here) in enumerate(pairs)]
    for copy in copies:
        copy.start()
    if meanwhile is not None:
        meanwhile()
    core = rank[0] % 2
    chip = rank[0] // 2
    base = (chip // row_chips * row_chips + chip % 2) * 2 * pages
    count = 4 * pages
    copies[0].wait()
    copies[1].wait()
    for s in range(slot_count):
        place = slots_here[s] - base
        near = (place >= 0) & (place < 2 * pages)
        far = (place >= 4 * pages) & (place < 6 * pages)
        place = jnp.where(near, place, jnp.where(far, place - 2 * pages, count))
        info[0, place] = s // max_pages
        info[1, place] = lengths_here[s // max_pages] - (s % max_pages) * page_len
    low = lax.broadcasted_iota(jnp.int32, (1, 128), 1) < depth
    col = lax.broadcasted_iota(jnp.int32, (bucket_count, 128), 1) % 64
    copies[2].wait()
    table = jnp.concatenate([table_here[...], jnp.zeros((8 - heads, bucket_count), F32)], axis=0).T
    spreads = []
    for h in range(heads):
        a, b, c = split_three(jnp.broadcast_to(table[:, h : h + 1], (bucket_count, 128)))
        last = jnp.where(col == NQ + 3, c.astype(F32), 0.0)
        spreads.append(
            jnp.where(col == NQ + 1, a.astype(F32), jnp.where(col == NQ + 2, b.astype(F32), last)).astype(BF)
        )
    spread = jnp.concatenate(spreads, axis=1)
    bucket_row = lax.broadcasted_iota(jnp.int32, (bucket_count, page_len), 0).astype(F32)
    slot = lax.broadcasted_iota(jnp.int32, (page_len, 128), 0)
    key_col = lax.broadcasted_iota(jnp.int32, (page_len, 128), 1) % 64
    mine = ((chip % row_chips // 2) * 2 + core) * pages
    for part, (key_rows, value_rows) in enumerate(((k0, v0), (k1, v1))):
        for page in range(pages):
            place = (mine ^ ((2 * side + part) * pages)) + page
            span = pl.ds((part * pages + page) * page_len, page_len)
            bucket = key_rows[keys : keys + 8, page * page_len : (page + 1) * page_len].astype(F32)[0:1]
            onehot = (jnp.broadcast_to(bucket, bucket_row.shape) == bucket_row).astype(F32).astype(BF)
            bias = lax.dot_general(onehot, spread, (((0,), (0,)), ((), ())), preferred_element_type=F32)
            holder = jnp.where(slot < info[1, place], info[0, place], NQ)
            marks = (key_col == holder).astype(F32)
            key = key_rows[page * page_len : (page + 1) * page_len, :].astype(F32)
            for h in range(heads):
                keep = low if h % 2 == 0 else jnp.logical_not(low)
                half = key[:, (h // 2) * 128 : (h // 2 + 1) * 128]
                keys_aug[h, span, :] = jnp.where(keep, half, bias[:, h * 128 : (h + 1) * 128] + marks).astype(BF)
            value = value_rows[page * page_len : (page + 1) * page_len, :]
            values_t[:, span] = value.astype(F32).T.astype(BF)


def attention_kernel(queries, keys_near, keys_far, values_near, values_far, extra, out, rows_aug):
    chips, tok_dev, width = queries.shape
    heads = keys_near.shape[0]
    depth = width // heads
    low = lax.broadcasted_iota(jnp.int32, (1, 128), 1) < depth
    left = lax.broadcasted_iota(jnp.int32, (1, 128), 1) < tok_dev
    rows = queries[...].reshape(chips * tok_dev, width)
    for h in range(heads):
        half = rows[:, (h // 2) * 128 : (h // 2 + 1) * 128].astype(F32)
        keep = low if h % 2 == 0 else jnp.logical_not(low)
        rows_aug[h] = jnp.where(keep, half, extra[...].astype(F32)).astype(BF)
    sums = []
    logs = []

    def score(h):
        return [
            lax.dot_general(keys[h], rows_aug[h], (((1,), (1,)), ((), ())), preferred_element_type=F32)
            for keys in (keys_near, keys_far)
        ]

    ready = score(0)
    for h in range(heads):
        span = slice(h * depth, (h + 1) * depth)
        scores = ready
        if h + 1 < heads:
            ready = score(h + 1)
        top = jnp.maximum(
            jnp.max(scores[0], axis=0, keepdims=True), jnp.max(scores[1], axis=0, keepdims=True)
        )
        total = jnp.zeros_like(top)
        summed = jnp.zeros((depth, chips * tok_dev), F32)
        for part, values in zip(scores, (values_near, values_far)):
            weights = jnp.exp(part - top)
            total += jnp.sum(weights, axis=0, keepdims=True)
            summed += jnp.dot(values[span, :], weights.astype(BF), preferred_element_type=F32)
        sums.append(summed / total)
        logs.append(top + jnp.log(total))
    for duo in range(chips // 2):
        lanes = slice(duo * 128, (duo + 1) * 128)
        pad = [jnp.zeros((6, 128), F32)]
        upper = jnp.concatenate([sums[0][:, lanes], sums[1][:, lanes]], axis=0)
        lower = jnp.concatenate([sums[2][:, lanes], sums[3][:, lanes]], axis=0)
        stat_upper = jnp.concatenate([logs[0][:, lanes], logs[1][:, lanes]] + pad, axis=0)
        stat_lower = jnp.concatenate([logs[2][:, lanes], logs[3][:, lanes]] + pad, axis=0)
        block = (
            jnp.where(left, upper, pltpu.roll(lower, tok_dev, 1)),
            jnp.where(left, pltpu.roll(upper, tok_dev, 1), lower),
        )
        stat = (
            jnp.where(left, stat_upper, pltpu.roll(stat_lower, tok_dev, 1)),
            jnp.where(left, pltpu.roll(stat_upper, tok_dev, 1), stat_lower),
        )
        for which in range(2):
            a, b, c = split_three(stat[which])
            packed = [a[0:2].astype(F32), b[0:2].astype(F32), c[0:2].astype(F32), jnp.zeros((2, 128), F32)]
            out[duo * 2 + which, 0:128, :] = block[which].astype(BF)
            out[duo * 2 + which, 128:136, :] = jnp.concatenate(packed, axis=0).astype(BF)


def combine_kernel(parts, out_weight, out):
    chips = parts.shape[0]
    logs = []
    for chip in range(chips):
        stat = parts[chip, 128:136, :].astype(F32)
        logs.append(stat[0:2] + stat[2:4] + stat[4:6])
    top = logs[0]
    for chip in range(1, chips):
        top = jnp.maximum(top, logs[chip])
    scales = [jnp.exp(log - top) for log in logs]
    whole = scales[0]
    for chip in range(1, chips):
        whole = whole + scales[chip]
    sums = [jnp.zeros((64, 128), F32), jnp.zeros((64, 128), F32)]
    for chip in range(chips):
        share = scales[chip] / whole
        for r in range(2):
            sums[r] = sums[r] + share[r : r + 1] * parts[chip, r * 64 : (r + 1) * 64, :].astype(F32)
    joined = jnp.concatenate(sums, axis=0).T
    context = jnp.concatenate([joined[0:64], joined[64:128]], axis=1).astype(BF)
    out[...] = jnp.dot(context, out_weight[...], preferred_element_type=F32).astype(BF)


def norm_kernel(terms, states, gain, score_vector, out, score):
    hidden = states[...].astype(F32)
    for source in range(terms.shape[0]):
        hidden = hidden + terms[source].astype(F32)
    normed = rms_scale(hidden, gain[...]).astype(BF)
    for target in range(out.shape[0]):
        out[target] = normed
    score[...] = jnp.broadcast_to(jnp.sum(hidden * score_vector[...], axis=-1, keepdims=True), score.shape)


def down_kernel(weight, score_vector, out_weight, out, fetched, weight_here, arrivals):
    copy = pltpu.make_async_copy(weight, weight_here, arrivals.at[0])
    fetch = pltpu.make_async_copy(out_weight, fetched, arrivals.at[1])
    fetch.start()
    copy.start()
    pieces = [piece.astype(F32) for piece in split_three(score_vector[...])]
    rows = jnp.concatenate(pieces + [jnp.zeros((5, score_vector.shape[1]), F32)], axis=0).astype(BF)
    copy.wait()
    terms = lax.dot_general(rows, weight_here[...], (((1,), (1,)), ((), ())), preferred_element_type=F32)
    out[...] = terms[0:1] + terms[1:2] + terms[2:3]
    fetch.wait()


def fetch_kernel(weight, out, arrival):
    copy = pltpu.make_async_copy(weight, out, arrival)
    copy.start()
    copy.wait()


def feed_kernel(rows, gate_weight, up_weight, down_score, own_score, own_docs, out, up_here, arrivals):
    steps = up_here.shape[0]
    size = rows.shape[1] // steps
    copies = [
        pltpu.make_async_copy(up_weight.at[pl.ds(i * size, size)], up_here.at[i], arrivals.at[i]) for i in range(steps)
    ]
    for copy in copies:
        copy.start()
    docs = own_docs[...]
    doc_dev = DOCS // out.shape[0]
    lane = lax.broadcasted_iota(jnp.int32, (docs.shape[0], 128), 1)
    holder = (docs // doc_dev == lane).astype(F32).astype(BF)
    gate = jnp.dot(rows[...], gate_weight[...], preferred_element_type=F32)
    gate = jax.nn.gelu(gate, approximate=True)
    upper = jnp.zeros_like(gate)
    for i in range(steps):
        copies[i].wait()
        upper += jnp.dot(rows[:, i * size : (i + 1) * size], up_here[i], preferred_element_type=F32)
    middle = (gate * upper).astype(BF).astype(F32)
    tok_score = jnp.sum(middle * down_score[...], axis=-1, keepdims=True) + own_score[...]
    placed = jnp.where(docs % doc_dev == lane, tok_score, 0.0)
    pieces = jnp.concatenate([piece.astype(F32) for piece in split_three(placed)], axis=1).astype(BF)
    sums = lax.dot_general(holder, pieces, (((0,), (0,)), ((), ())), preferred_element_type=F32)[0 : out.shape[0]]
    out[...] = sums[:, 0:128] + sums[:, 128:256] + sums[:, 256:384]


def fold_kernel(terms, out):
    out[...] = jnp.broadcast_to(jnp.sum(terms[...], axis=0, keepdims=True), out.shape)


def vmem():
    return pl.BlockSpec(memory_space=pltpu.VMEM)


def smem():
    return pl.BlockSpec(memory_space=pltpu.SMEM)


def in_hbm(value):
    return pltpu.with_memory_space_constraint(value, pltpu.HBM)


def hbm():
    return pl.BlockSpec(memory_space=pltpu.HBM)


def anywhere():
    return pl.BlockSpec(memory_space=pl.ANY)


def call(kernel, name, shapes, specs, scratch=()):
    single = not isinstance(shapes, (list, tuple))
    return pl.pallas_call(
        kernel,
        out_shape=shapes,
        in_specs=specs,
        out_specs=vmem() if single else [vmem()] * len(shapes),
        scratch_shapes=list(scratch),
        compiler_params=pltpu.CompilerParams(vmem_limit_bytes=40 << 20),
        name=name,
    )


def per_device(
    doc_states,
    gain_attn,
    query_weight,
    cache_keys,
    cache_values,
    rel_bucket,
    bias_table,
    out_weight,
    gain_ffn,
    wi_gate,
    wi_up,
    wo_ffn,
    score_vector,
    query_lengths,
    doc_query,
    doc_of_token,
    page_table,
):
    shape = jax.ShapeDtypeStruct
    tok_dev, model = doc_states.shape
    local_pages, page_len, local_width = cache_keys.shape
    local_heads = bias_table.shape[1]
    page_size = lax.axis_size("page")
    head_size = lax.axis_size("head")
    page_rank = lax.axis_index("page")
    head_rank = lax.axis_index("head")
    group = page_size // 4
    groups = [
        [y * 8 + (x + side) * 2 + core for y in range(4) for side in range(2)] for x in (0, 2) for core in range(2)
    ]
    core_swap = [(i, i ^ 1) for i in range(page_size)]
    side_swap = [(i, i ^ 4) for i in range(page_size)]

    def swap(value, pairs):
        return lax.ppermute(value, "page", pairs)

    keys_held = local_pages * page_len
    steps = 4
    copies, payload = call(
        project_kernel,
        "project",
        [shape((group, tok_dev, local_width), BF), shape((keys_held + 8, local_width), BF)],
        [hbm()] * 5,
        [
            pltpu.VMEM((tok_dev, model), BF),
            pltpu.VMEM((1, model), F32),
            pltpu.VMEM((steps, model // steps, local_width), BF),
            pltpu.VMEM((local_pages, page_len), jnp.int32),
            pltpu.SemaphoreType.DMA((steps + 4,)),
        ],
    )(
        in_hbm(doc_states),
        in_hbm(gain_attn.reshape(1, model)),
        in_hbm(query_weight),
        in_hbm(cache_keys.reshape(keys_held, local_width)),
        in_hbm(rel_bucket),
    )
    values_own = cache_values.reshape(keys_held, local_width)
    values_sent, copies = lax.optimization_barrier((values_own, copies))
    payload_side = swap(payload, side_swap)
    values_side = swap(values_sent, side_swap)
    payload_core = swap(payload, core_swap)
    values_core = swap(values_own, core_swap)
    payload_far = swap(payload_side, core_swap)
    values_far = swap(values_side, core_swap)
    gathered = lax.all_to_all(copies, "page", 0, 0, axis_index_groups=groups, tiled=True)

    rank = page_rank.reshape(1)
    doc_rows = doc_of_token.reshape(-1, 2 * tok_dev)
    key_count = 2 * local_pages * page_len

    shapes = [shape((local_heads, key_count, 128), BF), shape((local_width, key_count), BF)]
    scratch = [
        pltpu.VMEM(bias_table.T.shape, F32),
        pltpu.SMEM(page_table.shape, jnp.int32),
        pltpu.SMEM(query_lengths.shape, jnp.int32),
        pltpu.SMEM((2, 4 * local_pages + 1), jnp.int32),
        pltpu.SemaphoreType.DMA((3,)),
    ]
    tables = (in_hbm(bias_table.T), in_hbm(page_table), in_hbm(query_lengths))
    keys_near, values_near, extra = call(
        functools.partial(near_kernel, pages=local_pages),
        "near",
        shapes + [shape((group * tok_dev, 128), BF)],
        [smem()] + [vmem()] * 2 + [hbm(), vmem()] + [hbm()] * 5,
        scratch
        + [
            pltpu.VMEM((1, doc_query.shape[0]), jnp.int32),
            pltpu.VMEM(doc_rows.shape, jnp.int32),
            pltpu.VMEM(values_own.shape, BF),
            pltpu.SemaphoreType.DMA((3,)),
        ],
    )(rank, payload, payload_core, in_hbm(values_own), values_core, *tables, in_hbm(doc_query.reshape(1, -1)), in_hbm(doc_rows))
    keys_away, values_away = call(
        functools.partial(prepare_kernel, side=1, pages=local_pages),
        "away",
        shapes,
        [smem()] + [vmem()] * 4 + [hbm()] * 3,
        scratch,
    )(rank, payload_side, payload_far, values_side, values_far, *tables)
    partials = call(
        attention_kernel,
        "attention",
        shape((group, 136, 128), BF),
        [vmem()] * 6,
        [pltpu.VMEM((local_heads, group * tok_dev, 128), BF)],
    )(gathered, keys_near, keys_away, values_near, values_away, extra)
    partials, down_weight, late_weight = lax.optimization_barrier((partials, wo_ffn, out_weight))
    hidden_units = wi_gate.shape[1]
    down_score, fetched = call(
        down_kernel,
        "down",
        [shape((1, hidden_units), F32), shape(out_weight.shape, BF)],
        [hbm(), vmem(), hbm()],
        [pltpu.VMEM(wo_ffn.shape, BF), pltpu.SemaphoreType.DMA((2,))],
    )(in_hbm(down_weight), score_vector.reshape(1, model), in_hbm(late_weight))
    returned = lax.all_to_all(partials, "page", 0, 0, axis_index_groups=groups, tiled=True)
    projected = call(combine_kernel, "combine", shape((tok_dev, model), BF), [vmem()] * 2)(returned, fetched)

    own = tok_dev // head_size
    terms = lax.all_to_all(projected.reshape(head_size, own, model), "head", 0, 0, tiled=True)
    own_states = lax.dynamic_slice_in_dim(doc_states, head_rank * own, own, 0)
    spread, hidden_score = call(
        norm_kernel,
        "norm",
        [shape((head_size, own, model), BF), shape((own, 128), F32)],
        [vmem()] * 4,
    )(terms, own_states, gain_ffn.reshape(1, model), score_vector.reshape(1, model))
    spread, late_gate = lax.optimization_barrier((spread, wi_gate))
    gate_here = call(
        fetch_kernel, "fetch", shape(wi_gate.shape, BF), [hbm()], [pltpu.SemaphoreType.DMA(())]
    )(in_hbm(late_gate))
    rows = lax.all_to_all(spread, "head", 0, 0, tiled=True).reshape(tok_dev, model)
    token = jnp.arange(tok_dev, dtype=jnp.int32)[:, None]
    own_score = jnp.where(token // own == head_rank, jnp.tile(hidden_score[:, :1], (head_size, 1)), 0.0)
    own_docs = lax.dynamic_slice_in_dim(doc_of_token, page_rank * tok_dev, tok_dev, 0)[:, None]
    doc_dev = doc_query.shape[0] // page_size
    steps = 8
    doc_sums = call(
        feed_kernel, "feed", shape((page_size, 128), F32), [vmem(), vmem(), hbm(), vmem(), vmem(), vmem()],
        [pltpu.VMEM((steps, model // steps, hidden_units), BF), pltpu.SemaphoreType.DMA((steps,))],
    )(rows, gate_here, in_hbm(wi_up), down_score, own_score, own_docs)
    doc_sums = doc_sums.reshape(page_size, 1, 128)
    arrived = lax.all_to_all(doc_sums, "page", 0, 0, tiled=True)
    pooled = call(fold_kernel, "fold", shape((head_size, 1, 128), F32), [vmem()])(arrived)
    pooled = jnp.sum(lax.all_to_all(pooled, "head", 0, 0, tiled=True), axis=(0, 1))[:doc_dev]
    mine_docs = page_rank * doc_dev + jnp.arange(doc_dev, dtype=jnp.int32)
    counts = jnp.sum((doc_of_token[:, None] == mine_docs[None, :]).astype(F32), axis=0)
    return pooled / counts


def solution(mesh):
    return jax.shard_map(
        per_device,
        mesh=mesh,
        in_specs=(
            P("page", None),
            P(),
            P(None, "head"),
            P("page", None, "head"),
            P("page", None, "head"),
            P("page", None),
            P(None, "head"),
            P("head", None),
            P(),
            P(None, "head"),
            P(None, "head"),
            P("head", None),
            P(),
            P(),
            P(),
            P(),
            P(),
        ),
        out_specs=P("page"),
        check_vma=False,
    )
```

```python
import functools

import jax
import jax.numpy as jnp
from jax import lax
from jax.experimental import pallas as pl
from jax.experimental.pallas import tpu as pltpu
from jax.sharding import PartitionSpec as P

NQ = 8
DOCS = 256
MASKED = -1e30
BF = jnp.bfloat16
F32 = jnp.float32


def rms_scale(values, gain):
    values = values.astype(F32)
    return values * lax.rsqrt(jnp.mean(values * values, axis=-1, keepdims=True) + 1e-06) * gain


def split_three(value):
    first = value.astype(BF)
    rest = value - first.astype(F32)
    second = rest.astype(BF)
    third = (rest - second.astype(F32)).astype(BF)
    return first, second, third


def project_kernel(states, gain, weight, keys, values, buckets, out, payload, states_here, gain_here, weight_here,
                   buckets_here, arrivals):
    count = keys.shape[0]
    pairs = (
        (states, states_here),
        (gain, gain_here),
        (weight, weight_here),
        (buckets, buckets_here),
        (keys, payload.at[pl.ds(0, count)]),
        (values, payload.at[pl.ds(count + 8, count)]),
    )
    copies = [pltpu.make_async_copy(there, here, arrivals.at[i]) for i, (there, here) in enumerate(pairs)]
    for copy in copies:
        copy.start()
    copies[0].wait()
    copies[1].wait()
    normed = rms_scale(states_here[...], gain_here[...]).astype(BF)
    copies[3].wait()
    both = jnp.concatenate([buckets_here[0:1, :], buckets_here[1:2, :]], axis=1).astype(F32)
    payload[count : count + 8, :] = jnp.broadcast_to(both, (8, both.shape[1])).astype(BF)
    copies[2].wait()
    queries = jnp.dot(normed, weight_here[...], preferred_element_type=F32).astype(BF)
    for chip in range(out.shape[0]):
        out[chip] = queries
    copies[4].wait()
    copies[5].wait()


def near_kernel(rank, first, second, bias_table, page_table, query_lengths, doc_query, doc_rows, keys_aug, values_t,
                extra, table_here, slots_here, lengths_here, info, arrivals, query_here, rows_here, doc_arrivals, *, pages):
    copies = [
        pltpu.make_async_copy(doc_query, query_here, doc_arrivals.at[0]),
        pltpu.make_async_copy(doc_rows, rows_here, doc_arrivals.at[1]),
    ]
    for copy in copies:
        copy.start()

    def columns():
        for copy in copies:
            copy.wait()
        query_columns(rank, query_here, rows_here, extra)

    prepare_kernel(
        rank, first, second, None, bias_table, page_table, query_lengths, keys_aug, values_t, table_here, slots_here,
        lengths_here, info, arrivals, side=0, pages=pages, meanwhile=columns,
    )


def query_columns(rank, doc_query, doc_rows, extra):
    tokens = extra.shape[0]
    tok_dev = doc_rows.shape[1] // 2
    row_chips = 4
    core = rank[0] % 2
    chip = rank[0] // 2
    pair = chip - chip % 2
    doc_count = doc_query.shape[1]
    left = lax.broadcasted_iota(jnp.int32, (1, 128), 1) < tok_dev
    doc_id = lax.broadcasted_iota(jnp.int32, (doc_count, 128), 0)
    blocks = []
    for y in range(tokens // (2 * tok_dev)):
        two = doc_rows[pl.ds(y * row_chips + pair % row_chips, 2), :]
        turned = pltpu.roll(two, tok_dev, 1)
        row = jnp.where(
            left,
            jnp.where(core == 0, two[0:1], turned[0:1]),
            jnp.where(core == 0, turned[1:2], two[1:2]),
        )
        blocks.append((doc_id == row).astype(F32).astype(BF))
    member = jnp.concatenate(blocks, axis=1)
    asked = jnp.broadcast_to(doc_query[...].astype(F32), (128, doc_count)).astype(BF)
    tok_query = jnp.dot(asked, member, preferred_element_type=F32)
    mark = lax.broadcasted_iota(jnp.int32, (128, tokens), 0) % 64
    columns = jnp.where(
        mark < NQ,
        jnp.where(tok_query == mark.astype(F32), 0.0, MASKED),
        jnp.where(mark == NQ, MASKED, jnp.where(mark < NQ + 4, 1.0, 0.0)),
    )
    extra[...] = columns.T.astype(BF)


def prepare_kernel(rank, first, second, third, bias_table, page_table, query_lengths, keys_aug, values_t, table_here,
                   slots_here, lengths_here, info, arrivals, *, side, pages, meanwhile=None):
    width, total = values_t.shape
    page_len = total // (2 * pages)
    keys = pages * page_len
    heads, bucket_count = bias_table.shape
    depth = width // heads
    slot_count = page_table.shape[0]
    max_pages = slot_count // NQ
    row_chips = 4
    pairs = [(page_table, slots_here), (query_lengths, lengths_here), (bias_table, table_here)]
    copies = [pltpu.make_async_copy(there, here, arrivals.at[i]) for i, (there, here) in enumerate(pairs)]
    for copy in copies:
        copy.start()
    sources = ((first, keys + 8), (second, keys + 8) if third is None else (third, 0))
    for part, (value_rows, offset) in enumerate(sources):
        for page in range(pages):
            value = value_rows[offset + page * page_len : offset + (page + 1) * page_len, :]
            values_t[:, pl.ds((part * pages + page) * page_len, page_len)] = value.astype(F32).T.astype(BF)
    if meanwhile is not None:
        meanwhile()
    core = rank[0] % 2
    chip = rank[0] // 2
    base = (chip // row_chips * row_chips + chip % 2) * 2 * pages
    count = 4 * pages
    copies[0].wait()
    copies[1].wait()
    for s in range(slot_count):
        place = slots_here[s] - base
        near = (place >= 0) & (place < 2 * pages)
        far = (place >= 4 * pages) & (place < 6 * pages)
        place = jnp.where(near, place, jnp.where(far, place - 2 * pages, count))
        info[0, place] = s // max_pages
        info[1, place] = lengths_here[s // max_pages] - (s % max_pages) * page_len
    low = lax.broadcasted_iota(jnp.int32, (1, 128), 1) < depth
    col = lax.broadcasted_iota(jnp.int32, (bucket_count, 128), 1) % 64
    copies[2].wait()
    table = jnp.concatenate([table_here[...], jnp.zeros((8 - heads, bucket_count), F32)], axis=0).T
    spreads = []
    for h in range(heads):
        a, b, c = split_three(jnp.broadcast_to(table[:, h : h + 1], (bucket_count, 128)))
        last = jnp.where(col == NQ + 3, c.astype(F32), 0.0)
        spreads.append(
            jnp.where(col == NQ + 1, a.astype(F32), jnp.where(col == NQ + 2, b.astype(F32), last)).astype(BF)
        )
    spread = jnp.concatenate(spreads, axis=1)
    bucket_row = lax.broadcasted_iota(jnp.int32, (bucket_count, page_len), 0).astype(F32)
    slot = lax.broadcasted_iota(jnp.int32, (page_len, 128), 0)
    key_col = lax.broadcasted_iota(jnp.int32, (page_len, 128), 1) % 64
    mine = ((chip % row_chips // 2) * 2 + core) * pages
    for part, key_rows in enumerate((first, second)):
        for page in range(pages):
            place = (mine ^ ((2 * side + part) * pages)) + page
            span = pl.ds((part * pages + page) * page_len, page_len)
            bucket = key_rows[keys : keys + 8, page * page_len : (page + 1) * page_len].astype(F32)[0:1]
            onehot = (jnp.broadcast_to(bucket, bucket_row.shape) == bucket_row).astype(F32).astype(BF)
            bias = lax.dot_general(onehot, spread, (((0,), (0,)), ((), ())), preferred_element_type=F32)
            holder = jnp.where(slot < info[1, place], info[0, place], NQ)
            marks = (key_col == holder).astype(F32)
            key = key_rows[page * page_len : (page + 1) * page_len, :].astype(F32)
            for h in range(heads):
                keep = low if h % 2 == 0 else jnp.logical_not(low)
                half = key[:, (h // 2) * 128 : (h // 2 + 1) * 128]
                keys_aug[h, span, :] = jnp.where(keep, half, bias[:, h * 128 : (h + 1) * 128] + marks).astype(BF)


def attention_kernel(queries, keys_near, keys_far, values_near, values_far, extra, out, rows_aug):
    chips, tok_dev, width = queries.shape
    heads = keys_near.shape[0]
    depth = width // heads
    low = lax.broadcasted_iota(jnp.int32, (1, 128), 1) < depth
    left = lax.broadcasted_iota(jnp.int32, (1, 128), 1) < tok_dev
    rows = queries[...].reshape(chips * tok_dev, width)
    for h in range(heads):
        half = rows[:, (h // 2) * 128 : (h // 2 + 1) * 128].astype(F32)
        keep = low if h % 2 == 0 else jnp.logical_not(low)
        rows_aug[h] = jnp.where(keep, half, extra[...].astype(F32)).astype(BF)
    sums = []
    logs = []

    def score(h):
        return [
            lax.dot_general(keys[h], rows_aug[h], (((1,), (1,)), ((), ())), preferred_element_type=F32)
            for keys in (keys_near, keys_far)
        ]

    ready = score(0)
    for h in range(heads):
        span = slice(h * depth, (h + 1) * depth)
        scores = ready
        if h + 1 < heads:
            ready = score(h + 1)
        top = jnp.maximum(
            jnp.max(scores[0], axis=0, keepdims=True), jnp.max(scores[1], axis=0, keepdims=True)
        )
        total = jnp.zeros_like(top)
        summed = jnp.zeros((depth, chips * tok_dev), F32)
        for part, values in zip(scores, (values_near, values_far)):
            weights = jnp.exp(part - top)
            total += jnp.sum(weights, axis=0, keepdims=True)
            summed += jnp.dot(values[span, :], weights.astype(BF), preferred_element_type=F32)
        sums.append(summed / total)
        logs.append(top + jnp.log(total))
    for duo in range(chips // 2):
        lanes = slice(duo * 128, (duo + 1) * 128)
        pad = [jnp.zeros((6, 128), F32)]
        upper = jnp.concatenate([sums[0][:, lanes], sums[1][:, lanes]], axis=0)
        lower = jnp.concatenate([sums[2][:, lanes], sums[3][:, lanes]], axis=0)
        stat_upper = jnp.concatenate([logs[0][:, lanes], logs[1][:, lanes]] + pad, axis=0)
        stat_lower = jnp.concatenate([logs[2][:, lanes], logs[3][:, lanes]] + pad, axis=0)
        block = (
            jnp.where(left, upper, pltpu.roll(lower, tok_dev, 1)),
            jnp.where(left, pltpu.roll(upper, tok_dev, 1), lower),
        )
        stat = (
            jnp.where(left, stat_upper, pltpu.roll(stat_lower, tok_dev, 1)),
            jnp.where(left, pltpu.roll(stat_upper, tok_dev, 1), stat_lower),
        )
        for which in range(2):
            a, b, c = split_three(stat[which])
            packed = [a[0:2].astype(F32), b[0:2].astype(F32), c[0:2].astype(F32), jnp.zeros((2, 128), F32)]
            out[duo * 2 + which, 0:128, :] = block[which].astype(BF)
            out[duo * 2 + which, 128:136, :] = jnp.concatenate(packed, axis=0).astype(BF)


def combine_kernel(parts, out_weight, out):
    chips = parts.shape[0]
    logs = []
    for chip in range(chips):
        stat = parts[chip, 128:136, :].astype(F32)
        logs.append(stat[0:2] + stat[2:4] + stat[4:6])
    top = logs[0]
    for chip in range(1, chips):
        top = jnp.maximum(top, logs[chip])
    scales = [jnp.exp(log - top) for log in logs]
    whole = scales[0]
    for chip in range(1, chips):
        whole = whole + scales[chip]
    sums = [jnp.zeros((64, 128), F32), jnp.zeros((64, 128), F32)]
    for chip in range(chips):
        share = scales[chip] / whole
        for r in range(2):
            sums[r] = sums[r] + share[r : r + 1] * parts[chip, r * 64 : (r + 1) * 64, :].astype(F32)
    joined = jnp.concatenate(sums, axis=0).T
    context = jnp.concatenate([joined[0:64], joined[64:128]], axis=1).astype(BF)
    out[...] = jnp.dot(context, out_weight[...], preferred_element_type=F32).astype(BF)


def norm_kernel(terms, states, gain, score_vector, out, score):
    hidden = states[...].astype(F32)
    for source in range(terms.shape[0]):
        hidden = hidden + terms[source].astype(F32)
    normed = rms_scale(hidden, gain[...]).astype(BF)
    for target in range(out.shape[0]):
        out[target] = normed
    score[...] = jnp.broadcast_to(jnp.sum(hidden * score_vector[...], axis=-1, keepdims=True), score.shape)


def down_kernel(weight, score_vector, out_weight, out, fetched, weight_here, arrivals):
    copy = pltpu.make_async_copy(weight, weight_here, arrivals.at[0])
    fetch = pltpu.make_async_copy(out_weight, fetched, arrivals.at[1])
    fetch.start()
    copy.start()
    pieces = [piece.astype(F32) for piece in split_three(score_vector[...])]
    rows = jnp.concatenate(pieces + [jnp.zeros((5, score_vector.shape[1]), F32)], axis=0).astype(BF)
    copy.wait()
    terms = lax.dot_general(rows, weight_here[...], (((1,), (1,)), ((), ())), preferred_element_type=F32)
    out[...] = terms[0:1] + terms[1:2] + terms[2:3]
    fetch.wait()


def fetch_kernel(weight, out, arrival):
    copy = pltpu.make_async_copy(weight, out, arrival)
    copy.start()
    copy.wait()


def feed_kernel(rows, gate_weight, up_weight, down_score, own_score, own_docs, out, up_here, arrivals):
    steps = up_here.shape[0]
    size = rows.shape[1] // steps
    copies = [
        pltpu.make_async_copy(up_weight.at[pl.ds(i * size, size)], up_here.at[i], arrivals.at[i]) for i in range(steps)
    ]
    for copy in copies:
        copy.start()
    docs = own_docs[...]
    doc_dev = DOCS // out.shape[0]
    lane = lax.broadcasted_iota(jnp.int32, (docs.shape[0], 128), 1)
    holder = (docs // doc_dev == lane).astype(F32).astype(BF)
    gate = jnp.dot(rows[...], gate_weight[...], preferred_element_type=F32)
    gate = jax.nn.gelu(gate, approximate=True)
    upper = jnp.zeros_like(gate)
    for i in range(steps):
        copies[i].wait()
        upper += jnp.dot(rows[:, i * size : (i + 1) * size], up_here[i], preferred_element_type=F32)
    middle = (gate * upper).astype(BF).astype(F32)
    tok_score = jnp.sum(middle * down_score[...], axis=-1, keepdims=True) + own_score[...]
    placed = jnp.where(docs % doc_dev == lane, tok_score, 0.0)
    pieces = jnp.concatenate([piece.astype(F32) for piece in split_three(placed)], axis=1).astype(BF)
    sums = lax.dot_general(holder, pieces, (((0,), (0,)), ((), ())), preferred_element_type=F32)[0 : out.shape[0]]
    out[...] = sums[:, 0:128] + sums[:, 128:256] + sums[:, 256:384]


def fold_kernel(terms, out):
    out[...] = jnp.broadcast_to(jnp.sum(terms[...], axis=0, keepdims=True), out.shape)


def vmem():
    return pl.BlockSpec(memory_space=pltpu.VMEM)


def smem():
    return pl.BlockSpec(memory_space=pltpu.SMEM)


def in_hbm(value):
    return pltpu.with_memory_space_constraint(value, pltpu.HBM)


def hbm():
    return pl.BlockSpec(memory_space=pltpu.HBM)


def anywhere():
    return pl.BlockSpec(memory_space=pl.ANY)


def call(kernel, name, shapes, specs, scratch=()):
    single = not isinstance(shapes, (list, tuple))
    return pl.pallas_call(
        kernel,
        out_shape=shapes,
        in_specs=specs,
        out_specs=vmem() if single else [vmem()] * len(shapes),
        scratch_shapes=list(scratch),
        compiler_params=pltpu.CompilerParams(vmem_limit_bytes=40 << 20),
        name=name,
    )


def per_device(
    doc_states,
    gain_attn,
    query_weight,
    cache_keys,
    cache_values,
    rel_bucket,
    bias_table,
    out_weight,
    gain_ffn,
    wi_gate,
    wi_up,
    wo_ffn,
    score_vector,
    query_lengths,
    doc_query,
    doc_of_token,
    page_table,
):
    shape = jax.ShapeDtypeStruct
    tok_dev, model = doc_states.shape
    local_pages, page_len, local_width = cache_keys.shape
    local_heads = bias_table.shape[1]
    page_size = lax.axis_size("page")
    head_size = lax.axis_size("head")
    page_rank = lax.axis_index("page")
    head_rank = lax.axis_index("head")
    group = page_size // 4
    groups = [
        [y * 8 + (x + side) * 2 + core for y in range(4) for side in range(2)] for x in (0, 2) for core in range(2)
    ]
    core_swap = [(i, i ^ 1) for i in range(page_size)]
    side_swap = [(i, i ^ 4) for i in range(page_size)]

    def swap(value, pairs):
        return lax.ppermute(value, "page", pairs)

    keys_held = local_pages * page_len
    copies, payload = call(
        project_kernel,
        "project",
        [shape((group, tok_dev, local_width), BF), shape((2 * keys_held + 8, local_width), BF)],
        [hbm()] * 6,
        [
            pltpu.VMEM((tok_dev, model), BF),
            pltpu.VMEM((1, model), F32),
            pltpu.VMEM((model, local_width), BF),
            pltpu.VMEM((local_pages, page_len), jnp.int32),
            pltpu.SemaphoreType.DMA((6,)),
        ],
    )(
        in_hbm(doc_states),
        in_hbm(gain_attn.reshape(1, model)),
        in_hbm(query_weight),
        in_hbm(cache_keys.reshape(keys_held, local_width)),
        in_hbm(cache_values.reshape(keys_held, local_width)),
        in_hbm(rel_bucket),
    )
    payload_side = swap(payload, side_swap)
    payload_core = swap(payload, core_swap)
    keys_far = swap(payload_side[0 : keys_held + 8], core_swap)
    values_far = swap(payload_side[keys_held + 8 :], core_swap)
    gathered = lax.all_to_all(copies, "page", 0, 0, axis_index_groups=groups, tiled=True)

    rank = page_rank.reshape(1)
    doc_rows = doc_of_token.reshape(-1, 2 * tok_dev)
    key_count = 2 * local_pages * page_len

    shapes = [shape((local_heads, key_count, 128), BF), shape((local_width, key_count), BF)]
    scratch = [
        pltpu.VMEM(bias_table.T.shape, F32),
        pltpu.SMEM(page_table.shape, jnp.int32),
        pltpu.SMEM(query_lengths.shape, jnp.int32),
        pltpu.SMEM((2, 4 * local_pages + 1), jnp.int32),
        pltpu.SemaphoreType.DMA((3,)),
    ]
    tables = (in_hbm(bias_table.T), in_hbm(page_table), in_hbm(query_lengths))
    keys_near, values_near, extra = call(
        functools.partial(near_kernel, pages=local_pages),
        "near",
        shapes + [shape((group * tok_dev, 128), BF)],
        [smem()] + [vmem()] * 2 + [hbm()] * 5,
        scratch
        + [
            pltpu.VMEM((1, doc_query.shape[0]), jnp.int32),
            pltpu.VMEM(doc_rows.shape, jnp.int32),
            pltpu.SemaphoreType.DMA((2,)),
        ],
    )(rank, payload, payload_core, *tables, in_hbm(doc_query.reshape(1, -1)), in_hbm(doc_rows))
    keys_away, values_away = call(
        functools.partial(prepare_kernel, side=1, pages=local_pages),
        "away",
        shapes,
        [smem()] + [vmem()] * 3 + [hbm()] * 3,
        scratch,
    )(rank, payload_side, keys_far, values_far, *tables)
    partials = call(
        attention_kernel,
        "attention",
        shape((group, 136, 128), BF),
        [vmem()] * 6,
        [pltpu.VMEM((local_heads, group * tok_dev, 128), BF)],
    )(gathered, keys_near, keys_away, values_near, values_away, extra)
    partials, down_weight, late_weight = lax.optimization_barrier((partials, wo_ffn, out_weight))
    hidden_units = wi_gate.shape[1]
    down_score, fetched = call(
        down_kernel,
        "down",
        [shape((1, hidden_units), F32), shape(out_weight.shape, BF)],
        [hbm(), vmem(), hbm()],
        [pltpu.VMEM(wo_ffn.shape, BF), pltpu.SemaphoreType.DMA((2,))],
    )(in_hbm(down_weight), score_vector.reshape(1, model), in_hbm(late_weight))
    returned = lax.all_to_all(partials, "page", 0, 0, axis_index_groups=groups, tiled=True)
    projected = call(combine_kernel, "combine", shape((tok_dev, model), BF), [vmem()] * 2)(returned, fetched)

    own = tok_dev // head_size
    terms = lax.all_to_all(projected.reshape(head_size, own, model), "head", 0, 0, tiled=True)
    own_states = lax.dynamic_slice_in_dim(doc_states, head_rank * own, own, 0)
    spread, hidden_score = call(
        norm_kernel,
        "norm",
        [shape((head_size, own, model), BF), shape((own, 128), F32)],
        [vmem()] * 4,
    )(terms, own_states, gain_ffn.reshape(1, model), score_vector.reshape(1, model))
    spread, late_gate = lax.optimization_barrier((spread, wi_gate))
    gate_here = call(
        fetch_kernel, "fetch", shape(wi_gate.shape, BF), [hbm()], [pltpu.SemaphoreType.DMA(())]
    )(in_hbm(late_gate))
    rows = lax.all_to_all(spread, "head", 0, 0, tiled=True).reshape(tok_dev, model)
    token = jnp.arange(tok_dev, dtype=jnp.int32)[:, None]
    own_score = jnp.where(token // own == head_rank, jnp.tile(hidden_score[:, :1], (head_size, 1)), 0.0)
    own_docs = lax.dynamic_slice_in_dim(doc_of_token, page_rank * tok_dev, tok_dev, 0)[:, None]
    doc_dev = doc_query.shape[0] // page_size
    steps = 4
    doc_sums = call(
        feed_kernel, "feed", shape((page_size, 128), F32), [vmem(), vmem(), hbm(), vmem(), vmem(), vmem()],
        [pltpu.VMEM((steps, model // steps, hidden_units), BF), pltpu.SemaphoreType.DMA((steps,))],
    )(rows, gate_here, in_hbm(wi_up), down_score, own_score, own_docs)
    doc_sums = doc_sums.reshape(page_size, 1, 128)
    arrived = lax.all_to_all(doc_sums, "page", 0, 0, tiled=True)
    pooled = call(fold_kernel, "fold", shape((head_size, 1, 128), F32), [vmem()])(arrived)
    pooled = jnp.sum(lax.all_to_all(pooled, "head", 0, 0, tiled=True), axis=(0, 1))[:doc_dev]
    mine_docs = page_rank * doc_dev + jnp.arange(doc_dev, dtype=jnp.int32)
    counts = jnp.sum((doc_of_token[:, None] == mine_docs[None, :]).astype(F32), axis=0)
    return pooled / counts


def solution(mesh):
    return jax.shard_map(
        per_device,
        mesh=mesh,
        in_specs=(
            P("page", None),
            P(),
            P(None, "head"),
            P("page", None, "head"),
            P("page", None, "head"),
            P("page", None),
            P(None, "head"),
            P("head", None),
            P(),
            P(None, "head"),
            P(None, "head"),
            P("head", None),
            P(),
            P(),
            P(),
            P(),
            P(),
        ),
        out_specs=P("page"),
        check_vma=False,
    )
```

```python
import functools

import jax
import jax.numpy as jnp
from jax import lax
from jax.experimental import pallas as pl
from jax.experimental.pallas import tpu as pltpu
from jax.sharding import PartitionSpec as P

NQ = 8
DOCS = 256
MASKED = -1e30
BF = jnp.bfloat16
F32 = jnp.float32


def rms_scale(values, gain):
    values = values.astype(F32)
    return values * lax.rsqrt(jnp.mean(values * values, axis=-1, keepdims=True) + 1e-06) * gain


def split_three(value):
    first = value.astype(BF)
    rest = value - first.astype(F32)
    second = rest.astype(BF)
    third = (rest - second.astype(F32)).astype(BF)
    return first, second, third


def project_kernel(states, gain, weight, keys, values, buckets, out, payload, states_here, gain_here, weight_here,
                   buckets_here, queries_here, arrivals, sent):
    count = keys.shape[0]
    pairs = (
        (states, states_here),
        (gain, gain_here),
        (weight, weight_here),
        (buckets, buckets_here),
        (keys, payload.at[pl.ds(0, count)]),
        (values, payload.at[pl.ds(count + 8, count)]),
    )
    copies = [pltpu.make_async_copy(there, here, arrivals.at[i]) for i, (there, here) in enumerate(pairs)]
    for copy in copies:
        copy.start()
    copies[0].wait()
    copies[1].wait()
    normed = rms_scale(states_here[...], gain_here[...]).astype(BF)
    copies[3].wait()
    both = jnp.concatenate([buckets_here[0:1, :], buckets_here[1:2, :]], axis=1).astype(F32)
    payload[count : count + 8, :] = jnp.broadcast_to(both, (8, both.shape[1])).astype(BF)
    copies[2].wait()
    queries = jnp.dot(normed, weight_here[...], preferred_element_type=F32).astype(BF)
    queries_here[...] = queries
    sends = [pltpu.make_async_copy(queries_here, out.at[i], sent.at[i]) for i in range(out.shape[0])]
    for send in sends:
        send.start()
    copies[4].wait()
    copies[5].wait()
    for send in sends:
        send.wait()


def near_kernel(rank, first, second, bias_table, page_table, query_lengths, doc_query, doc_rows, keys_aug, values_t,
                extra, table_here, slots_here, lengths_here, info, arrivals, query_here, rows_here, doc_arrivals, *, pages):
    copies = [
        pltpu.make_async_copy(doc_query, query_here, doc_arrivals.at[0]),
        pltpu.make_async_copy(doc_rows, rows_here, doc_arrivals.at[1]),
    ]
    for copy in copies:
        copy.start()

    def columns():
        for copy in copies:
            copy.wait()
        query_columns(rank, query_here, rows_here, extra)

    prepare_kernel(
        rank, first, second, None, bias_table, page_table, query_lengths, keys_aug, values_t, table_here, slots_here,
        lengths_here, info, arrivals, side=0, pages=pages, meanwhile=columns,
    )


def query_columns(rank, doc_query, doc_rows, extra):
    tokens = extra.shape[0]
    tok_dev = doc_rows.shape[1] // 2
    row_chips = 4
    core = rank[0] % 2
    chip = rank[0] // 2
    pair = chip - chip % 2
    doc_count = doc_query.shape[1]
    left = lax.broadcasted_iota(jnp.int32, (1, 128), 1) < tok_dev
    doc_id = lax.broadcasted_iota(jnp.int32, (doc_count, 128), 0)
    blocks = []
    for y in range(tokens // (2 * tok_dev)):
        two = doc_rows[pl.ds(y * row_chips + pair % row_chips, 2), :]
        turned = pltpu.roll(two, tok_dev, 1)
        row = jnp.where(
            left,
            jnp.where(core == 0, two[0:1], turned[0:1]),
            jnp.where(core == 0, turned[1:2], two[1:2]),
        )
        blocks.append((doc_id == row).astype(F32).astype(BF))
    member = jnp.concatenate(blocks, axis=1)
    asked = jnp.broadcast_to(doc_query[...].astype(F32), (128, doc_count)).astype(BF)
    tok_query = jnp.dot(asked, member, preferred_element_type=F32)
    mark = lax.broadcasted_iota(jnp.int32, (128, tokens), 0) % 64
    columns = jnp.where(
        mark < NQ,
        jnp.where(tok_query == mark.astype(F32), 0.0, MASKED),
        jnp.where(mark == NQ, MASKED, jnp.where(mark < NQ + 4, 1.0, 0.0)),
    )
    extra[...] = columns.T.astype(BF)


def prepare_kernel(rank, first, second, third, bias_table, page_table, query_lengths, keys_aug, values_t, table_here,
                   slots_here, lengths_here, info, arrivals, *, side, pages, meanwhile=None):
    width, total = values_t.shape
    page_len = total // (2 * pages)
    keys = pages * page_len
    heads, bucket_count = bias_table.shape
    depth = width // heads
    slot_count = page_table.shape[0]
    max_pages = slot_count // NQ
    row_chips = 4
    pairs = [(page_table, slots_here), (query_lengths, lengths_here), (bias_table, table_here)]
    copies = [pltpu.make_async_copy(there, here, arrivals.at[i]) for i, (there, here) in enumerate(pairs)]
    for copy in copies:
        copy.start()
    sources = ((first, keys + 8), (second, keys + 8) if third is None else (third, 0))
    for part, (value_rows, offset) in enumerate(sources):
        for page in range(pages):
            value = value_rows[offset + page * page_len : offset + (page + 1) * page_len, :]
            values_t[:, pl.ds((part * pages + page) * page_len, page_len)] = value.astype(F32).T.astype(BF)
    if meanwhile is not None:
        meanwhile()
    core = rank[0] % 2
    chip = rank[0] // 2
    base = (chip // row_chips * row_chips + chip % 2) * 2 * pages
    count = 4 * pages
    copies[0].wait()
    copies[1].wait()
    for s in range(slot_count):
        place = slots_here[s] - base
        near = (place >= 0) & (place < 2 * pages)
        far = (place >= 4 * pages) & (place < 6 * pages)
        place = jnp.where(near, place, jnp.where(far, place - 2 * pages, count))
        info[0, place] = s // max_pages
        info[1, place] = lengths_here[s // max_pages] - (s % max_pages) * page_len
    low = lax.broadcasted_iota(jnp.int32, (1, 128), 1) < depth
    col = lax.broadcasted_iota(jnp.int32, (bucket_count, 128), 1) % 64
    copies[2].wait()
    table = jnp.concatenate([table_here[...], jnp.zeros((8 - heads, bucket_count), F32)], axis=0).T
    spreads = []
    for h in range(heads):
        a, b, c = split_three(jnp.broadcast_to(table[:, h : h + 1], (bucket_count, 128)))
        last = jnp.where(col == NQ + 3, c.astype(F32), 0.0)
        spreads.append(
            jnp.where(col == NQ + 1, a.astype(F32), jnp.where(col == NQ + 2, b.astype(F32), last)).astype(BF)
        )
    spread = jnp.concatenate(spreads, axis=1)
    bucket_row = lax.broadcasted_iota(jnp.int32, (bucket_count, page_len), 0).astype(F32)
    slot = lax.broadcasted_iota(jnp.int32, (page_len, 128), 0)
    key_col = lax.broadcasted_iota(jnp.int32, (page_len, 128), 1) % 64
    mine = ((chip % row_chips // 2) * 2 + core) * pages
    for part, key_rows in enumerate((first, second)):
        for page in range(pages):
            place = (mine ^ ((2 * side + part) * pages)) + page
            span = pl.ds((part * pages + page) * page_len, page_len)
            bucket = key_rows[keys : keys + 8, page * page_len : (page + 1) * page_len].astype(F32)[0:1]
            onehot = (jnp.broadcast_to(bucket, bucket_row.shape) == bucket_row).astype(F32).astype(BF)
            bias = lax.dot_general(onehot, spread, (((0,), (0,)), ((), ())), preferred_element_type=F32)
            holder = jnp.where(slot < info[1, place], info[0, place], NQ)
            marks = (key_col == holder).astype(F32)
            key = key_rows[page * page_len : (page + 1) * page_len, :].astype(F32)
            for h in range(heads):
                keep = low if h % 2 == 0 else jnp.logical_not(low)
                half = key[:, (h // 2) * 128 : (h // 2 + 1) * 128]
                keys_aug[h, span, :] = jnp.where(keep, half, bias[:, h * 128 : (h + 1) * 128] + marks).astype(BF)


def attention_kernel(queries, keys_near, keys_far, values_near, values_far, extra, out, rows_aug, parts, sent):
    chips, tok_dev, width = queries.shape
    heads = keys_near.shape[0]
    depth = width // heads
    low = lax.broadcasted_iota(jnp.int32, (1, 128), 1) < depth
    left = lax.broadcasted_iota(jnp.int32, (1, 128), 1) < tok_dev
    rows = queries[...].reshape(chips * tok_dev, width)
    for h in range(heads):
        half = rows[:, (h // 2) * 128 : (h // 2 + 1) * 128].astype(F32)
        keep = low if h % 2 == 0 else jnp.logical_not(low)
        rows_aug[h] = jnp.where(keep, half, extra[...].astype(F32)).astype(BF)
    sums = []
    logs = []

    def score(h):
        return [
            lax.dot_general(keys[h], rows_aug[h], (((1,), (1,)), ((), ())), preferred_element_type=F32)
            for keys in (keys_near, keys_far)
        ]

    ready = score(0)
    for h in range(heads):
        span = slice(h * depth, (h + 1) * depth)
        scores = ready
        if h + 1 < heads:
            ready = score(h + 1)
        top = jnp.maximum(
            jnp.max(scores[0], axis=0, keepdims=True), jnp.max(scores[1], axis=0, keepdims=True)
        )
        total = jnp.zeros_like(top)
        summed = jnp.zeros((depth, chips * tok_dev), F32)
        for part, values in zip(scores, (values_near, values_far)):
            weights = jnp.exp(part - top)
            total += jnp.sum(weights, axis=0, keepdims=True)
            summed += jnp.dot(values[span, :], weights.astype(BF), preferred_element_type=F32)
        sums.append(summed / total)
        logs.append(top + jnp.log(total))
    sends = []
    for duo in range(chips // 2):
        lanes = slice(duo * 128, (duo + 1) * 128)
        pad = [jnp.zeros((6, 128), F32)]
        upper = jnp.concatenate([sums[0][:, lanes], sums[1][:, lanes]], axis=0)
        lower = jnp.concatenate([sums[2][:, lanes], sums[3][:, lanes]], axis=0)
        stat_upper = jnp.concatenate([logs[0][:, lanes], logs[1][:, lanes]] + pad, axis=0)
        stat_lower = jnp.concatenate([logs[2][:, lanes], logs[3][:, lanes]] + pad, axis=0)
        block = (
            jnp.where(left, upper, pltpu.roll(lower, tok_dev, 1)),
            jnp.where(left, pltpu.roll(upper, tok_dev, 1), lower),
        )
        stat = (
            jnp.where(left, stat_upper, pltpu.roll(stat_lower, tok_dev, 1)),
            jnp.where(left, pltpu.roll(stat_upper, tok_dev, 1), stat_lower),
        )
        for which in range(2):
            a, b, c = split_three(stat[which])
            packed = [a[0:2].astype(F32), b[0:2].astype(F32), c[0:2].astype(F32), jnp.zeros((2, 128), F32)]
            parts[duo * 2 + which, 0:128, :] = block[which].astype(BF)
            parts[duo * 2 + which, 128:136, :] = jnp.concatenate(packed, axis=0).astype(BF)
        sends.append(pltpu.make_async_copy(parts.at[pl.ds(duo * 2, 2)], out.at[pl.ds(duo * 2, 2)], sent.at[duo]))
        sends[duo].start()
    for send in sends:
        send.wait()


def combine_kernel(parts, out_weight, out, product, sent):
    chips = parts.shape[0]
    logs = []
    for chip in range(chips):
        stat = parts[chip, 128:136, :].astype(F32)
        logs.append(stat[0:2] + stat[2:4] + stat[4:6])
    top = logs[0]
    for chip in range(1, chips):
        top = jnp.maximum(top, logs[chip])
    scales = [jnp.exp(log - top) for log in logs]
    whole = scales[0]
    for chip in range(1, chips):
        whole = whole + scales[chip]
    sums = [jnp.zeros((64, 128), F32), jnp.zeros((64, 128), F32)]
    for chip in range(chips):
        share = scales[chip] / whole
        for r in range(2):
            sums[r] = sums[r] + share[r : r + 1] * parts[chip, r * 64 : (r + 1) * 64, :].astype(F32)
    joined = jnp.concatenate(sums, axis=0).T
    context = jnp.concatenate([joined[0:64], joined[64:128]], axis=1).astype(BF)
    sends = []
    for i in range(product.shape[0]):
        cols = slice(i * product.shape[2], (i + 1) * product.shape[2])
        product[i] = jnp.dot(context, out_weight[:, cols], preferred_element_type=F32).astype(BF)
        place = out.at[:, pl.ds(i * product.shape[2], product.shape[2])]
        sends.append(pltpu.make_async_copy(product.at[i], place, sent.at[i]))
        sends[i].start()
    for send in sends:
        send.wait()


def norm_kernel(terms, states, gain, score_vector, out, score, normed, sent):
    hidden = states[...].astype(F32)
    for source in range(terms.shape[0]):
        hidden = hidden + terms[source].astype(F32)
    normed[...] = rms_scale(hidden, gain[...]).astype(BF)
    sends = [pltpu.make_async_copy(normed, out.at[i], sent.at[i]) for i in range(out.shape[0])]
    for send in sends:
        send.start()
    score[...] = jnp.broadcast_to(jnp.sum(hidden * score_vector[...], axis=-1, keepdims=True), score.shape)
    for send in sends:
        send.wait()


def down_kernel(weight, score_vector, out_weight, out, fetched, weight_here, arrivals):
    copy = pltpu.make_async_copy(weight, weight_here, arrivals.at[0])
    fetch = pltpu.make_async_copy(out_weight, fetched, arrivals.at[1])
    fetch.start()
    copy.start()
    pieces = [piece.astype(F32) for piece in split_three(score_vector[...])]
    rows = jnp.concatenate(pieces + [jnp.zeros((5, score_vector.shape[1]), F32)], axis=0).astype(BF)
    copy.wait()
    terms = lax.dot_general(rows, weight_here[...], (((1,), (1,)), ((), ())), preferred_element_type=F32)
    out[...] = terms[0:1] + terms[1:2] + terms[2:3]
    fetch.wait()


def fetch_kernel(weight, out, arrival):
    copy = pltpu.make_async_copy(weight, out, arrival)
    copy.start()
    copy.wait()


def feed_kernel(rows, gate_weight, up_weight, down_score, own_score, own_docs, out, up_here, arrivals):
    steps = up_here.shape[0]
    size = rows.shape[1] // steps
    copies = [
        pltpu.make_async_copy(up_weight.at[pl.ds(i * size, size)], up_here.at[i], arrivals.at[i]) for i in range(steps)
    ]
    for copy in copies:
        copy.start()
    docs = own_docs[...]
    doc_dev = DOCS // out.shape[0]
    lane = lax.broadcasted_iota(jnp.int32, (docs.shape[0], 128), 1)
    holder = (docs // doc_dev == lane).astype(F32).astype(BF)
    gate = jnp.dot(rows[...], gate_weight[...], preferred_element_type=F32)
    gate = jax.nn.gelu(gate, approximate=True)
    upper = jnp.zeros_like(gate)
    for i in range(steps):
        copies[i].wait()
        upper += jnp.dot(rows[:, i * size : (i + 1) * size], up_here[i], preferred_element_type=F32)
    middle = (gate * upper).astype(BF).astype(F32)
    tok_score = jnp.sum(middle * down_score[...], axis=-1, keepdims=True) + own_score[...]
    placed = jnp.where(docs % doc_dev == lane, tok_score, 0.0)
    pieces = jnp.concatenate([piece.astype(F32) for piece in split_three(placed)], axis=1).astype(BF)
    sums = lax.dot_general(holder, pieces, (((0,), (0,)), ((), ())), preferred_element_type=F32)[0 : out.shape[0]]
    out[...] = sums[:, 0:128] + sums[:, 128:256] + sums[:, 256:384]


def fold_kernel(terms, out):
    out[...] = jnp.broadcast_to(jnp.sum(terms[...], axis=0, keepdims=True), out.shape)


def vmem():
    return pl.BlockSpec(memory_space=pltpu.VMEM)


def smem():
    return pl.BlockSpec(memory_space=pltpu.SMEM)


def in_hbm(value):
    return pltpu.with_memory_space_constraint(value, pltpu.HBM)


def hbm():
    return pl.BlockSpec(memory_space=pltpu.HBM)


def anywhere():
    return pl.BlockSpec(memory_space=pl.ANY)


def call(kernel, name, shapes, specs, scratch=(), results=None):
    single = not isinstance(shapes, (list, tuple))
    return pl.pallas_call(
        kernel,
        out_shape=shapes,
        in_specs=specs,
        out_specs=results or (vmem() if single else [vmem()] * len(shapes)),
        scratch_shapes=list(scratch),
        compiler_params=pltpu.CompilerParams(vmem_limit_bytes=40 << 20),
        name=name,
    )


def per_device(
    doc_states,
    gain_attn,
    query_weight,
    cache_keys,
    cache_values,
    rel_bucket,
    bias_table,
    out_weight,
    gain_ffn,
    wi_gate,
    wi_up,
    wo_ffn,
    score_vector,
    query_lengths,
    doc_query,
    doc_of_token,
    page_table,
):
    shape = jax.ShapeDtypeStruct
    tok_dev, model = doc_states.shape
    local_pages, page_len, local_width = cache_keys.shape
    local_heads = bias_table.shape[1]
    page_size = lax.axis_size("page")
    head_size = lax.axis_size("head")
    page_rank = lax.axis_index("page")
    head_rank = lax.axis_index("head")
    group = page_size // 4
    groups = [
        [y * 8 + (x + side) * 2 + core for y in range(4) for side in range(2)] for x in (0, 2) for core in range(2)
    ]
    core_swap = [(i, i ^ 1) for i in range(page_size)]
    side_swap = [(i, i ^ 4) for i in range(page_size)]

    def swap(value, pairs):
        return lax.ppermute(value, "page", pairs)

    keys_held = local_pages * page_len
    copies, payload = call(
        project_kernel,
        "project",
        [shape((group, tok_dev, local_width), BF), shape((2 * keys_held + 8, local_width), BF)],
        [hbm()] * 6,
        [
            pltpu.VMEM((tok_dev, model), BF),
            pltpu.VMEM((1, model), F32),
            pltpu.VMEM((model, local_width), BF),
            pltpu.VMEM((local_pages, page_len), jnp.int32),
            pltpu.VMEM((tok_dev, local_width), BF),
            pltpu.SemaphoreType.DMA((6,)),
            pltpu.SemaphoreType.DMA((group,)),
        ],
        [hbm(), vmem()],
    )(
        in_hbm(doc_states),
        in_hbm(gain_attn.reshape(1, model)),
        in_hbm(query_weight),
        in_hbm(cache_keys.reshape(keys_held, local_width)),
        in_hbm(cache_values.reshape(keys_held, local_width)),
        in_hbm(rel_bucket),
    )
    payload_side = swap(payload, side_swap)
    payload_core = swap(payload, core_swap)
    keys_far = swap(payload_side[0 : keys_held + 8], core_swap)
    values_far = swap(payload_side[keys_held + 8 :], core_swap)
    gathered = lax.all_to_all(copies, "page", 0, 0, axis_index_groups=groups, tiled=True)

    rank = page_rank.reshape(1)
    doc_rows = doc_of_token.reshape(-1, 2 * tok_dev)
    key_count = 2 * local_pages * page_len

    shapes = [shape((local_heads, key_count, 128), BF), shape((local_width, key_count), BF)]
    scratch = [
        pltpu.VMEM(bias_table.T.shape, F32),
        pltpu.SMEM(page_table.shape, jnp.int32),
        pltpu.SMEM(query_lengths.shape, jnp.int32),
        pltpu.SMEM((2, 4 * local_pages + 1), jnp.int32),
        pltpu.SemaphoreType.DMA((3,)),
    ]
    tables = (in_hbm(bias_table.T), in_hbm(page_table), in_hbm(query_lengths))
    keys_near, values_near, extra = call(
        functools.partial(near_kernel, pages=local_pages),
        "near",
        shapes + [shape((group * tok_dev, 128), BF)],
        [smem()] + [vmem()] * 2 + [hbm()] * 5,
        scratch
        + [
            pltpu.VMEM((1, doc_query.shape[0]), jnp.int32),
            pltpu.VMEM(doc_rows.shape, jnp.int32),
            pltpu.SemaphoreType.DMA((2,)),
        ],
    )(rank, payload, payload_core, *tables, in_hbm(doc_query.reshape(1, -1)), in_hbm(doc_rows))
    keys_away, values_away = call(
        functools.partial(prepare_kernel, side=1, pages=local_pages),
        "away",
        shapes,
        [smem()] + [vmem()] * 3 + [hbm()] * 3,
        scratch,
    )(rank, payload_side, keys_far, values_far, *tables)
    partials = call(
        attention_kernel,
        "attention",
        shape((group, 136, 128), BF),
        [vmem()] * 6,
        [
            pltpu.VMEM((local_heads, group * tok_dev, 128), BF),
            pltpu.VMEM((group, 136, 128), BF),
            pltpu.SemaphoreType.DMA((group // 2,)),
        ],
        hbm(),
    )(gathered, keys_near, keys_away, values_near, values_away, extra)
    partials, down_weight, late_weight = lax.optimization_barrier((partials, wo_ffn, out_weight))
    hidden_units = wi_gate.shape[1]
    down_score, fetched = call(
        down_kernel,
        "down",
        [shape((1, hidden_units), F32), shape(out_weight.shape, BF)],
        [hbm(), vmem(), hbm()],
        [pltpu.VMEM(wo_ffn.shape, BF), pltpu.SemaphoreType.DMA((2,))],
    )(in_hbm(down_weight), score_vector.reshape(1, model), in_hbm(late_weight))
    returned = lax.all_to_all(partials, "page", 0, 0, axis_index_groups=groups, tiled=True)
    projected = call(
        combine_kernel, "combine", shape((tok_dev, model), BF), [vmem()] * 2,
        [pltpu.VMEM((4, tok_dev, model // 4), BF), pltpu.SemaphoreType.DMA((4,))],
        hbm(),
    )(returned, fetched)

    own = tok_dev // head_size
    terms = lax.all_to_all(projected.reshape(head_size, own, model), "head", 0, 0, tiled=True)
    own_states = lax.dynamic_slice_in_dim(doc_states, head_rank * own, own, 0)
    spread, hidden_score = call(
        norm_kernel,
        "norm",
        [shape((head_size, own, model), BF), shape((own, 128), F32)],
        [vmem()] * 4,
        [pltpu.VMEM((own, model), BF), pltpu.SemaphoreType.DMA((head_size,))],
        [hbm(), vmem()],
    )(terms, own_states, gain_ffn.reshape(1, model), score_vector.reshape(1, model))
    spread, late_gate = lax.optimization_barrier((spread, wi_gate))
    gate_here = call(
        fetch_kernel, "fetch", shape(wi_gate.shape, BF), [hbm()], [pltpu.SemaphoreType.DMA(())]
    )(in_hbm(late_gate))
    rows = lax.all_to_all(spread, "head", 0, 0, tiled=True).reshape(tok_dev, model)
    token = jnp.arange(tok_dev, dtype=jnp.int32)[:, None]
    own_score = jnp.where(token // own == head_rank, jnp.tile(hidden_score[:, :1], (head_size, 1)), 0.0)
    own_docs = lax.dynamic_slice_in_dim(doc_of_token, page_rank * tok_dev, tok_dev, 0)[:, None]
    doc_dev = doc_query.shape[0] // page_size
    steps = 4
    doc_sums = call(
        feed_kernel, "feed", shape((page_size, 128), F32), [vmem(), vmem(), hbm(), vmem(), vmem(), vmem()],
        [pltpu.VMEM((steps, model // steps, hidden_units), BF), pltpu.SemaphoreType.DMA((steps,))],
    )(rows, gate_here, in_hbm(wi_up), down_score, own_score, own_docs)
    doc_sums = doc_sums.reshape(page_size, 1, 128)
    arrived = lax.all_to_all(doc_sums, "page", 0, 0, tiled=True)
    pooled = call(fold_kernel, "fold", shape((head_size, 1, 128), F32), [vmem()])(arrived)
    pooled = jnp.sum(lax.all_to_all(pooled, "head", 0, 0, tiled=True), axis=(0, 1))[:doc_dev]
    mine_docs = page_rank * doc_dev + jnp.arange(doc_dev, dtype=jnp.int32)
    counts = jnp.sum((doc_of_token[:, None] == mine_docs[None, :]).astype(F32), axis=0)
    return pooled / counts


def solution(mesh):
    return jax.shard_map(
        per_device,
        mesh=mesh,
        in_specs=(
            P("page", None),
            P(),
            P(None, "head"),
            P("page", None, "head"),
            P("page", None, "head"),
            P("page", None),
            P(None, "head"),
            P("head", None),
            P(),
            P(None, "head"),
            P(None, "head"),
            P("head", None),
            P(),
            P(),
            P(),
            P(),
            P(),
        ),
        out_specs=P("page"),
        check_vma=False,
    )
```

```python
import functools

import jax
import jax.numpy as jnp
from jax import lax
from jax.experimental import pallas as pl
from jax.experimental.pallas import tpu as pltpu
from jax.sharding import PartitionSpec as P

NQ = 8
DOCS = 256
MASKED = -1e30
BF = jnp.bfloat16
F32 = jnp.float32


def rms_scale(values, gain):
    values = values.astype(F32)
    return values * lax.rsqrt(jnp.mean(values * values, axis=-1, keepdims=True) + 1e-06) * gain


def split_three(value):
    first = value.astype(BF)
    rest = value - first.astype(F32)
    second = rest.astype(BF)
    third = (rest - second.astype(F32)).astype(BF)
    return first, second, third


def project_kernel(states, gain, weight, keys, values, buckets, out, payload, states_here, gain_here, weight_here,
                   buckets_here, arrivals):
    count = keys.shape[0]
    pairs = (
        (states, states_here),
        (gain, gain_here),
        (weight, weight_here),
        (buckets, buckets_here),
        (keys, payload.at[pl.ds(0, count)]),
        (values, payload.at[pl.ds(count + 8, count)]),
    )
    copies = [pltpu.make_async_copy(there, here, arrivals.at[i]) for i, (there, here) in enumerate(pairs)]
    for copy in copies:
        copy.start()
    copies[0].wait()
    copies[1].wait()
    normed = rms_scale(states_here[...], gain_here[...]).astype(BF)
    copies[3].wait()
    both = jnp.concatenate([buckets_here[0:1, :], buckets_here[1:2, :]], axis=1).astype(F32)
    payload[count : count + 8, :] = jnp.broadcast_to(both, (8, both.shape[1])).astype(BF)
    copies[2].wait()
    queries = jnp.dot(normed, weight_here[...], preferred_element_type=F32).astype(BF)
    for chip in range(out.shape[0]):
        out[chip] = queries
    copies[4].wait()
    copies[5].wait()


def near_kernel(rank, first, second, bias_table, page_table, query_lengths, doc_query, doc_rows, keys_aug, values_t,
                extra, table_here, slots_here, lengths_here, info, arrivals, query_here, rows_here, doc_arrivals, *, pages):
    copies = [
        pltpu.make_async_copy(doc_query, query_here, doc_arrivals.at[0]),
        pltpu.make_async_copy(doc_rows, rows_here, doc_arrivals.at[1]),
    ]
    for copy in copies:
        copy.start()

    def columns():
        for copy in copies:
            copy.wait()
        query_columns(rank, query_here, rows_here, extra)

    prepare_kernel(
        rank, first, second, None, bias_table, page_table, query_lengths, keys_aug, values_t, table_here, slots_here,
        lengths_here, info, arrivals, side=0, pages=pages, meanwhile=columns,
    )


def query_columns(rank, doc_query, doc_rows, extra):
    tokens = extra.shape[0]
    tok_dev = doc_rows.shape[1] // 2
    row_chips = 4
    core = rank[0] % 2
    chip = rank[0] // 2
    pair = chip - chip % 2
    doc_count = doc_query.shape[1]
    left = lax.broadcasted_iota(jnp.int32, (1, 128), 1) < tok_dev
    doc_id = lax.broadcasted_iota(jnp.int32, (doc_count, 128), 0)
    blocks = []
    for y in range(tokens // (2 * tok_dev)):
        two = doc_rows[pl.ds(y * row_chips + pair % row_chips, 2), :]
        turned = pltpu.roll(two, tok_dev, 1)
        row = jnp.where(
            left,
            jnp.where(core == 0, two[0:1], turned[0:1]),
            jnp.where(core == 0, turned[1:2], two[1:2]),
        )
        blocks.append((doc_id == row).astype(F32).astype(BF))
    member = jnp.concatenate(blocks, axis=1)
    asked = jnp.broadcast_to(doc_query[...].astype(F32), (128, doc_count)).astype(BF)
    tok_query = jnp.dot(asked, member, preferred_element_type=F32)
    mark = lax.broadcasted_iota(jnp.int32, (128, tokens), 0) % 64
    columns = jnp.where(
        mark < NQ,
        jnp.where(tok_query == mark.astype(F32), 0.0, MASKED),
        jnp.where(mark == NQ, MASKED, jnp.where(mark < NQ + 4, 1.0, 0.0)),
    )
    extra[...] = columns.T.astype(BF)


def prepare_kernel(rank, first, second, third, bias_table, page_table, query_lengths, keys_aug, values_t, table_here,
                   slots_here, lengths_here, info, arrivals, *, side, pages, meanwhile=None):
    width, total = values_t.shape
    page_len = total // (2 * pages)
    keys = pages * page_len
    heads, bucket_count = bias_table.shape
    depth = width // heads
    slot_count = page_table.shape[0]
    max_pages = slot_count // NQ
    row_chips = 4
    pairs = [(page_table, slots_here), (query_lengths, lengths_here), (bias_table, table_here)]
    copies = [pltpu.make_async_copy(there, here, arrivals.at[i]) for i, (there, here) in enumerate(pairs)]
    for copy in copies:
        copy.start()
    sources = ((first, keys + 8), (second, keys + 8) if third is None else (third, 0))
    for part, (value_rows, offset) in enumerate(sources):
        for page in range(pages):
            value = value_rows[offset + page * page_len : offset + (page + 1) * page_len, :]
            values_t[:, pl.ds((part * pages + page) * page_len, page_len)] = value.astype(F32).T.astype(BF)
    if meanwhile is not None:
        meanwhile()
    core = rank[0] % 2
    chip = rank[0] // 2
    base = (chip // row_chips * row_chips + chip % 2) * 2 * pages
    count = 4 * pages
    copies[0].wait()
    copies[1].wait()
    for s in range(slot_count):
        place = slots_here[s] - base
        near = (place >= 0) & (place < 2 * pages)
        far = (place >= 4 * pages) & (place < 6 * pages)
        place = jnp.where(near, place, jnp.where(far, place - 2 * pages, count))
        info[0, place] = s // max_pages
        info[1, place] = lengths_here[s // max_pages] - (s % max_pages) * page_len
    low = lax.broadcasted_iota(jnp.int32, (1, 128), 1) < depth
    col = lax.broadcasted_iota(jnp.int32, (bucket_count, 128), 1) % 64
    copies[2].wait()
    table = jnp.concatenate([table_here[...], jnp.zeros((8 - heads, bucket_count), F32)], axis=0).T
    spreads = []
    for h in range(heads):
        a, b, c = split_three(jnp.broadcast_to(table[:, h : h + 1], (bucket_count, 128)))
        last = jnp.where(col == NQ + 3, c.astype(F32), 0.0)
        spreads.append(
            jnp.where(col == NQ + 1, a.astype(F32), jnp.where(col == NQ + 2, b.astype(F32), last)).astype(BF)
        )
    spread = jnp.concatenate(spreads, axis=1)
    bucket_row = lax.broadcasted_iota(jnp.int32, (bucket_count, page_len), 0).astype(F32)
    slot = lax.broadcasted_iota(jnp.int32, (page_len, 128), 0)
    key_col = lax.broadcasted_iota(jnp.int32, (page_len, 128), 1) % 64
    mine = ((chip % row_chips // 2) * 2 + core) * pages
    for part, key_rows in enumerate((first, second)):
        for page in range(pages):
            place = (mine ^ ((2 * side + part) * pages)) + page
            span = pl.ds((part * pages + page) * page_len, page_len)
            bucket = key_rows[keys : keys + 8, page * page_len : (page + 1) * page_len].astype(F32)[0:1]
            onehot = (jnp.broadcast_to(bucket, bucket_row.shape) == bucket_row).astype(F32).astype(BF)
            bias = lax.dot_general(onehot, spread, (((0,), (0,)), ((), ())), preferred_element_type=F32)
            holder = jnp.where(slot < info[1, place], info[0, place], NQ)
            marks = (key_col == holder).astype(F32)
            key = key_rows[page * page_len : (page + 1) * page_len, :].astype(F32)
            for h in range(heads):
                keep = low if h % 2 == 0 else jnp.logical_not(low)
                half = key[:, (h // 2) * 128 : (h // 2 + 1) * 128]
                keys_aug[h, span, :] = jnp.where(keep, half, bias[:, h * 128 : (h + 1) * 128] + marks).astype(BF)


def attention_kernel(queries, keys_near, keys_far, values_near, values_far, extra, out, rows_aug):
    chips, tok_dev, width = queries.shape
    heads = keys_near.shape[0]
    depth = width // heads
    low = lax.broadcasted_iota(jnp.int32, (1, 128), 1) < depth
    left = lax.broadcasted_iota(jnp.int32, (1, 128), 1) < tok_dev
    rows = queries[...].reshape(chips * tok_dev, width)
    for h in range(heads):
        half = rows[:, (h // 2) * 128 : (h // 2 + 1) * 128].astype(F32)
        keep = low if h % 2 == 0 else jnp.logical_not(low)
        rows_aug[h] = jnp.where(keep, half, extra[...].astype(F32)).astype(BF)
    sums = []
    logs = []

    def score(h):
        return [
            lax.dot_general(keys[h], rows_aug[h], (((1,), (1,)), ((), ())), preferred_element_type=F32)
            for keys in (keys_near, keys_far)
        ]

    ready = score(0)
    for h in range(heads):
        span = slice(h * depth, (h + 1) * depth)
        scores = ready
        if h + 1 < heads:
            ready = score(h + 1)
        top = jnp.maximum(
            jnp.max(scores[0], axis=0, keepdims=True), jnp.max(scores[1], axis=0, keepdims=True)
        )
        total = jnp.zeros_like(top)
        summed = jnp.zeros((depth, chips * tok_dev), F32)
        for part, values in zip(scores, (values_near, values_far)):
            weights = jnp.exp(part - top)
            total += jnp.sum(weights, axis=0, keepdims=True)
            summed += jnp.dot(values[span, :], weights.astype(BF), preferred_element_type=F32)
        sums.append(summed / total)
        logs.append(top + jnp.log(total))
    for duo in range(chips // 2):
        lanes = slice(duo * 128, (duo + 1) * 128)
        pad = [jnp.zeros((6, 128), F32)]
        upper = jnp.concatenate([sums[0][:, lanes], sums[1][:, lanes]], axis=0)
        lower = jnp.concatenate([sums[2][:, lanes], sums[3][:, lanes]], axis=0)
        stat_upper = jnp.concatenate([logs[0][:, lanes], logs[1][:, lanes]] + pad, axis=0)
        stat_lower = jnp.concatenate([logs[2][:, lanes], logs[3][:, lanes]] + pad, axis=0)
        block = (
            jnp.where(left, upper, pltpu.roll(lower, tok_dev, 1)),
            jnp.where(left, pltpu.roll(upper, tok_dev, 1), lower),
        )
        stat = (
            jnp.where(left, stat_upper, pltpu.roll(stat_lower, tok_dev, 1)),
            jnp.where(left, pltpu.roll(stat_upper, tok_dev, 1), stat_lower),
        )
        for which in range(2):
            a, b, c = split_three(stat[which])
            packed = [a[0:2].astype(F32), b[0:2].astype(F32), c[0:2].astype(F32), jnp.zeros((2, 128), F32)]
            out[duo * 2 + which, 0:128, :] = block[which].astype(BF)
            out[duo * 2 + which, 128:136, :] = jnp.concatenate(packed, axis=0).astype(BF)


def combine_kernel(parts, out_weight, out):
    chips = parts.shape[0]
    logs = []
    for chip in range(chips):
        stat = parts[chip, 128:136, :].astype(F32)
        logs.append(stat[0:2] + stat[2:4] + stat[4:6])
    top = logs[0]
    for chip in range(1, chips):
        top = jnp.maximum(top, logs[chip])
    scales = [jnp.exp(log - top) for log in logs]
    whole = scales[0]
    for chip in range(1, chips):
        whole = whole + scales[chip]
    sums = [jnp.zeros((64, 128), F32), jnp.zeros((64, 128), F32)]
    for chip in range(chips):
        share = scales[chip] / whole
        for r in range(2):
            sums[r] = sums[r] + share[r : r + 1] * parts[chip, r * 64 : (r + 1) * 64, :].astype(F32)
    joined = jnp.concatenate(sums, axis=0).T
    context = jnp.concatenate([joined[0:64], joined[64:128]], axis=1).astype(BF)
    out[...] = jnp.dot(context, out_weight[...], preferred_element_type=F32).astype(BF)


def norm_kernel(terms, states, gain, score_vector, out, score):
    hidden = states[...].astype(F32)
    for source in range(terms.shape[0]):
        hidden = hidden + terms[source].astype(F32)
    normed = rms_scale(hidden, gain[...]).astype(BF)
    for target in range(out.shape[0]):
        out[target] = normed
    score[...] = jnp.broadcast_to(jnp.sum(hidden * score_vector[...], axis=-1, keepdims=True), score.shape)


def down_kernel(weight, score_vector, out_weight, out, fetched, weight_here, arrivals):
    copy = pltpu.make_async_copy(weight, weight_here, arrivals.at[0])
    fetch = pltpu.make_async_copy(out_weight, fetched, arrivals.at[1])
    fetch.start()
    copy.start()
    pieces = [piece.astype(F32) for piece in split_three(score_vector[...])]
    rows = jnp.concatenate(pieces + [jnp.zeros((5, score_vector.shape[1]), F32)], axis=0).astype(BF)
    copy.wait()
    terms = lax.dot_general(rows, weight_here[...], (((1,), (1,)), ((), ())), preferred_element_type=F32)
    out[...] = terms[0:1] + terms[1:2] + terms[2:3]
    fetch.wait()


def fetch_kernel(weight, out, arrival):
    copy = pltpu.make_async_copy(weight, out, arrival)
    copy.start()
    copy.wait()


def feed_kernel(rows, gate_weight, up_weight, down_score, own_score, own_docs, out, up_here, arrivals):
    steps = up_here.shape[0]
    size = rows.shape[1] // steps
    copies = [
        pltpu.make_async_copy(up_weight.at[pl.ds(i * size, size)], up_here.at[i], arrivals.at[i]) for i in range(steps)
    ]
    for copy in copies:
        copy.start()
    docs = own_docs[...]
    doc_dev = DOCS // out.shape[0]
    lane = lax.broadcasted_iota(jnp.int32, (docs.shape[0], 128), 1)
    holder = (docs // doc_dev == lane).astype(F32).astype(BF)
    gate = jnp.dot(rows[...], gate_weight[...], preferred_element_type=F32)
    gate = jax.nn.gelu(gate, approximate=True)
    upper = jnp.zeros_like(gate)
    for i in range(steps):
        copies[i].wait()
        upper += jnp.dot(rows[:, i * size : (i + 1) * size], up_here[i], preferred_element_type=F32)
    middle = (gate * upper).astype(BF).astype(F32)
    tok_score = jnp.sum(middle * down_score[...], axis=-1, keepdims=True) + own_score[...]
    placed = jnp.where(docs % doc_dev == lane, tok_score, 0.0)
    pieces = jnp.concatenate([piece.astype(F32) for piece in split_three(placed)], axis=1).astype(BF)
    sums = lax.dot_general(holder, pieces, (((0,), (0,)), ((), ())), preferred_element_type=F32)[0 : out.shape[0]]
    out[...] = sums[:, 0:128] + sums[:, 128:256] + sums[:, 256:384]


def fold_kernel(terms, out):
    out[...] = jnp.broadcast_to(jnp.sum(terms[...], axis=0, keepdims=True), out.shape)


def vmem():
    return pl.BlockSpec(memory_space=pltpu.VMEM)


def smem():
    return pl.BlockSpec(memory_space=pltpu.SMEM)


def in_hbm(value):
    return pltpu.with_memory_space_constraint(value, pltpu.HBM)


def hbm():
    return pl.BlockSpec(memory_space=pltpu.HBM)


def anywhere():
    return pl.BlockSpec(memory_space=pl.ANY)


def call(kernel, name, shapes, specs, scratch=()):
    single = not isinstance(shapes, (list, tuple))
    return pl.pallas_call(
        kernel,
        out_shape=shapes,
        in_specs=specs,
        out_specs=vmem() if single else [vmem()] * len(shapes),
        scratch_shapes=list(scratch),
        compiler_params=pltpu.CompilerParams(vmem_limit_bytes=40 << 20),
        name=name,
    )


def per_device(
    doc_states,
    gain_attn,
    query_weight,
    cache_keys,
    cache_values,
    rel_bucket,
    bias_table,
    out_weight,
    gain_ffn,
    wi_gate,
    wi_up,
    wo_ffn,
    score_vector,
    query_lengths,
    doc_query,
    doc_of_token,
    page_table,
):
    shape = jax.ShapeDtypeStruct
    tok_dev, model = doc_states.shape
    local_pages, page_len, local_width = cache_keys.shape
    local_heads = bias_table.shape[1]
    page_size = lax.axis_size("page")
    head_size = lax.axis_size("head")
    page_rank = lax.axis_index("page")
    head_rank = lax.axis_index("head")
    group = page_size // 4
    groups = [
        [y * 8 + (x + side) * 2 + core for y in range(4) for side in range(2)] for x in (0, 2) for core in range(2)
    ]
    core_swap = [(i, i ^ 1) for i in range(page_size)]
    side_swap = [(i, i ^ 4) for i in range(page_size)]

    def swap(value, pairs):
        return lax.ppermute(value, "page", pairs)

    keys_held = local_pages * page_len
    copies, payload = call(
        project_kernel,
        "project",
        [shape((group, tok_dev, local_width), BF), shape((2 * keys_held + 8, local_width), BF)],
        [hbm()] * 6,
        [
            pltpu.VMEM((tok_dev, model), BF),
            pltpu.VMEM((1, model), F32),
            pltpu.VMEM((model, local_width), BF),
            pltpu.VMEM((local_pages, page_len), jnp.int32),
            pltpu.SemaphoreType.DMA((6,)),
        ],
    )(
        in_hbm(doc_states),
        in_hbm(gain_attn.reshape(1, model)),
        in_hbm(query_weight),
        in_hbm(cache_keys.reshape(keys_held, local_width)),
        in_hbm(cache_values.reshape(keys_held, local_width)),
        in_hbm(rel_bucket),
    )
    payload_side = swap(payload, side_swap)
    payload_core = swap(payload, core_swap)
    keys_far = swap(payload_side[0 : keys_held + 8], core_swap)
    values_far = swap(payload_side[keys_held + 8 :], core_swap)
    gathered = lax.all_to_all(copies, "page", 0, 0, axis_index_groups=groups, tiled=True)

    rank = page_rank.reshape(1)
    doc_rows = doc_of_token.reshape(-1, 2 * tok_dev)
    key_count = 2 * local_pages * page_len

    shapes = [shape((local_heads, key_count, 128), BF), shape((local_width, key_count), BF)]
    scratch = [
        pltpu.VMEM(bias_table.T.shape, F32),
        pltpu.SMEM(page_table.shape, jnp.int32),
        pltpu.SMEM(query_lengths.shape, jnp.int32),
        pltpu.SMEM((2, 4 * local_pages + 1), jnp.int32),
        pltpu.SemaphoreType.DMA((3,)),
    ]
    tables = (in_hbm(bias_table.T), in_hbm(page_table), in_hbm(query_lengths))
    keys_near, values_near, extra = call(
        functools.partial(near_kernel, pages=local_pages),
        "near",
        shapes + [shape((group * tok_dev, 128), BF)],
        [smem()] + [vmem()] * 2 + [hbm()] * 5,
        scratch
        + [
            pltpu.VMEM((1, doc_query.shape[0]), jnp.int32),
            pltpu.VMEM(doc_rows.shape, jnp.int32),
            pltpu.SemaphoreType.DMA((2,)),
        ],
    )(rank, payload, payload_core, *tables, in_hbm(doc_query.reshape(1, -1)), in_hbm(doc_rows))
    keys_away, values_away = call(
        functools.partial(prepare_kernel, side=1, pages=local_pages),
        "away",
        shapes,
        [smem()] + [vmem()] * 3 + [hbm()] * 3,
        scratch,
    )(rank, payload_side, keys_far, values_far, *tables)
    partials = call(
        attention_kernel,
        "attention",
        shape((group, 136, 128), BF),
        [vmem()] * 6,
        [pltpu.VMEM((local_heads, group * tok_dev, 128), BF)],
    )(gathered, keys_near, keys_away, values_near, values_away, extra)
    partials, down_weight, late_weight = lax.optimization_barrier((partials, wo_ffn, out_weight))
    hidden_units = wi_gate.shape[1]
    down_score, fetched = call(
        down_kernel,
        "down",
        [shape((1, hidden_units), F32), shape(out_weight.shape, BF)],
        [hbm(), vmem(), hbm()],
        [pltpu.VMEM(wo_ffn.shape, BF), pltpu.SemaphoreType.DMA((2,))],
    )(in_hbm(down_weight), score_vector.reshape(1, model), in_hbm(late_weight))
    returned = lax.all_to_all(partials, "page", 0, 0, axis_index_groups=groups, tiled=True)
    projected = call(combine_kernel, "combine", shape((tok_dev, model), BF), [vmem()] * 2)(returned, fetched)

    doc_dev = doc_query.shape[0] // page_size
    mine_docs = page_rank * doc_dev + jnp.arange(doc_dev, dtype=jnp.int32)
    counts = jnp.sum((doc_of_token[:, None] == mine_docs[None, :]).astype(F32), axis=0)
    own = tok_dev // head_size
    own_states = lax.dynamic_slice_in_dim(doc_states, head_rank * own, own, 0)
    projected, counts, own_states = lax.optimization_barrier((projected, counts, own_states))
    terms = lax.all_to_all(projected.reshape(head_size, own, model), "head", 0, 0, tiled=True)
    spread, hidden_score = call(
        norm_kernel,
        "norm",
        [shape((head_size, own, model), BF), shape((own, 128), F32)],
        [vmem()] * 4,
    )(terms, own_states, gain_ffn.reshape(1, model), score_vector.reshape(1, model))
    spread, late_gate = lax.optimization_barrier((spread, wi_gate))
    gate_here = call(
        fetch_kernel, "fetch", shape(wi_gate.shape, BF), [hbm()], [pltpu.SemaphoreType.DMA(())]
    )(in_hbm(late_gate))
    rows = lax.all_to_all(spread, "head", 0, 0, tiled=True).reshape(tok_dev, model)
    token = jnp.arange(tok_dev, dtype=jnp.int32)[:, None]
    own_score = jnp.where(token // own == head_rank, jnp.tile(hidden_score[:, :1], (head_size, 1)), 0.0)
    own_docs = lax.dynamic_slice_in_dim(doc_of_token, page_rank * tok_dev, tok_dev, 0)[:, None]
    steps = 4
    doc_sums = call(
        feed_kernel, "feed", shape((page_size, 128), F32), [vmem(), vmem(), hbm(), vmem(), vmem(), vmem()],
        [pltpu.VMEM((steps, model // steps, hidden_units), BF), pltpu.SemaphoreType.DMA((steps,))],
    )(rows, gate_here, in_hbm(wi_up), down_score, own_score, own_docs)
    doc_sums = doc_sums.reshape(page_size, 1, 128)
    arrived = lax.all_to_all(doc_sums, "page", 0, 0, tiled=True)
    pooled = call(fold_kernel, "fold", shape((head_size, 1, 128), F32), [vmem()])(arrived)
    pooled = jnp.sum(lax.all_to_all(pooled, "head", 0, 0, tiled=True), axis=(0, 1))[:doc_dev]
    return pooled / counts


def solution(mesh):
    return jax.shard_map(
        per_device,
        mesh=mesh,
        in_specs=(
            P("page", None),
            P(),
            P(None, "head"),
            P("page", None, "head"),
            P("page", None, "head"),
            P("page", None),
            P(None, "head"),
            P("head", None),
            P(),
            P(None, "head"),
            P(None, "head"),
            P("head", None),
            P(),
            P(),
            P(),
            P(),
            P(),
        ),
        out_specs=P("page"),
        check_vma=False,
    )
```

```python
import functools

import jax
import jax.numpy as jnp
from jax import lax
from jax.experimental import pallas as pl
from jax.experimental.pallas import tpu as pltpu
from jax.sharding import PartitionSpec as P

NQ = 8
DOCS = 256
MASKED = -1e30
BF = jnp.bfloat16
F32 = jnp.float32


def rms_scale(values, gain):
    values = values.astype(F32)
    return values * lax.rsqrt(jnp.mean(values * values, axis=-1, keepdims=True) + 1e-06) * gain


def split_three(value):
    first = value.astype(BF)
    rest = value - first.astype(F32)
    second = rest.astype(BF)
    third = (rest - second.astype(F32)).astype(BF)
    return first, second, third


def project_kernel(states, gain, weight, keys, values, buckets, out, payload, states_here, gain_here, weight_here,
                   buckets_here, arrivals):
    count = keys.shape[0]
    pairs = (
        (states, states_here),
        (gain, gain_here),
        (weight, weight_here),
        (buckets, buckets_here),
        (keys, payload.at[pl.ds(0, count)]),
        (values, payload.at[pl.ds(count + 8, count)]),
    )
    copies = [pltpu.make_async_copy(there, here, arrivals.at[i]) for i, (there, here) in enumerate(pairs)]
    for copy in copies:
        copy.start()
    copies[0].wait()
    copies[1].wait()
    normed = rms_scale(states_here[...], gain_here[...]).astype(BF)
    copies[3].wait()
    both = jnp.concatenate([buckets_here[0:1, :], buckets_here[1:2, :]], axis=1).astype(F32)
    payload[count : count + 8, :] = jnp.broadcast_to(both, (8, both.shape[1])).astype(BF)
    copies[2].wait()
    queries = jnp.dot(normed, weight_here[...], preferred_element_type=F32).astype(BF)
    for chip in range(out.shape[0]):
        out[chip] = queries
    copies[4].wait()
    copies[5].wait()


def near_kernel(rank, first, second, bias_table, page_table, query_lengths, doc_query, doc_rows, keys_aug, values_t,
                extra, table_here, slots_here, lengths_here, info, arrivals, query_here, rows_here, doc_arrivals, *, pages):
    copies = [
        pltpu.make_async_copy(doc_query, query_here, doc_arrivals.at[0]),
        pltpu.make_async_copy(doc_rows, rows_here, doc_arrivals.at[1]),
    ]
    for copy in copies:
        copy.start()

    def columns():
        for copy in copies:
            copy.wait()
        query_columns(rank, query_here, rows_here, extra)

    prepare_kernel(
        rank, first, second, None, bias_table, page_table, query_lengths, keys_aug, values_t, table_here, slots_here,
        lengths_here, info, arrivals, side=0, pages=pages, meanwhile=columns,
    )


def query_columns(rank, doc_query, doc_rows, extra):
    tokens = extra.shape[0]
    tok_dev = doc_rows.shape[1] // 2
    row_chips = 4
    core = rank[0] % 2
    chip = rank[0] // 2
    pair = chip - chip % 2
    doc_count = doc_query.shape[1]
    left = lax.broadcasted_iota(jnp.int32, (1, 128), 1) < tok_dev
    doc_id = lax.broadcasted_iota(jnp.int32, (doc_count, 128), 0)
    blocks = []
    for y in range(tokens // (2 * tok_dev)):
        two = doc_rows[pl.ds(y * row_chips + pair % row_chips, 2), :]
        turned = pltpu.roll(two, tok_dev, 1)
        row = jnp.where(
            left,
            jnp.where(core == 0, two[0:1], turned[0:1]),
            jnp.where(core == 0, turned[1:2], two[1:2]),
        )
        blocks.append((doc_id == row).astype(F32).astype(BF))
    member = jnp.concatenate(blocks, axis=1)
    asked = jnp.broadcast_to(doc_query[...].astype(F32), (128, doc_count)).astype(BF)
    tok_query = jnp.dot(asked, member, preferred_element_type=F32)
    mark = lax.broadcasted_iota(jnp.int32, (128, tokens), 0) % 64
    columns = jnp.where(
        mark < NQ,
        jnp.where(tok_query == mark.astype(F32), 0.0, MASKED),
        jnp.where(mark == NQ, MASKED, jnp.where(mark < NQ + 4, 1.0, 0.0)),
    )
    extra[...] = columns.T.astype(BF)


def prepare_kernel(rank, first, second, third, bias_table, page_table, query_lengths, keys_aug, values_t, table_here,
                   slots_here, lengths_here, info, arrivals, *, side, pages, meanwhile=None):
    width, total = values_t.shape
    page_len = total // (2 * pages)
    keys = pages * page_len
    heads, bucket_count = bias_table.shape
    depth = width // heads
    slot_count = page_table.shape[0]
    max_pages = slot_count // NQ
    row_chips = 4
    pairs = [(page_table, slots_here), (query_lengths, lengths_here), (bias_table, table_here)]
    copies = [pltpu.make_async_copy(there, here, arrivals.at[i]) for i, (there, here) in enumerate(pairs)]
    for copy in copies:
        copy.start()
    sources = ((first, keys + 8), (second, keys + 8) if third is None else (third, 0))
    for part, (value_rows, offset) in enumerate(sources):
        for page in range(pages):
            value = value_rows[offset + page * page_len : offset + (page + 1) * page_len, :]
            values_t[:, pl.ds((part * pages + page) * page_len, page_len)] = value.astype(F32).T.astype(BF)
    if meanwhile is not None:
        meanwhile()
    core = rank[0] % 2
    chip = rank[0] // 2
    base = (chip // row_chips * row_chips + chip % 2) * 2 * pages
    count = 4 * pages
    copies[0].wait()
    copies[1].wait()
    for s in range(slot_count):
        place = slots_here[s] - base
        near = (place >= 0) & (place < 2 * pages)
        far = (place >= 4 * pages) & (place < 6 * pages)
        place = jnp.where(near, place, jnp.where(far, place - 2 * pages, count))
        info[0, place] = s // max_pages
        info[1, place] = lengths_here[s // max_pages] - (s % max_pages) * page_len
    low = lax.broadcasted_iota(jnp.int32, (1, 128), 1) < depth
    col = lax.broadcasted_iota(jnp.int32, (bucket_count, 128), 1) % 64
    copies[2].wait()
    table = jnp.concatenate([table_here[...], jnp.zeros((8 - heads, bucket_count), F32)], axis=0).T
    spreads = []
    for h in range(heads):
        a, b, c = split_three(jnp.broadcast_to(table[:, h : h + 1], (bucket_count, 128)))
        last = jnp.where(col == NQ + 3, c.astype(F32), 0.0)
        spreads.append(
            jnp.where(col == NQ + 1, a.astype(F32), jnp.where(col == NQ + 2, b.astype(F32), last)).astype(BF)
        )
    spread = jnp.concatenate(spreads, axis=1)
    bucket_row = lax.broadcasted_iota(jnp.int32, (bucket_count, page_len), 0).astype(F32)
    slot = lax.broadcasted_iota(jnp.int32, (page_len, 128), 0)
    key_col = lax.broadcasted_iota(jnp.int32, (page_len, 128), 1) % 64
    mine = ((chip % row_chips // 2) * 2 + core) * pages
    for part, key_rows in enumerate((first, second)):
        for page in range(pages):
            place = (mine ^ ((2 * side + part) * pages)) + page
            span = pl.ds((part * pages + page) * page_len, page_len)
            bucket = key_rows[keys : keys + 8, page * page_len : (page + 1) * page_len].astype(F32)[0:1]
            onehot = (jnp.broadcast_to(bucket, bucket_row.shape) == bucket_row).astype(F32).astype(BF)
            bias = lax.dot_general(onehot, spread, (((0,), (0,)), ((), ())), preferred_element_type=F32)
            holder = jnp.where(slot < info[1, place], info[0, place], NQ)
            marks = (key_col == holder).astype(F32)
            key = key_rows[page * page_len : (page + 1) * page_len, :].astype(F32)
            for h in range(heads):
                keep = low if h % 2 == 0 else jnp.logical_not(low)
                half = key[:, (h // 2) * 128 : (h // 2 + 1) * 128]
                keys_aug[h, span, :] = jnp.where(keep, half, bias[:, h * 128 : (h + 1) * 128] + marks).astype(BF)


def attention_kernel(rank, queries, keys_near, keys_far, values_near, values_far, extra, states, out_weight, out, own, fetched,
                     rows_aug, arrivals):
    start = pl.multiple_of(rank[0] * own.shape[0], own.shape[0])
    copies = [
        pltpu.make_async_copy(out_weight, fetched, arrivals.at[0]),
        pltpu.make_async_copy(states.at[pl.ds(start, own.shape[0])], own, arrivals.at[1]),
    ]
    for copy in copies:
        copy.start()
    chips, tok_dev, width = queries.shape
    heads = keys_near.shape[0]
    depth = width // heads
    low = lax.broadcasted_iota(jnp.int32, (1, 128), 1) < depth
    left = lax.broadcasted_iota(jnp.int32, (1, 128), 1) < tok_dev
    rows = queries[...].reshape(chips * tok_dev, width)
    for h in range(heads):
        half = rows[:, (h // 2) * 128 : (h // 2 + 1) * 128].astype(F32)
        keep = low if h % 2 == 0 else jnp.logical_not(low)
        rows_aug[h] = jnp.where(keep, half, extra[...].astype(F32)).astype(BF)
    sums = []
    logs = []

    def score(h):
        return [
            lax.dot_general(keys[h], rows_aug[h], (((1,), (1,)), ((), ())), preferred_element_type=F32)
            for keys in (keys_near, keys_far)
        ]

    ready = score(0)
    for h in range(heads):
        span = slice(h * depth, (h + 1) * depth)
        scores = ready
        if h + 1 < heads:
            ready = score(h + 1)
        top = jnp.maximum(
            jnp.max(scores[0], axis=0, keepdims=True), jnp.max(scores[1], axis=0, keepdims=True)
        )
        total = jnp.zeros_like(top)
        summed = jnp.zeros((depth, chips * tok_dev), F32)
        for part, values in zip(scores, (values_near, values_far)):
            weights = jnp.exp(part - top)
            total += jnp.sum(weights, axis=0, keepdims=True)
            summed += jnp.dot(values[span, :], weights.astype(BF), preferred_element_type=F32)
        sums.append(summed / total)
        logs.append(top + jnp.log(total))
    for duo in range(chips // 2):
        lanes = slice(duo * 128, (duo + 1) * 128)
        pad = [jnp.zeros((6, 128), F32)]
        upper = jnp.concatenate([sums[0][:, lanes], sums[1][:, lanes]], axis=0)
        lower = jnp.concatenate([sums[2][:, lanes], sums[3][:, lanes]], axis=0)
        stat_upper = jnp.concatenate([logs[0][:, lanes], logs[1][:, lanes]] + pad, axis=0)
        stat_lower = jnp.concatenate([logs[2][:, lanes], logs[3][:, lanes]] + pad, axis=0)
        block = (
            jnp.where(left, upper, pltpu.roll(lower, tok_dev, 1)),
            jnp.where(left, pltpu.roll(upper, tok_dev, 1), lower),
        )
        stat = (
            jnp.where(left, stat_upper, pltpu.roll(stat_lower, tok_dev, 1)),
            jnp.where(left, pltpu.roll(stat_upper, tok_dev, 1), stat_lower),
        )
        for which in range(2):
            a, b, c = split_three(stat[which])
            packed = [a[0:2].astype(F32), b[0:2].astype(F32), c[0:2].astype(F32), jnp.zeros((2, 128), F32)]
            out[duo * 2 + which, 0:128, :] = block[which].astype(BF)
            out[duo * 2 + which, 128:136, :] = jnp.concatenate(packed, axis=0).astype(BF)
    for copy in copies:
        copy.wait()


def combine_kernel(parts, out_weight, out):
    chips = parts.shape[0]
    logs = []
    for chip in range(chips):
        stat = parts[chip, 128:136, :].astype(F32)
        logs.append(stat[0:2] + stat[2:4] + stat[4:6])
    top = logs[0]
    for chip in range(1, chips):
        top = jnp.maximum(top, logs[chip])
    scales = [jnp.exp(log - top) for log in logs]
    whole = scales[0]
    for chip in range(1, chips):
        whole = whole + scales[chip]
    sums = [jnp.zeros((64, 128), F32), jnp.zeros((64, 128), F32)]
    for chip in range(chips):
        share = scales[chip] / whole
        for r in range(2):
            sums[r] = sums[r] + share[r : r + 1] * parts[chip, r * 64 : (r + 1) * 64, :].astype(F32)
    joined = jnp.concatenate(sums, axis=0).T
    context = jnp.concatenate([joined[0:64], joined[64:128]], axis=1).astype(BF)
    out[...] = jnp.dot(context, out_weight[...], preferred_element_type=F32).astype(BF)


def norm_kernel(terms, states, gain, score_vector, out, score):
    hidden = states[...].astype(F32)
    for source in range(terms.shape[0]):
        hidden = hidden + terms[source].astype(F32)
    normed = rms_scale(hidden, gain[...]).astype(BF)
    for target in range(out.shape[0]):
        out[target] = normed
    score[...] = jnp.broadcast_to(jnp.sum(hidden * score_vector[...], axis=-1, keepdims=True), score.shape)


def down_kernel(weight, score_vector, gate_weight, out, fetched, weight_here, arrivals):
    copy = pltpu.make_async_copy(weight, weight_here, arrivals.at[0])
    fetch = pltpu.make_async_copy(gate_weight, fetched, arrivals.at[1])
    copy.start()
    fetch.start()
    pieces = [piece.astype(F32) for piece in split_three(score_vector[...])]
    rows = jnp.concatenate(pieces + [jnp.zeros((5, score_vector.shape[1]), F32)], axis=0).astype(BF)
    copy.wait()
    terms = lax.dot_general(rows, weight_here[...], (((1,), (1,)), ((), ())), preferred_element_type=F32)
    out[...] = terms[0:1] + terms[1:2] + terms[2:3]
    fetch.wait()


def feed_kernel(rows, gate_weight, up_weight, down_score, own_score, own_docs, out, up_here, arrivals):
    steps = up_here.shape[0]
    size = rows.shape[1] // steps
    copies = [
        pltpu.make_async_copy(up_weight.at[pl.ds(i * size, size)], up_here.at[i], arrivals.at[i]) for i in range(steps)
    ]
    for copy in copies:
        copy.start()
    docs = own_docs[...]
    doc_dev = DOCS // out.shape[0]
    lane = lax.broadcasted_iota(jnp.int32, (docs.shape[0], 128), 1)
    holder = (docs // doc_dev == lane).astype(F32).astype(BF)
    gate = jnp.dot(rows[...], gate_weight[...], preferred_element_type=F32)
    gate = jax.nn.gelu(gate, approximate=True)
    upper = jnp.zeros_like(gate)
    for i in range(steps):
        copies[i].wait()
        upper += jnp.dot(rows[:, i * size : (i + 1) * size], up_here[i], preferred_element_type=F32)
    middle = (gate * upper).astype(BF).astype(F32)
    tok_score = jnp.sum(middle * down_score[...], axis=-1, keepdims=True) + own_score[...]
    placed = jnp.where(docs % doc_dev == lane, tok_score, 0.0)
    pieces = jnp.concatenate([piece.astype(F32) for piece in split_three(placed)], axis=1).astype(BF)
    sums = lax.dot_general(holder, pieces, (((0,), (0,)), ((), ())), preferred_element_type=F32)[0 : out.shape[0]]
    out[...] = sums[:, 0:128] + sums[:, 128:256] + sums[:, 256:384]


def fold_kernel(terms, out):
    out[...] = jnp.broadcast_to(jnp.sum(terms[...], axis=0, keepdims=True), out.shape)


def vmem():
    return pl.BlockSpec(memory_space=pltpu.VMEM)


def smem():
    return pl.BlockSpec(memory_space=pltpu.SMEM)


def in_hbm(value):
    return pltpu.with_memory_space_constraint(value, pltpu.HBM)


def hbm():
    return pl.BlockSpec(memory_space=pltpu.HBM)


def anywhere():
    return pl.BlockSpec(memory_space=pl.ANY)


def call(kernel, name, shapes, specs, scratch=()):
    single = not isinstance(shapes, (list, tuple))
    return pl.pallas_call(
        kernel,
        out_shape=shapes,
        in_specs=specs,
        out_specs=vmem() if single else [vmem()] * len(shapes),
        scratch_shapes=list(scratch),
        compiler_params=pltpu.CompilerParams(vmem_limit_bytes=40 << 20),
        name=name,
    )


def per_device(
    doc_states,
    gain_attn,
    query_weight,
    cache_keys,
    cache_values,
    rel_bucket,
    bias_table,
    out_weight,
    gain_ffn,
    wi_gate,
    wi_up,
    wo_ffn,
    score_vector,
    query_lengths,
    doc_query,
    doc_of_token,
    page_table,
):
    shape = jax.ShapeDtypeStruct
    tok_dev, model = doc_states.shape
    local_pages, page_len, local_width = cache_keys.shape
    local_heads = bias_table.shape[1]
    page_size = lax.axis_size("page")
    head_size = lax.axis_size("head")
    page_rank = lax.axis_index("page")
    head_rank = lax.axis_index("head")
    group = page_size // 4
    groups = [
        [y * 8 + (x + side) * 2 + core for y in range(4) for side in range(2)] for x in (0, 2) for core in range(2)
    ]
    core_swap = [(i, i ^ 1) for i in range(page_size)]
    side_swap = [(i, i ^ 4) for i in range(page_size)]

    def swap(value, pairs):
        return lax.ppermute(value, "page", pairs)

    keys_held = local_pages * page_len
    copies, payload = call(
        project_kernel,
        "project",
        [shape((group, tok_dev, local_width), BF), shape((2 * keys_held + 8, local_width), BF)],
        [hbm()] * 6,
        [
            pltpu.VMEM((tok_dev, model), BF),
            pltpu.VMEM((1, model), F32),
            pltpu.VMEM((model, local_width), BF),
            pltpu.VMEM((local_pages, page_len), jnp.int32),
            pltpu.SemaphoreType.DMA((6,)),
        ],
    )(
        in_hbm(doc_states),
        in_hbm(gain_attn.reshape(1, model)),
        in_hbm(query_weight),
        in_hbm(cache_keys.reshape(keys_held, local_width)),
        in_hbm(cache_values.reshape(keys_held, local_width)),
        in_hbm(rel_bucket),
    )
    payload_side = swap(payload, side_swap)
    payload_core = swap(payload, core_swap)
    keys_far = swap(payload_side[0 : keys_held + 8], core_swap)
    values_far = swap(payload_side[keys_held + 8 :], core_swap)
    gathered = lax.all_to_all(copies, "page", 0, 0, axis_index_groups=groups, tiled=True)

    rank = page_rank.reshape(1)
    doc_rows = doc_of_token.reshape(-1, 2 * tok_dev)
    key_count = 2 * local_pages * page_len

    shapes = [shape((local_heads, key_count, 128), BF), shape((local_width, key_count), BF)]
    scratch = [
        pltpu.VMEM(bias_table.T.shape, F32),
        pltpu.SMEM(page_table.shape, jnp.int32),
        pltpu.SMEM(query_lengths.shape, jnp.int32),
        pltpu.SMEM((2, 4 * local_pages + 1), jnp.int32),
        pltpu.SemaphoreType.DMA((3,)),
    ]
    tables = (in_hbm(bias_table.T), in_hbm(page_table), in_hbm(query_lengths))
    keys_near, values_near, extra = call(
        functools.partial(near_kernel, pages=local_pages),
        "near",
        shapes + [shape((group * tok_dev, 128), BF)],
        [smem()] + [vmem()] * 2 + [hbm()] * 5,
        scratch
        + [
            pltpu.VMEM((1, doc_query.shape[0]), jnp.int32),
            pltpu.VMEM(doc_rows.shape, jnp.int32),
            pltpu.SemaphoreType.DMA((2,)),
        ],
    )(rank, payload, payload_core, *tables, in_hbm(doc_query.reshape(1, -1)), in_hbm(doc_rows))
    keys_away, values_away = call(
        functools.partial(prepare_kernel, side=1, pages=local_pages),
        "away",
        shapes,
        [smem()] + [vmem()] * 3 + [hbm()] * 3,
        scratch,
    )(rank, payload_side, keys_far, values_far, *tables)
    own = tok_dev // head_size
    partials, own_states, fetched = call(
        attention_kernel,
        "attention",
        [shape((group, 136, 128), BF), shape((own, model), BF), shape(out_weight.shape, BF)],
        [smem()] + [vmem()] * 6 + [hbm()] * 2,
        [pltpu.VMEM((local_heads, group * tok_dev, 128), BF), pltpu.SemaphoreType.DMA((2,))],
    )(
        head_rank.reshape(1), gathered, keys_near, keys_away, values_near, values_away, extra,
        in_hbm(doc_states), in_hbm(out_weight),
    )
    hidden_units = wi_gate.shape[1]
    returned = lax.all_to_all(partials, "page", 0, 0, axis_index_groups=groups, tiled=True)
    projected = call(combine_kernel, "combine", shape((tok_dev, model), BF), [vmem()] * 2)(returned, fetched)

    doc_dev = doc_query.shape[0] // page_size
    terms = lax.all_to_all(projected.reshape(head_size, own, model), "head", 0, 0, tiled=True)
    spread, hidden_score = call(
        norm_kernel,
        "norm",
        [shape((head_size, own, model), BF), shape((own, 128), F32)],
        [vmem()] * 4,
    )(terms, own_states, gain_ffn.reshape(1, model), score_vector.reshape(1, model))
    spread, late_gate, down_weight, late_docs, late_rank = lax.optimization_barrier(
        (spread, wi_gate, wo_ffn, doc_of_token, page_rank)
    )
    down_score, gate_here = call(
        down_kernel,
        "down",
        [shape((1, hidden_units), F32), shape(wi_gate.shape, BF)],
        [hbm(), vmem(), hbm()],
        [pltpu.VMEM(wo_ffn.shape, BF), pltpu.SemaphoreType.DMA((2,))],
    )(in_hbm(down_weight), score_vector.reshape(1, model), in_hbm(late_gate))
    mine_docs = late_rank * doc_dev + jnp.arange(doc_dev, dtype=jnp.int32)
    counts = jnp.sum((late_docs[:, None] == mine_docs[None, :]).astype(F32), axis=0)
    rows = lax.all_to_all(spread, "head", 0, 0, tiled=True).reshape(tok_dev, model)
    rows, counts = lax.optimization_barrier((rows, counts))
    token = jnp.arange(tok_dev, dtype=jnp.int32)[:, None]
    own_score = jnp.where(token // own == head_rank, jnp.tile(hidden_score[:, :1], (head_size, 1)), 0.0)
    own_docs = lax.dynamic_slice_in_dim(late_docs, page_rank * tok_dev, tok_dev, 0)[:, None]
    steps = 4
    doc_sums = call(
        feed_kernel, "feed", shape((page_size, 128), F32), [vmem(), vmem(), hbm(), vmem(), vmem(), vmem()],
        [pltpu.VMEM((steps, model // steps, hidden_units), BF), pltpu.SemaphoreType.DMA((steps,))],
    )(rows, gate_here, in_hbm(wi_up), down_score, own_score, own_docs)
    doc_sums = doc_sums.reshape(page_size, 1, 128)
    arrived = lax.all_to_all(doc_sums, "page", 0, 0, tiled=True)
    pooled = call(fold_kernel, "fold", shape((head_size, 1, 128), F32), [vmem()])(arrived)
    pooled = jnp.sum(lax.all_to_all(pooled, "head", 0, 0, tiled=True), axis=(0, 1))[:doc_dev]
    return pooled / counts


def solution(mesh):
    return jax.shard_map(
        per_device,
        mesh=mesh,
        in_specs=(
            P("page", None),
            P(),
            P(None, "head"),
            P("page", None, "head"),
            P("page", None, "head"),
            P("page", None),
            P(None, "head"),
            P("head", None),
            P(),
            P(None, "head"),
            P(None, "head"),
            P("head", None),
            P(),
            P(),
            P(),
            P(),
            P(),
        ),
        out_specs=P("page"),
        check_vma=False,
    )
```

```python
import functools

import jax
import jax.numpy as jnp
from jax import lax
from jax.experimental import pallas as pl
from jax.experimental.pallas import tpu as pltpu
from jax.sharding import PartitionSpec as P

NQ = 8
DOCS = 256
MASKED = -1e30
BF = jnp.bfloat16
F32 = jnp.float32


def rms_scale(values, gain):
    values = values.astype(F32)
    return values * lax.rsqrt(jnp.mean(values * values, axis=-1, keepdims=True) + 1e-06) * gain


def split_three(value):
    first = value.astype(BF)
    rest = value - first.astype(F32)
    second = rest.astype(BF)
    third = (rest - second.astype(F32)).astype(BF)
    return first, second, third


def project_kernel(states, gain, weight, keys, values, buckets, out, payload, states_here, gain_here, weight_here,
                   buckets_here, arrivals):
    count = keys.shape[0]
    pairs = (
        (states, states_here),
        (gain, gain_here),
        (weight, weight_here),
        (buckets, buckets_here),
        (keys, payload.at[pl.ds(0, count)]),
        (values, payload.at[pl.ds(count + 8, count)]),
    )
    copies = [pltpu.make_async_copy(there, here, arrivals.at[i]) for i, (there, here) in enumerate(pairs)]
    for copy in copies:
        copy.start()
    copies[0].wait()
    copies[1].wait()
    normed = rms_scale(states_here[...], gain_here[...]).astype(BF)
    copies[3].wait()
    both = jnp.concatenate([buckets_here[0:1, :], buckets_here[1:2, :]], axis=1).astype(F32)
    payload[count : count + 8, :] = jnp.broadcast_to(both, (8, both.shape[1])).astype(BF)
    copies[2].wait()
    queries = jnp.dot(normed, weight_here[...], preferred_element_type=F32).astype(BF)
    for chip in range(out.shape[0]):
        out[chip] = queries
    copies[4].wait()
    copies[5].wait()


def near_kernel(rank, first, second, bias_table, page_table, query_lengths, doc_query, doc_rows, keys_aug, values_t,
                extra, table_here, slots_here, lengths_here, info, arrivals, query_here, rows_here, doc_arrivals, *, pages):
    copies = [
        pltpu.make_async_copy(doc_query, query_here, doc_arrivals.at[0]),
        pltpu.make_async_copy(doc_rows, rows_here, doc_arrivals.at[1]),
    ]
    for copy in copies:
        copy.start()

    def columns():
        for copy in copies:
            copy.wait()
        query_columns(rank, query_here, rows_here, extra)

    prepare_kernel(
        rank, first, second, None, bias_table, page_table, query_lengths, keys_aug, values_t, table_here, slots_here,
        lengths_here, info, arrivals, side=0, pages=pages, meanwhile=columns,
    )


def query_columns(rank, doc_query, doc_rows, extra):
    tokens = extra.shape[0]
    tok_dev = doc_rows.shape[1] // 2
    row_chips = 4
    core = rank[0] % 2
    chip = rank[0] // 2
    pair = chip - chip % 2
    doc_count = doc_query.shape[1]
    left = lax.broadcasted_iota(jnp.int32, (1, 128), 1) < tok_dev
    doc_id = lax.broadcasted_iota(jnp.int32, (doc_count, 128), 0)
    blocks = []
    for y in range(tokens // (2 * tok_dev)):
        two = doc_rows[pl.ds(y * row_chips + pair % row_chips, 2), :]
        turned = pltpu.roll(two, tok_dev, 1)
        row = jnp.where(
            left,
            jnp.where(core == 0, two[0:1], turned[0:1]),
            jnp.where(core == 0, turned[1:2], two[1:2]),
        )
        blocks.append((doc_id == row).astype(F32).astype(BF))
    member = jnp.concatenate(blocks, axis=1)
    asked = jnp.broadcast_to(doc_query[...].astype(F32), (128, doc_count)).astype(BF)
    tok_query = jnp.dot(asked, member, preferred_element_type=F32)
    mark = lax.broadcasted_iota(jnp.int32, (128, tokens), 0) % 64
    columns = jnp.where(
        mark < NQ,
        jnp.where(tok_query == mark.astype(F32), 0.0, MASKED),
        jnp.where(mark == NQ, MASKED, jnp.where(mark < NQ + 4, 1.0, 0.0)),
    )
    extra[...] = columns.T.astype(BF)


def prepare_kernel(rank, first, second, third, bias_table, page_table, query_lengths, keys_aug, values_t, table_here,
                   slots_here, lengths_here, info, arrivals, *, side, pages, meanwhile=None):
    width, total = values_t.shape
    page_len = total // (2 * pages)
    keys = pages * page_len
    heads, bucket_count = bias_table.shape
    depth = width // heads
    slot_count = page_table.shape[0]
    max_pages = slot_count // NQ
    row_chips = 4
    pairs = [(page_table, slots_here), (query_lengths, lengths_here), (bias_table, table_here)]
    copies = [pltpu.make_async_copy(there, here, arrivals.at[i]) for i, (there, here) in enumerate(pairs)]
    for copy in copies:
        copy.start()
    sources = ((first, keys + 8), (second, keys + 8) if third is None else (third, 0))
    for part, (value_rows, offset) in enumerate(sources):
        for page in range(pages):
            value = value_rows[offset + page * page_len : offset + (page + 1) * page_len, :]
            values_t[:, pl.ds((part * pages + page) * page_len, page_len)] = value.astype(F32).T.astype(BF)
    if meanwhile is not None:
        meanwhile()
    core = rank[0] % 2
    chip = rank[0] // 2
    base = (chip // row_chips * row_chips + chip % 2) * 2 * pages
    count = 4 * pages
    copies[0].wait()
    copies[1].wait()
    for s in range(slot_count):
        place = slots_here[s] - base
        near = (place >= 0) & (place < 2 * pages)
        far = (place >= 4 * pages) & (place < 6 * pages)
        place = jnp.where(near, place, jnp.where(far, place - 2 * pages, count))
        info[0, place] = s // max_pages
        info[1, place] = lengths_here[s // max_pages] - (s % max_pages) * page_len
    low = lax.broadcasted_iota(jnp.int32, (1, 128), 1) < depth
    col = lax.broadcasted_iota(jnp.int32, (bucket_count, 128), 1) % 64
    copies[2].wait()
    table = jnp.concatenate([table_here[...], jnp.zeros((8 - heads, bucket_count), F32)], axis=0).T
    spreads = []
    for h in range(heads):
        a, b, c = split_three(jnp.broadcast_to(table[:, h : h + 1], (bucket_count, 128)))
        last = jnp.where(col == NQ + 3, c.astype(F32), 0.0)
        spreads.append(
            jnp.where(col == NQ + 1, a.astype(F32), jnp.where(col == NQ + 2, b.astype(F32), last)).astype(BF)
        )
    spread = jnp.concatenate(spreads, axis=1)
    bucket_row = lax.broadcasted_iota(jnp.int32, (bucket_count, page_len), 0).astype(F32)
    slot = lax.broadcasted_iota(jnp.int32, (page_len, 128), 0)
    key_col = lax.broadcasted_iota(jnp.int32, (page_len, 128), 1) % 64
    mine = ((chip % row_chips // 2) * 2 + core) * pages
    for part, key_rows in enumerate((first, second)):
        for page in range(pages):
            place = (mine ^ ((2 * side + part) * pages)) + page
            span = pl.ds((part * pages + page) * page_len, page_len)
            bucket = key_rows[keys : keys + 8, page * page_len : (page + 1) * page_len].astype(F32)[0:1]
            onehot = (jnp.broadcast_to(bucket, bucket_row.shape) == bucket_row).astype(F32).astype(BF)
            bias = lax.dot_general(onehot, spread, (((0,), (0,)), ((), ())), preferred_element_type=F32)
            holder = jnp.where(slot < info[1, place], info[0, place], NQ)
            marks = (key_col == holder).astype(F32)
            key = key_rows[page * page_len : (page + 1) * page_len, :].astype(F32)
            for h in range(heads):
                keep = low if h % 2 == 0 else jnp.logical_not(low)
                half = key[:, (h // 2) * 128 : (h // 2 + 1) * 128]
                keys_aug[h, span, :] = jnp.where(keep, half, bias[:, h * 128 : (h + 1) * 128] + marks).astype(BF)


def attention_kernel(rank, queries, keys_near, keys_far, values_near, values_far, extra, states, out_weight, out, own, fetched,
                     rows_aug, arrivals):
    start = pl.multiple_of(rank[0] * own.shape[0], own.shape[0])
    copies = [
        pltpu.make_async_copy(out_weight, fetched, arrivals.at[0]),
        pltpu.make_async_copy(states.at[pl.ds(start, own.shape[0])], own, arrivals.at[1]),
    ]
    for copy in copies:
        copy.start()
    chips, tok_dev, width = queries.shape
    heads = keys_near.shape[0]
    depth = width // heads
    low = lax.broadcasted_iota(jnp.int32, (1, 128), 1) < depth
    left = lax.broadcasted_iota(jnp.int32, (1, 128), 1) < tok_dev
    rows = queries[...].reshape(chips * tok_dev, width)
    for h in range(heads):
        half = rows[:, (h // 2) * 128 : (h // 2 + 1) * 128].astype(F32)
        keep = low if h % 2 == 0 else jnp.logical_not(low)
        rows_aug[h] = jnp.where(keep, half, extra[...].astype(F32)).astype(BF)
    sums = []
    logs = []

    def score(h):
        return [
            lax.dot_general(keys[h], rows_aug[h], (((1,), (1,)), ((), ())), preferred_element_type=F32)
            for keys in (keys_near, keys_far)
        ]

    ready = score(0)
    for h in range(heads):
        span = slice(h * depth, (h + 1) * depth)
        scores = ready
        if h + 1 < heads:
            ready = score(h + 1)
        top = jnp.maximum(
            jnp.max(scores[0], axis=0, keepdims=True), jnp.max(scores[1], axis=0, keepdims=True)
        )
        total = jnp.zeros_like(top)
        summed = jnp.zeros((depth, chips * tok_dev), F32)
        for part, values in zip(scores, (values_near, values_far)):
            weights = jnp.exp(part - top)
            total += jnp.sum(weights, axis=0, keepdims=True)
            summed += jnp.dot(values[span, :], weights.astype(BF), preferred_element_type=F32)
        sums.append(summed / total)
        logs.append(top + jnp.log(total))
    for duo in range(chips // 2):
        lanes = slice(duo * 128, (duo + 1) * 128)
        pad = [jnp.zeros((6, 128), F32)]
        upper = jnp.concatenate([sums[0][:, lanes], sums[1][:, lanes]], axis=0)
        lower = jnp.concatenate([sums[2][:, lanes], sums[3][:, lanes]], axis=0)
        stat_upper = jnp.concatenate([logs[0][:, lanes], logs[1][:, lanes]] + pad, axis=0)
        stat_lower = jnp.concatenate([logs[2][:, lanes], logs[3][:, lanes]] + pad, axis=0)
        block = (
            jnp.where(left, upper, pltpu.roll(lower, tok_dev, 1)),
            jnp.where(left, pltpu.roll(upper, tok_dev, 1), lower),
        )
        stat = (
            jnp.where(left, stat_upper, pltpu.roll(stat_lower, tok_dev, 1)),
            jnp.where(left, pltpu.roll(stat_upper, tok_dev, 1), stat_lower),
        )
        for which in range(2):
            a, b, c = split_three(stat[which])
            packed = [a[0:2].astype(F32), b[0:2].astype(F32), c[0:2].astype(F32), jnp.zeros((2, 128), F32)]
            out[duo * 2 + which, 0:128, :] = block[which].astype(BF)
            out[duo * 2 + which, 128:136, :] = jnp.concatenate(packed, axis=0).astype(BF)
    for copy in copies:
        copy.wait()


def combine_kernel(parts, out_weight, out):
    chips = parts.shape[0]
    logs = []
    for chip in range(chips):
        stat = parts[chip, 128:136, :].astype(F32)
        logs.append(stat[0:2] + stat[2:4] + stat[4:6])
    top = logs[0]
    for chip in range(1, chips):
        top = jnp.maximum(top, logs[chip])
    scales = [jnp.exp(log - top) for log in logs]
    whole = scales[0]
    for chip in range(1, chips):
        whole = whole + scales[chip]
    sums = [jnp.zeros((64, 128), F32), jnp.zeros((64, 128), F32)]
    for chip in range(chips):
        share = scales[chip] / whole
        for r in range(2):
            sums[r] = sums[r] + share[r : r + 1] * parts[chip, r * 64 : (r + 1) * 64, :].astype(F32)
    joined = jnp.concatenate(sums, axis=0).T
    context = jnp.concatenate([joined[0:64], joined[64:128]], axis=1).astype(BF)
    out[...] = jnp.dot(context, out_weight[...], preferred_element_type=F32).astype(BF)


def norm_kernel(terms, states, gain, score_vector, out, score):
    hidden = states[...].astype(F32)
    for source in range(terms.shape[0]):
        hidden = hidden + terms[source].astype(F32)
    normed = rms_scale(hidden, gain[...]).astype(BF)
    for target in range(out.shape[0]):
        out[target] = normed
    score[...] = jnp.broadcast_to(jnp.sum(hidden * score_vector[...], axis=-1, keepdims=True), score.shape)


def down_kernel(weight, score_vector, gate_weight, out, fetched, weight_here, arrivals):
    copy = pltpu.make_async_copy(weight, weight_here, arrivals.at[0])
    fetch = pltpu.make_async_copy(gate_weight, fetched, arrivals.at[1])
    copy.start()
    fetch.start()
    pieces = [piece.astype(F32) for piece in split_three(score_vector[...])]
    rows = jnp.concatenate(pieces + [jnp.zeros((5, score_vector.shape[1]), F32)], axis=0).astype(BF)
    copy.wait()
    terms = lax.dot_general(rows, weight_here[...], (((1,), (1,)), ((), ())), preferred_element_type=F32)
    out[...] = terms[0:1] + terms[1:2] + terms[2:3]
    fetch.wait()


def feed_kernel(rows, gate_weight, up_weight, down_score, own_score, own_docs, out, up_here, arrivals):
    steps = up_here.shape[0]
    size = rows.shape[1] // steps
    copies = [
        pltpu.make_async_copy(up_weight.at[pl.ds(i * size, size)], up_here.at[i], arrivals.at[i]) for i in range(steps)
    ]
    for copy in copies:
        copy.start()
    docs = own_docs[...]
    doc_dev = DOCS // out.shape[0]
    lane = lax.broadcasted_iota(jnp.int32, (docs.shape[0], 128), 1)
    holder = (docs // doc_dev == lane).astype(F32).astype(BF)
    gate = jnp.dot(rows[...], gate_weight[...], preferred_element_type=F32)
    gate = jax.nn.gelu(gate, approximate=True)
    upper = jnp.zeros_like(gate)
    for i in range(steps):
        copies[i].wait()
        upper += jnp.dot(rows[:, i * size : (i + 1) * size], up_here[i], preferred_element_type=F32)
    middle = (gate * upper).astype(BF).astype(F32)
    tok_score = jnp.sum(middle * down_score[...], axis=-1, keepdims=True) + own_score[...]
    placed = jnp.where(docs % doc_dev == lane, tok_score, 0.0)
    pieces = jnp.concatenate([piece.astype(F32) for piece in split_three(placed)], axis=1).astype(BF)
    sums = lax.dot_general(holder, pieces, (((0,), (0,)), ((), ())), preferred_element_type=F32)[0 : out.shape[0]]
    out[...] = sums[:, 0:128] + sums[:, 128:256] + sums[:, 256:384]


def fold_kernel(terms, out):
    out[...] = jnp.broadcast_to(jnp.sum(terms[...], axis=0, keepdims=True), out.shape)


def vmem():
    return pl.BlockSpec(memory_space=pltpu.VMEM)


def smem():
    return pl.BlockSpec(memory_space=pltpu.SMEM)


def in_hbm(value):
    return pltpu.with_memory_space_constraint(value, pltpu.HBM)


def hbm():
    return pl.BlockSpec(memory_space=pltpu.HBM)


def anywhere():
    return pl.BlockSpec(memory_space=pl.ANY)


def call(kernel, name, shapes, specs, scratch=()):
    single = not isinstance(shapes, (list, tuple))
    return pl.pallas_call(
        kernel,
        out_shape=shapes,
        in_specs=specs,
        out_specs=vmem() if single else [vmem()] * len(shapes),
        scratch_shapes=list(scratch),
        compiler_params=pltpu.CompilerParams(vmem_limit_bytes=40 << 20),
        name=name,
    )


def per_device(
    doc_states,
    gain_attn,
    query_weight,
    cache_keys,
    cache_values,
    rel_bucket,
    bias_table,
    out_weight,
    gain_ffn,
    wi_gate,
    wi_up,
    wo_ffn,
    score_vector,
    query_lengths,
    doc_query,
    doc_of_token,
    page_table,
):
    shape = jax.ShapeDtypeStruct
    tok_dev, model = doc_states.shape
    local_pages, page_len, local_width = cache_keys.shape
    local_heads = bias_table.shape[1]
    page_size = lax.axis_size("page")
    head_size = lax.axis_size("head")
    page_rank = lax.axis_index("page")
    head_rank = lax.axis_index("head")
    group = page_size // 4
    groups = [
        [y * 8 + (x + side) * 2 + core for y in range(4) for side in range(2)] for x in (0, 2) for core in range(2)
    ]
    core_swap = [(i, i ^ 1) for i in range(page_size)]
    side_swap = [(i, i ^ 4) for i in range(page_size)]

    def swap(value, pairs):
        return lax.ppermute(value, "page", pairs)

    keys_held = local_pages * page_len
    copies, payload = call(
        project_kernel,
        "project",
        [shape((group, tok_dev, local_width), BF), shape((2 * keys_held + 8, local_width), BF)],
        [hbm()] * 6,
        [
            pltpu.VMEM((tok_dev, model), BF),
            pltpu.VMEM((1, model), F32),
            pltpu.VMEM((model, local_width), BF),
            pltpu.VMEM((local_pages, page_len), jnp.int32),
            pltpu.SemaphoreType.DMA((6,)),
        ],
    )(
        in_hbm(doc_states),
        in_hbm(gain_attn.reshape(1, model)),
        in_hbm(query_weight),
        in_hbm(cache_keys.reshape(keys_held, local_width)),
        in_hbm(cache_values.reshape(keys_held, local_width)),
        in_hbm(rel_bucket),
    )
    payload_side = swap(payload, side_swap)
    payload_core = swap(payload, core_swap)
    keys_far = swap(payload_side[0 : keys_held + 8], core_swap)
    values_far = swap(payload_side[keys_held + 8 :], core_swap)
    gathered = lax.all_to_all(copies, "page", 0, 0, axis_index_groups=groups, tiled=True)

    rank = page_rank.reshape(1)
    doc_rows = doc_of_token.reshape(-1, 2 * tok_dev)
    key_count = 2 * local_pages * page_len

    shapes = [shape((local_heads, key_count, 128), BF), shape((local_width, key_count), BF)]
    scratch = [
        pltpu.VMEM(bias_table.T.shape, F32),
        pltpu.SMEM(page_table.shape, jnp.int32),
        pltpu.SMEM(query_lengths.shape, jnp.int32),
        pltpu.SMEM((2, 4 * local_pages + 1), jnp.int32),
        pltpu.SemaphoreType.DMA((3,)),
    ]
    tables = (in_hbm(bias_table.T), in_hbm(page_table), in_hbm(query_lengths))
    keys_near, values_near, extra = call(
        functools.partial(near_kernel, pages=local_pages),
        "near",
        shapes + [shape((group * tok_dev, 128), BF)],
        [smem()] + [vmem()] * 2 + [hbm()] * 5,
        scratch
        + [
            pltpu.VMEM((1, doc_query.shape[0]), jnp.int32),
            pltpu.VMEM(doc_rows.shape, jnp.int32),
            pltpu.SemaphoreType.DMA((2,)),
        ],
    )(rank, payload, payload_core, *tables, in_hbm(doc_query.reshape(1, -1)), in_hbm(doc_rows))
    keys_away, values_away = call(
        functools.partial(prepare_kernel, side=1, pages=local_pages),
        "away",
        shapes,
        [smem()] + [vmem()] * 3 + [hbm()] * 3,
        scratch,
    )(rank, payload_side, keys_far, values_far, *tables)
    own = tok_dev // head_size
    partials, own_states, fetched = call(
        attention_kernel,
        "attention",
        [shape((group, 136, 128), BF), shape((own, model), BF), shape(out_weight.shape, BF)],
        [smem()] + [vmem()] * 6 + [hbm()] * 2,
        [pltpu.VMEM((local_heads, group * tok_dev, 128), BF), pltpu.SemaphoreType.DMA((2,))],
    )(
        head_rank.reshape(1), gathered, keys_near, keys_away, values_near, values_away, extra,
        in_hbm(doc_states), in_hbm(out_weight),
    )
    hidden_units = wi_gate.shape[1]
    returned = lax.all_to_all(partials, "page", 0, 0, axis_index_groups=groups, tiled=True)
    projected = call(combine_kernel, "combine", shape((tok_dev, model), BF), [vmem()] * 2)(returned, fetched)

    doc_dev = doc_query.shape[0] // page_size
    terms = lax.all_to_all(projected.reshape(head_size, own, model), "head", 0, 0, tiled=True)
    spread, hidden_score = call(
        norm_kernel,
        "norm",
        [shape((head_size, own, model), BF), shape((own, 128), F32)],
        [vmem()] * 4,
    )(terms, own_states, gain_ffn.reshape(1, model), score_vector.reshape(1, model))
    spread, late_gate, down_weight, late_docs, late_rank = lax.optimization_barrier(
        (spread, wi_gate, wo_ffn, doc_of_token, page_rank)
    )
    down_score, gate_here = call(
        down_kernel,
        "down",
        [shape((1, hidden_units), F32), shape(wi_gate.shape, BF)],
        [hbm(), vmem(), hbm()],
        [pltpu.VMEM(wo_ffn.shape, BF), pltpu.SemaphoreType.DMA((2,))],
    )(in_hbm(down_weight), score_vector.reshape(1, model), in_hbm(late_gate))
    mine_docs = late_rank * doc_dev + jnp.arange(doc_dev, dtype=jnp.int32)
    counts = jnp.sum((late_docs[:, None] == mine_docs[None, :]).astype(F32), axis=0)
    rows = lax.all_to_all(spread, "head", 0, 0, tiled=True).reshape(tok_dev, model)
    rows, counts = lax.optimization_barrier((rows, counts))
    token = jnp.arange(tok_dev, dtype=jnp.int32)[:, None]
    own_score = jnp.where(token // own == head_rank, jnp.tile(hidden_score[:, :1], (head_size, 1)), 0.0)
    own_docs = lax.dynamic_slice_in_dim(late_docs, late_rank * tok_dev, tok_dev, 0)[:, None]
    steps = 4
    doc_sums = call(
        feed_kernel, "feed", shape((page_size, 128), F32), [vmem(), vmem(), hbm(), vmem(), vmem(), vmem()],
        [pltpu.VMEM((steps, model // steps, hidden_units), BF), pltpu.SemaphoreType.DMA((steps,))],
    )(rows, gate_here, in_hbm(wi_up), down_score, own_score, own_docs)
    doc_sums = doc_sums.reshape(page_size, 1, 128)
    arrived = lax.all_to_all(doc_sums, "page", 0, 0, tiled=True)
    pooled = call(fold_kernel, "fold", shape((head_size, 1, 128), F32), [vmem()])(arrived)
    pooled = jnp.sum(lax.all_to_all(pooled, "head", 0, 0, tiled=True), axis=(0, 1))[:doc_dev]
    return pooled / counts


def solution(mesh):
    return jax.shard_map(
        per_device,
        mesh=mesh,
        in_specs=(
            P("page", None),
            P(),
            P(None, "head"),
            P("page", None, "head"),
            P("page", None, "head"),
            P("page", None),
            P(None, "head"),
            P("head", None),
            P(),
            P(None, "head"),
            P(None, "head"),
            P("head", None),
            P(),
            P(),
            P(),
            P(),
            P(),
        ),
        out_specs=P("page"),
        check_vma=False,
    )
```

```python
import functools

import jax
import jax.numpy as jnp
from jax import lax
from jax.experimental import pallas as pl
from jax.experimental.pallas import tpu as pltpu
from jax.sharding import PartitionSpec as P

NQ = 8
DOCS = 256
MASKED = -1e30
BF = jnp.bfloat16
F32 = jnp.float32


def rms_scale(values, gain):
    values = values.astype(F32)
    return values * lax.rsqrt(jnp.mean(values * values, axis=-1, keepdims=True) + 1e-06) * gain


def split_three(value):
    first = value.astype(BF)
    rest = value - first.astype(F32)
    second = rest.astype(BF)
    third = (rest - second.astype(F32)).astype(BF)
    return first, second, third


def project_kernel(states, gain, weight, keys, values, buckets, out, payload, states_here, gain_here, weight_here,
                   buckets_here, arrivals):
    count = keys.shape[0]
    pairs = (
        (states, states_here),
        (gain, gain_here),
        (weight, weight_here),
        (buckets, buckets_here),
        (keys, payload.at[pl.ds(0, count)]),
        (values, payload.at[pl.ds(count + 8, count)]),
    )
    copies = [pltpu.make_async_copy(there, here, arrivals.at[i]) for i, (there, here) in enumerate(pairs)]
    for copy in copies:
        copy.start()
    copies[0].wait()
    copies[1].wait()
    normed = rms_scale(states_here[...], gain_here[...]).astype(BF)
    copies[3].wait()
    both = jnp.concatenate([buckets_here[0:1, :], buckets_here[1:2, :]], axis=1).astype(F32)
    payload[count : count + 8, :] = jnp.broadcast_to(both, (8, both.shape[1])).astype(BF)
    copies[2].wait()
    queries = jnp.dot(normed, weight_here[...], preferred_element_type=F32).astype(BF)
    for chip in range(out.shape[0]):
        out[chip] = queries
    copies[4].wait()
    copies[5].wait()


def near_kernel(rank, first, second, bias_table, page_table, query_lengths, doc_query, doc_rows, keys_aug, values_t,
                extra, table_here, slots_here, lengths_here, info, arrivals, query_here, rows_here, doc_arrivals, *, pages):
    copies = [
        pltpu.make_async_copy(doc_query, query_here, doc_arrivals.at[0]),
        pltpu.make_async_copy(doc_rows, rows_here, doc_arrivals.at[1]),
    ]
    for copy in copies:
        copy.start()

    def columns():
        for copy in copies:
            copy.wait()
        query_columns(rank, query_here, rows_here, extra)

    prepare_kernel(
        rank, first, second, None, bias_table, page_table, query_lengths, keys_aug, values_t, table_here, slots_here,
        lengths_here, info, arrivals, side=0, pages=pages, meanwhile=columns,
    )


def query_columns(rank, doc_query, doc_rows, extra):
    tokens = extra.shape[0]
    tok_dev = doc_rows.shape[1] // 2
    row_chips = 4
    core = rank[0] % 2
    chip = rank[0] // 2
    pair = chip - chip % 2
    doc_count = doc_query.shape[1]
    left = lax.broadcasted_iota(jnp.int32, (1, 128), 1) < tok_dev
    doc_id = lax.broadcasted_iota(jnp.int32, (doc_count, 128), 0)
    blocks = []
    for y in range(tokens // (2 * tok_dev)):
        two = doc_rows[pl.ds(y * row_chips + pair % row_chips, 2), :]
        turned = pltpu.roll(two, tok_dev, 1)
        row = jnp.where(
            left,
            jnp.where(core == 0, two[0:1], turned[0:1]),
            jnp.where(core == 0, turned[1:2], two[1:2]),
        )
        blocks.append((doc_id == row).astype(F32).astype(BF))
    member = jnp.concatenate(blocks, axis=1)
    asked = jnp.broadcast_to(doc_query[...].astype(F32), (128, doc_count)).astype(BF)
    tok_query = jnp.dot(asked, member, preferred_element_type=F32)
    mark = lax.broadcasted_iota(jnp.int32, (128, tokens), 0) % 64
    columns = jnp.where(
        mark < NQ,
        jnp.where(tok_query == mark.astype(F32), 0.0, MASKED),
        jnp.where(mark == NQ, MASKED, jnp.where(mark < NQ + 4, 1.0, 0.0)),
    )
    extra[...] = columns.T.astype(BF)


def prepare_kernel(rank, first, second, third, bias_table, page_table, query_lengths, keys_aug, values_t, table_here,
                   slots_here, lengths_here, info, arrivals, *, side, pages, meanwhile=None):
    width, total = values_t.shape
    page_len = total // (2 * pages)
    keys = pages * page_len
    heads, bucket_count = bias_table.shape
    depth = width // heads
    slot_count = page_table.shape[0]
    max_pages = slot_count // NQ
    row_chips = 4
    pairs = [(page_table, slots_here), (query_lengths, lengths_here), (bias_table, table_here)]
    copies = [pltpu.make_async_copy(there, here, arrivals.at[i]) for i, (there, here) in enumerate(pairs)]
    for copy in copies:
        copy.start()
    sources = ((first, keys + 8), (second, keys + 8) if third is None else (third, 0))
    for part, (value_rows, offset) in enumerate(sources):
        for page in range(pages):
            value = value_rows[offset + page * page_len : offset + (page + 1) * page_len, :]
            values_t[:, pl.ds((part * pages + page) * page_len, page_len)] = value.astype(F32).T.astype(BF)
    if meanwhile is not None:
        meanwhile()
    core = rank[0] % 2
    chip = rank[0] // 2
    base = (chip // row_chips * row_chips + chip % 2) * 2 * pages
    count = 4 * pages
    copies[0].wait()
    copies[1].wait()
    for s in range(slot_count):
        place = slots_here[s] - base
        near = (place >= 0) & (place < 2 * pages)
        far = (place >= 4 * pages) & (place < 6 * pages)
        place = jnp.where(near, place, jnp.where(far, place - 2 * pages, count))
        info[0, place] = s // max_pages
        info[1, place] = lengths_here[s // max_pages] - (s % max_pages) * page_len
    low = lax.broadcasted_iota(jnp.int32, (1, 128), 1) < depth
    col = lax.broadcasted_iota(jnp.int32, (bucket_count, 128), 1) % 64
    copies[2].wait()
    table = jnp.concatenate([table_here[...], jnp.zeros((8 - heads, bucket_count), F32)], axis=0).T
    spreads = []
    for h in range(heads):
        a, b, c = split_three(jnp.broadcast_to(table[:, h : h + 1], (bucket_count, 128)))
        last = jnp.where(col == NQ + 3, c.astype(F32), 0.0)
        spreads.append(
            jnp.where(col == NQ + 1, a.astype(F32), jnp.where(col == NQ + 2, b.astype(F32), last)).astype(BF)
        )
    spread = jnp.concatenate(spreads, axis=1)
    bucket_row = lax.broadcasted_iota(jnp.int32, (bucket_count, page_len), 0).astype(F32)
    slot = lax.broadcasted_iota(jnp.int32, (page_len, 128), 0)
    key_col = lax.broadcasted_iota(jnp.int32, (page_len, 128), 1) % 64
    mine = ((chip % row_chips // 2) * 2 + core) * pages
    for part, key_rows in enumerate((first, second)):
        for page in range(pages):
            place = (mine ^ ((2 * side + part) * pages)) + page
            span = pl.ds((part * pages + page) * page_len, page_len)
            bucket = key_rows[keys : keys + 8, page * page_len : (page + 1) * page_len].astype(F32)[0:1]
            onehot = (jnp.broadcast_to(bucket, bucket_row.shape) == bucket_row).astype(F32).astype(BF)
            bias = lax.dot_general(onehot, spread, (((0,), (0,)), ((), ())), preferred_element_type=F32)
            holder = jnp.where(slot < info[1, place], info[0, place], NQ)
            marks = (key_col == holder).astype(F32)
            key = key_rows[page * page_len : (page + 1) * page_len, :].astype(F32)
            for h in range(heads):
                keep = low if h % 2 == 0 else jnp.logical_not(low)
                half = key[:, (h // 2) * 128 : (h // 2 + 1) * 128]
                keys_aug[h, span, :] = jnp.where(keep, half, bias[:, h * 128 : (h + 1) * 128] + marks).astype(BF)


def attention_kernel(rank, queries, keys_near, keys_far, values_near, values_far, extra, states, out_weight, out, own, fetched,
                     rows_aug, arrivals):
    start = pl.multiple_of(rank[0] * own.shape[0], own.shape[0])
    copies = [
        pltpu.make_async_copy(out_weight, fetched, arrivals.at[0]),
        pltpu.make_async_copy(states.at[pl.ds(start, own.shape[0])], own, arrivals.at[1]),
    ]
    for copy in copies:
        copy.start()
    chips, tok_dev, width = queries.shape
    heads = keys_near.shape[0]
    depth = width // heads
    low = lax.broadcasted_iota(jnp.int32, (1, 128), 1) < depth
    left = lax.broadcasted_iota(jnp.int32, (1, 128), 1) < tok_dev
    rows = queries[...].reshape(chips * tok_dev, width)
    for h in range(heads):
        half = rows[:, (h // 2) * 128 : (h // 2 + 1) * 128].astype(F32)
        keep = low if h % 2 == 0 else jnp.logical_not(low)
        rows_aug[h] = jnp.where(keep, half, extra[...].astype(F32)).astype(BF)
    sums = []
    logs = []

    def score(h):
        return [
            lax.dot_general(keys[h], rows_aug[h], (((1,), (1,)), ((), ())), preferred_element_type=F32)
            for keys in (keys_near, keys_far)
        ]

    ready = score(0)
    for h in range(heads):
        span = slice(h * depth, (h + 1) * depth)
        scores = ready
        if h + 1 < heads:
            ready = score(h + 1)
        top = jnp.maximum(
            jnp.max(scores[0], axis=0, keepdims=True), jnp.max(scores[1], axis=0, keepdims=True)
        )
        total = jnp.zeros_like(top)
        summed = jnp.zeros((depth, chips * tok_dev), F32)
        for part, values in zip(scores, (values_near, values_far)):
            weights = jnp.exp(part - top)
            total += jnp.sum(weights, axis=0, keepdims=True)
            summed += jnp.dot(values[span, :], weights.astype(BF), preferred_element_type=F32)
        sums.append(summed * (1.0 / total))
        logs.append(top + jnp.log(total))
    for duo in range(chips // 2):
        lanes = slice(duo * 128, (duo + 1) * 128)
        pad = [jnp.zeros((6, 128), F32)]
        upper = jnp.concatenate([sums[0][:, lanes], sums[1][:, lanes]], axis=0)
        lower = jnp.concatenate([sums[2][:, lanes], sums[3][:, lanes]], axis=0)
        stat_upper = jnp.concatenate([logs[0][:, lanes], logs[1][:, lanes]] + pad, axis=0)
        stat_lower = jnp.concatenate([logs[2][:, lanes], logs[3][:, lanes]] + pad, axis=0)
        block = (
            jnp.where(left, upper, pltpu.roll(lower, tok_dev, 1)),
            jnp.where(left, pltpu.roll(upper, tok_dev, 1), lower),
        )
        stat = (
            jnp.where(left, stat_upper, pltpu.roll(stat_lower, tok_dev, 1)),
            jnp.where(left, pltpu.roll(stat_upper, tok_dev, 1), stat_lower),
        )
        for which in range(2):
            a, b, c = split_three(stat[which])
            packed = [a[0:2].astype(F32), b[0:2].astype(F32), c[0:2].astype(F32), jnp.zeros((2, 128), F32)]
            out[duo * 2 + which, 0:128, :] = block[which].astype(BF)
            out[duo * 2 + which, 128:136, :] = jnp.concatenate(packed, axis=0).astype(BF)
    for copy in copies:
        copy.wait()


def combine_kernel(parts, out_weight, out):
    chips = parts.shape[0]
    logs = []
    for chip in range(chips):
        stat = parts[chip, 128:136, :].astype(F32)
        logs.append(stat[0:2] + stat[2:4] + stat[4:6])
    top = logs[0]
    for chip in range(1, chips):
        top = jnp.maximum(top, logs[chip])
    scales = [jnp.exp(log - top) for log in logs]
    whole = scales[0]
    for chip in range(1, chips):
        whole = whole + scales[chip]
    sums = [jnp.zeros((64, 128), F32), jnp.zeros((64, 128), F32)]
    for chip in range(chips):
        share = scales[chip] / whole
        for r in range(2):
            sums[r] = sums[r] + share[r : r + 1] * parts[chip, r * 64 : (r + 1) * 64, :].astype(F32)
    joined = jnp.concatenate(sums, axis=0).T
    context = jnp.concatenate([joined[0:64], joined[64:128]], axis=1).astype(BF)
    out[...] = jnp.dot(context, out_weight[...], preferred_element_type=F32).astype(BF)


def norm_kernel(terms, states, gain, score_vector, out, score):
    hidden = states[...].astype(F32)
    for source in range(terms.shape[0]):
        hidden = hidden + terms[source].astype(F32)
    normed = rms_scale(hidden, gain[...]).astype(BF)
    for target in range(out.shape[0]):
        out[target] = normed
    score[...] = jnp.broadcast_to(jnp.sum(hidden * score_vector[...], axis=-1, keepdims=True), score.shape)


def down_kernel(weight, score_vector, gate_weight, out, fetched, weight_here, arrivals):
    copy = pltpu.make_async_copy(weight, weight_here, arrivals.at[0])
    fetch = pltpu.make_async_copy(gate_weight, fetched, arrivals.at[1])
    copy.start()
    fetch.start()
    pieces = [piece.astype(F32) for piece in split_three(score_vector[...])]
    rows = jnp.concatenate(pieces + [jnp.zeros((5, score_vector.shape[1]), F32)], axis=0).astype(BF)
    copy.wait()
    terms = lax.dot_general(rows, weight_here[...], (((1,), (1,)), ((), ())), preferred_element_type=F32)
    out[...] = terms[0:1] + terms[1:2] + terms[2:3]
    fetch.wait()


def feed_kernel(rows, gate_weight, up_weight, down_score, own_score, own_docs, out, up_here, arrivals):
    steps = up_here.shape[0]
    size = rows.shape[1] // steps
    copies = [
        pltpu.make_async_copy(up_weight.at[pl.ds(i * size, size)], up_here.at[i], arrivals.at[i]) for i in range(steps)
    ]
    for copy in copies:
        copy.start()
    docs = own_docs[...]
    doc_dev = DOCS // out.shape[0]
    lane = lax.broadcasted_iota(jnp.int32, (docs.shape[0], 128), 1)
    holder = (docs // doc_dev == lane).astype(F32).astype(BF)
    gate = jnp.dot(rows[...], gate_weight[...], preferred_element_type=F32)
    gate = jax.nn.gelu(gate, approximate=True)
    upper = jnp.zeros_like(gate)
    for i in range(steps):
        copies[i].wait()
        upper += jnp.dot(rows[:, i * size : (i + 1) * size], up_here[i], preferred_element_type=F32)
    middle = (gate * upper).astype(BF).astype(F32)
    tok_score = jnp.sum(middle * down_score[...], axis=-1, keepdims=True) + own_score[...]
    placed = jnp.where(docs % doc_dev == lane, tok_score, 0.0)
    pieces = jnp.concatenate([piece.astype(F32) for piece in split_three(placed)], axis=1).astype(BF)
    sums = lax.dot_general(holder, pieces, (((0,), (0,)), ((), ())), preferred_element_type=F32)[0 : out.shape[0]]
    out[...] = sums[:, 0:128] + sums[:, 128:256] + sums[:, 256:384]


def fold_kernel(terms, out):
    out[...] = jnp.broadcast_to(jnp.sum(terms[...], axis=0, keepdims=True), out.shape)


def vmem():
    return pl.BlockSpec(memory_space=pltpu.VMEM)


def smem():
    return pl.BlockSpec(memory_space=pltpu.SMEM)


def in_hbm(value):
    return pltpu.with_memory_space_constraint(value, pltpu.HBM)


def hbm():
    return pl.BlockSpec(memory_space=pltpu.HBM)


def anywhere():
    return pl.BlockSpec(memory_space=pl.ANY)


def call(kernel, name, shapes, specs, scratch=()):
    single = not isinstance(shapes, (list, tuple))
    return pl.pallas_call(
        kernel,
        out_shape=shapes,
        in_specs=specs,
        out_specs=vmem() if single else [vmem()] * len(shapes),
        scratch_shapes=list(scratch),
        compiler_params=pltpu.CompilerParams(vmem_limit_bytes=40 << 20),
        name=name,
    )


def per_device(
    doc_states,
    gain_attn,
    query_weight,
    cache_keys,
    cache_values,
    rel_bucket,
    bias_table,
    out_weight,
    gain_ffn,
    wi_gate,
    wi_up,
    wo_ffn,
    score_vector,
    query_lengths,
    doc_query,
    doc_of_token,
    page_table,
):
    shape = jax.ShapeDtypeStruct
    tok_dev, model = doc_states.shape
    local_pages, page_len, local_width = cache_keys.shape
    local_heads = bias_table.shape[1]
    page_size = lax.axis_size("page")
    head_size = lax.axis_size("head")
    page_rank = lax.axis_index("page")
    head_rank = lax.axis_index("head")
    group = page_size // 4
    groups = [
        [y * 8 + (x + side) * 2 + core for y in range(4) for side in range(2)] for x in (0, 2) for core in range(2)
    ]
    core_swap = [(i, i ^ 1) for i in range(page_size)]
    side_swap = [(i, i ^ 4) for i in range(page_size)]

    def swap(value, pairs):
        return lax.ppermute(value, "page", pairs)

    keys_held = local_pages * page_len
    copies, payload = call(
        project_kernel,
        "project",
        [shape((group, tok_dev, local_width), BF), shape((2 * keys_held + 8, local_width), BF)],
        [hbm()] * 6,
        [
            pltpu.VMEM((tok_dev, model), BF),
            pltpu.VMEM((1, model), F32),
            pltpu.VMEM((model, local_width), BF),
            pltpu.VMEM((local_pages, page_len), jnp.int32),
            pltpu.SemaphoreType.DMA((6,)),
        ],
    )(
        in_hbm(doc_states),
        in_hbm(gain_attn.reshape(1, model)),
        in_hbm(query_weight),
        in_hbm(cache_keys.reshape(keys_held, local_width)),
        in_hbm(cache_values.reshape(keys_held, local_width)),
        in_hbm(rel_bucket),
    )
    payload_side = swap(payload, side_swap)
    payload_core = swap(payload, core_swap)
    keys_far = swap(payload_side[0 : keys_held + 8], core_swap)
    values_far = swap(payload_side[keys_held + 8 :], core_swap)
    gathered = lax.all_to_all(copies, "page", 0, 0, axis_index_groups=groups, tiled=True)

    rank = page_rank.reshape(1)
    doc_rows = doc_of_token.reshape(-1, 2 * tok_dev)
    key_count = 2 * local_pages * page_len

    shapes = [shape((local_heads, key_count, 128), BF), shape((local_width, key_count), BF)]
    scratch = [
        pltpu.VMEM(bias_table.T.shape, F32),
        pltpu.SMEM(page_table.shape, jnp.int32),
        pltpu.SMEM(query_lengths.shape, jnp.int32),
        pltpu.SMEM((2, 4 * local_pages + 1), jnp.int32),
        pltpu.SemaphoreType.DMA((3,)),
    ]
    tables = (in_hbm(bias_table.T), in_hbm(page_table), in_hbm(query_lengths))
    keys_near, values_near, extra = call(
        functools.partial(near_kernel, pages=local_pages),
        "near",
        shapes + [shape((group * tok_dev, 128), BF)],
        [smem()] + [vmem()] * 2 + [hbm()] * 5,
        scratch
        + [
            pltpu.VMEM((1, doc_query.shape[0]), jnp.int32),
            pltpu.VMEM(doc_rows.shape, jnp.int32),
            pltpu.SemaphoreType.DMA((2,)),
        ],
    )(rank, payload, payload_core, *tables, in_hbm(doc_query.reshape(1, -1)), in_hbm(doc_rows))
    keys_away, values_away = call(
        functools.partial(prepare_kernel, side=1, pages=local_pages),
        "away",
        shapes,
        [smem()] + [vmem()] * 3 + [hbm()] * 3,
        scratch,
    )(rank, payload_side, keys_far, values_far, *tables)
    own = tok_dev // head_size
    partials, own_states, fetched = call(
        attention_kernel,
        "attention",
        [shape((group, 136, 128), BF), shape((own, model), BF), shape(out_weight.shape, BF)],
        [smem()] + [vmem()] * 6 + [hbm()] * 2,
        [pltpu.VMEM((local_heads, group * tok_dev, 128), BF), pltpu.SemaphoreType.DMA((2,))],
    )(
        head_rank.reshape(1), gathered, keys_near, keys_away, values_near, values_away, extra,
        in_hbm(doc_states), in_hbm(out_weight),
    )
    hidden_units = wi_gate.shape[1]
    returned = lax.all_to_all(partials, "page", 0, 0, axis_index_groups=groups, tiled=True)
    projected = call(combine_kernel, "combine", shape((tok_dev, model), BF), [vmem()] * 2)(returned, fetched)

    doc_dev = doc_query.shape[0] // page_size
    terms = lax.all_to_all(projected.reshape(head_size, own, model), "head", 0, 0, tiled=True)
    spread, hidden_score = call(
        norm_kernel,
        "norm",
        [shape((head_size, own, model), BF), shape((own, 128), F32)],
        [vmem()] * 4,
    )(terms, own_states, gain_ffn.reshape(1, model), score_vector.reshape(1, model))
    spread, late_gate, down_weight, late_docs, late_rank = lax.optimization_barrier(
        (spread, wi_gate, wo_ffn, doc_of_token, page_rank)
    )
    down_score, gate_here = call(
        down_kernel,
        "down",
        [shape((1, hidden_units), F32), shape(wi_gate.shape, BF)],
        [hbm(), vmem(), hbm()],
        [pltpu.VMEM(wo_ffn.shape, BF), pltpu.SemaphoreType.DMA((2,))],
    )(in_hbm(down_weight), score_vector.reshape(1, model), in_hbm(late_gate))
    mine_docs = late_rank * doc_dev + jnp.arange(doc_dev, dtype=jnp.int32)
    counts = jnp.sum((late_docs[:, None] == mine_docs[None, :]).astype(F32), axis=0)
    rows = lax.all_to_all(spread, "head", 0, 0, tiled=True).reshape(tok_dev, model)
    rows, counts = lax.optimization_barrier((rows, counts))
    token = jnp.arange(tok_dev, dtype=jnp.int32)[:, None]
    own_score = jnp.where(token // own == head_rank, jnp.tile(hidden_score[:, :1], (head_size, 1)), 0.0)
    own_docs = lax.dynamic_slice_in_dim(late_docs, late_rank * tok_dev, tok_dev, 0)[:, None]
    steps = 4
    doc_sums = call(
        feed_kernel, "feed", shape((page_size, 128), F32), [vmem(), vmem(), hbm(), vmem(), vmem(), vmem()],
        [pltpu.VMEM((steps, model // steps, hidden_units), BF), pltpu.SemaphoreType.DMA((steps,))],
    )(rows, gate_here, in_hbm(wi_up), down_score, own_score, own_docs)
    doc_sums = doc_sums.reshape(page_size, 1, 128)
    arrived = lax.all_to_all(doc_sums, "page", 0, 0, tiled=True)
    pooled = call(fold_kernel, "fold", shape((head_size, 1, 128), F32), [vmem()])(arrived)
    pooled = jnp.sum(lax.all_to_all(pooled, "head", 0, 0, tiled=True), axis=(0, 1))[:doc_dev]
    return pooled / counts


def solution(mesh):
    return jax.shard_map(
        per_device,
        mesh=mesh,
        in_specs=(
            P("page", None),
            P(),
            P(None, "head"),
            P("page", None, "head"),
            P("page", None, "head"),
            P("page", None),
            P(None, "head"),
            P("head", None),
            P(),
            P(None, "head"),
            P(None, "head"),
            P("head", None),
            P(),
            P(),
            P(),
            P(),
            P(),
        ),
        out_specs=P("page"),
        check_vma=False,
    )
```
